32 devices in a mesh: row: 16 (over z, x, core), col: 2 (over y).
Axes of the slice: x: 2, y: 2, z: 4, core: 2. Of those that a mesh axis runs over, the one named last changes fastest.
Arguments:
- ham: bfloat16 [8192, 8192], P('row'), may hold values from -0.2 to 1.7, as said below
- coeff: bfloat16 [8192, 8192], P('row', 'col'), may hold values from -40 to 40, as said below
- tile_mask: int32 [256, 256], P('row'), may hold values from 0 to 1, as said below
- occupation: int32 [16, 8192], replicated, may hold values from 0 to 1, as said below
- orbital_energy: float32 [16], replicated, may hold values from -0.4 to 0.6
- coulomb: float32 [16, 16], replicated, may hold values from 0.005 to 0.04
Outputs:
- correction: float32 [8192, 8192], P('row', 'col')
- stats: float32 [2], replicated
The draws below stay inside these ranges and needn't reach their ends.
Inputs may be any that keep to these rules, and one draw needn't show every extreme that they name: ham is symmetric. coeff is symmetric. tile_mask is symmetric with ones on its diagonal. `occupation`: every column holds exactly 6 ones.
All inputs are finite; a program needn't handle non-finite values.
Results may differ from the reference program's by a relative error of at most 0.0003.
Values may be sent and summed in bfloat16 or wider, within the bound.
A program may use at most 192 MiB of HBM per device.

```python
import math
import jax
import jax.numpy as jnp
from jax import lax

NS = 8192
NORB = 16
NEL = 6
STR_BLOCK = 32


def string_scales(key):
    uniform_part = jax.random.uniform(key, (NS,), jnp.float32)
    position = jnp.arange(NS, dtype=jnp.float32) / NS
    return jnp.exp(uniform_part * math.log(10.0)) * (1.0 + position)


def draw_coeff(key, part):
    key_entries = jax.random.fold_in(key, 11)
    key_scales = jax.random.fold_in(key, 12)
    entries = jax.random.normal(key_entries, (NS, NS), jnp.float32)
    scales = string_scales(key_scales)
    norm_scale = 50.0
    paired = jnp.clip((entries + entries.T) * 0.7071, -4.0, 4.0)
    return (paired * scales[:, None] * scales[None, :] / norm_scale).astype(jnp.bfloat16)


def draw_ham(key, part):
    key_entries = jax.random.fold_in(key, 21)
    key_diagonal = jax.random.fold_in(key, 22)
    entries = jnp.clip(jax.random.normal(key_entries, (NS, NS), jnp.float32), -6.0, 6.0)
    diagonal = jax.random.uniform(key_diagonal, (NS,), jnp.float32, 0.5, 1.5)
    paired = (entries + entries.T) * (0.7071 / math.sqrt(NS))
    return (paired + jnp.diag(diagonal)).astype(jnp.bfloat16)


def draw_tile_mask(key, part):
    block_count = NS // STR_BLOCK
    coin_flips = jax.random.randint(jax.random.fold_in(key, 31), (block_count, block_count), 0, 2, jnp.int32)
    row_index = jnp.arange(block_count, dtype=jnp.int32)[:, None]
    col_index = jnp.arange(block_count, dtype=jnp.int32)[None, :]
    mirrored = jnp.where(row_index <= col_index, coin_flips, coin_flips.T)
    return jnp.where(row_index == col_index, 1, mirrored).astype(jnp.int32)


def draw_occupation(key, part):
    keys_all = jax.random.split(jax.random.fold_in(key, 41), NS)
    orders = jax.vmap(lambda one_key: jax.random.permutation(one_key, NORB))(keys_all)
    return (orders < NEL).astype(jnp.int32).T


def setup_inputs(seed: int = 0) -> dict:
    arg_keys = jax.random.split(jax.random.key(seed), 7)
    return {
        "ham": draw_ham(jax.random.fold_in(arg_keys[6], 71), 0),
        "coeff": draw_coeff(jax.random.fold_in(arg_keys[6], 71), 0),
        "tile_mask": draw_tile_mask(jax.random.fold_in(arg_keys[6], 71), 0),
        "occupation": draw_occupation(jax.random.fold_in(arg_keys[6], 71), 0),
        "orbital_energy": jnp.clip(jax.random.uniform(arg_keys[4], (NORB,), jnp.float32, -0.4, 0.6), -0.4, 0.6),
        "coulomb": jnp.clip(jnp.exp(jax.random.uniform(arg_keys[5], (NORB, NORB), jnp.float32, math.log(0.005), math.log(0.04))), 0.005, 0.04),
    }


def reference(ham, coeff, tile_mask, occupation, orbital_energy, coulomb):
    block_count = tile_mask.shape[0]
    block_size = NS // block_count
    weights = tile_mask.astype(jnp.bfloat16)[:, None, :, None]
    masked = (ham.reshape(block_count, block_size, block_count, block_size) * weights).reshape(NS, NS)
    product = jnp.dot(masked, coeff, preferred_element_type=jnp.float32)
    sigma = product + product.T
    coeff_float = coeff.astype(jnp.float32)
    theta = jnp.sum(coeff_float * sigma) / jnp.sum(coeff_float * coeff_float)
    occ_float = occupation.astype(jnp.float32)
    energy = jnp.dot(orbital_energy, occ_float, precision=lax.Precision.HIGHEST)
    coupling = jnp.dot(jnp.dot(occ_float.T, coulomb, precision=lax.Precision.HIGHEST), occ_float, precision=lax.Precision.HIGHEST)
    diagonal = energy[:, None] + energy[None, :] + coupling
    residual = sigma - theta * coeff_float
    update = residual / jnp.maximum(jnp.abs(diagonal - theta), 1.0)
    squares = jnp.sum(residual * residual)
    spread = jnp.sum(update * update)
    correction = update * lax.rsqrt(spread / (NS * NS) + 1e-06)
    stats = jnp.stack([theta, jnp.sqrt(squares / (NS * NS))])
    return (correction, stats)
```

```python
import functools
import math

import jax
import jax.numpy as jnp
from jax import lax
from jax.experimental import pallas as pl
from jax.experimental.layout import Layout, with_layout_constraint
from jax.experimental.pallas import tpu as pltpu
from jax.sharding import PartitionSpec as P

MESH = pl.DeviceIdType.MESH
HIGH = lax.Precision.HIGHEST


def turn_kernel(row_count, col_count, total, chunk, chunks, *refs):
    last = chunk == chunks - 1
    if last:
        products, arrived = refs[:chunks], refs[chunks : 2 * chunks - 1]
        diagonal_ref, c_ref, out_ref, stats_ref, recv = refs[2 * chunks - 1 : 2 * chunks + 4]
        refs = refs[2 * chunks + 4 :]
        mine, sums, sum_send, sum_recv = refs[-4:]
    else:
        products = refs[:1]
        recv = refs[1]
        refs = refs[2:]
    p_ref, packed, relay_a, relay_b, load_sem, own_send, recv_sem, arrive_a, arrive_b, send_a, send_b, self_sem = refs[:12]
    row = lax.axis_index("row")
    col = lax.axis_index("col")
    tile = p_ref.shape[0]
    half = tile // 2
    fold = row_count // col_count
    per = fold // chunks
    home = lax.div(row, fold)
    place = lax.rem(row, fold)
    turn = lax.div(place, chunks)
    count = row_count * col_count
    me = row * col_count + col
    is_home = home == col
    takes = lax.rem(place, chunks) == chunk
    if last:
        loads = [
            pltpu.make_async_copy(
                product.at[:, pl.ds(k * tile, tile)],
                p_ref.at[:, pl.ds((q + chunks * k) * tile, tile)],
                load_sem.at[q * per + k],
            )
            for q, product in enumerate(products)
            for k in range(per)
        ]
    else:
        loads = [pltpu.make_async_copy(products[0], p_ref, load_sem.at[0])]
    for load in loads:
        load.start()
    if last:
        diagonal_load = pltpu.make_async_copy(diagonal_ref, out_ref, self_sem.at[3])
        diagonal_load.start()

    barrier = pltpu.get_barrier_semaphore()

    def greet(d, carry):
        other = lax.rem(me + d, count)
        pl.semaphore_signal(
            barrier,
            inc=1,
            device_id=(lax.div(other, col_count), lax.rem(other, col_count)),
            device_id_type=MESH,
        )
        return carry

    lax.fori_loop(1, count, greet, 0)
    pl.semaphore_wait(barrier, count - 1)
    for load in loads:
        load.wait()

    def columns(s):
        return pl.ds(pl.multiple_of(s * tile, tile), tile)

    def remote(src, dst, send, arrive, to_row, to_col):
        return pltpu.make_async_remote_copy(
            src_ref=src,
            dst_ref=dst,
            send_sem=send,
            recv_sem=arrive,
            device_id=(to_row, to_col),
            device_id_type=MESH,
        )

    def spot(k):
        kk = lax.rem(turn + k, per)
        return kk, chunk + chunks * kk

    def own_direct(k):
        kk, s = spot(k)
        near = col * fold + s
        return [
            remote(packed.at[kk, h], recv.at[place, h], own_send.at[kk, h], recv_sem.at[place, h], near, col)
            for h in range(2)
        ]

    def own_relayed(k):
        kk, s = spot(k)
        near = col * fold + s
        slot_a = col - (col > home).astype(jnp.int32)
        slot_b = row - fold * (home > col).astype(jnp.int32)
        return [
            remote(packed.at[kk, 0], relay_a.at[slot_a, kk], own_send.at[kk, 0], arrive_a.at[slot_a, kk], row, home),
            remote(packed.at[kk, 1], relay_b.at[slot_b], own_send.at[kk, 1], arrive_b.at[slot_b], near, col),
        ]

    def own_local():
        return [pltpu.make_async_copy(packed.at[turn, h], recv.at[place, h], self_sem.at[h]) for h in range(2)]

    def pack(k):
        kk, s = spot(k)
        cols = columns(s) if last else columns(kk)
        for h in range(2):
            peak = jnp.max(jnp.abs(p_ref[pl.ds(h * half, half), cols]), axis=0, keepdims=True)
            code = jnp.floor(jnp.log2(jnp.maximum(peak, 1e-30)) * 128.0) + 2.0
            grow = jnp.exp2(code * (-1.0 / 128.0)) * 32767.0
            packed[kk, h, pl.ds(half, 16)] = jnp.broadcast_to(code, (16, tile)).astype(jnp.int32).astype(jnp.int16)
            rows = min(64, half)
            for r in range(0, half, rows):
                value = p_ref[pl.ds(h * half + r, rows), cols] * grow
                packed[kk, h, pl.ds(r, rows)] = jnp.floor(value + 0.5).astype(jnp.int32).astype(jnp.int16)

    def exchange(phase, start):
        def one(d, carry):
            other = lax.rem(me + d, count)
            copy = remote(
                mine.at[phase],
                sums.at[phase, me],
                sum_send.at[phase, d],
                sum_recv.at[phase, me],
                lax.div(other, col_count),
                lax.rem(other, col_count),
            )
            if start:
                copy.start()
            else:
                copy.wait_send()
            return carry

        lax.fori_loop(1, count, one, 0)

    def gather_sums(phase):
        def one(d, carry):
            other = lax.rem(me + d, count)
            remote(
                mine.at[phase],
                sums.at[phase, other],
                sum_send.at[phase, d],
                sum_recv.at[phase, other],
                lax.div(other, col_count),
                lax.rem(other, col_count),
            ).wait_recv()
            return carry

        lax.fori_loop(1, count, one, 0)
        sums[phase, pl.ds(me, 1)] = mine[pl.ds(phase, 1)]
        every = jnp.sum(sums[phase], axis=0)
        return jnp.sum(every[0:8]), jnp.sum(every[8:16])

    def fold_sum(x):
        lanes = x.shape[1] // 128
        out = x[:, 0:128]
        for q in range(1, lanes):
            out = out + x[:, q * 128 : (q + 1) * 128]
        return jnp.sum(out.reshape(x.shape[0] // 8, 8, 128), axis=0)

    zero = jnp.zeros((8, 128), jnp.float32)
    if last:
        step_rows = min(32, tile)

        def early(r, carry):
            rows = pl.ds(pl.multiple_of(r * step_rows, step_rows), step_rows)
            c = c_ref[rows, :].astype(jnp.float32)
            return carry[0] + fold_sum(c * p_ref[rows, :]), carry[1] + fold_sum(c * c)

        proj, weight = lax.fori_loop(0, tile // step_rows, early, (zero, zero))
        mine[0, 0:8] = proj
        mine[0, 8:16] = weight
        exchange(0, True)

    def launch(k, carry):
        pack(k)

        @pl.when(jnp.logical_not(is_home))
        def _():
            for copy in own_relayed(k):
                copy.start()

        @pl.when(jnp.logical_and(is_home, jnp.logical_or(k > 0, jnp.logical_not(takes))))
        def _():
            for copy in own_direct(k):
                copy.start()

        return carry

    lax.fori_loop(0, per, launch, 0)

    @pl.when(jnp.logical_and(is_home, takes))
    def _():
        for copy in own_local():
            copy.start()
        for copy in own_local():
            copy.wait()

    def relay_first(t):
        slot = lax.div(t, per)
        group = slot + (slot >= col).astype(jnp.int32)
        kk, s = spot(lax.rem(t, per))
        return slot, kk, remote(
            relay_a.at[slot, kk], recv.at[place, 0], send_a.at[t], recv_sem.at[place, 0], group * fold + s, col
        )

    def relay_second(t):
        slot = lax.div(t, fold)
        group = slot + (slot >= col).astype(jnp.int32)
        far = lax.rem(place - lax.rem(t, fold) + fold, fold)
        slot_b = slot * fold + far
        return slot_b, remote(
            relay_b.at[slot_b], recv.at[far, 1], send_b.at[t], recv_sem.at[far, 1], row, group
        )

    @pl.when(is_home)
    def _():
        def step(t, carry):
            slot, kk, copy = relay_first(t)
            pltpu.make_async_copy(relay_a.at[slot, kk], relay_a.at[slot, kk], arrive_a.at[slot, kk]).wait()
            copy.start()
            return carry

        lax.fori_loop(0, (col_count - 1) * per, step, 0)

    @pl.when(jnp.logical_and(is_home, takes))
    def _():
        def step(t, carry):
            slot_b, copy = relay_second(t)
            pltpu.make_async_copy(relay_b.at[slot_b], relay_b.at[slot_b], arrive_b.at[slot_b]).wait()
            copy.start()
            return carry

        lax.fori_loop(0, (col_count - 1) * fold, step, 0)

    def await_piece(k):
        s = lax.rem(place - k + fold, fold)

        @pl.when(jnp.logical_and(takes, jnp.logical_not(jnp.logical_and(is_home, k == 0))))
        def _():
            for h in range(2):
                pltpu.make_async_copy(recv.at[s, h], recv.at[s, h], recv_sem.at[s, h]).wait()

    def settle():
        @pl.when(is_home)
        def _():
            def done(k, carry):
                @pl.when(jnp.logical_or(k > 0, jnp.logical_not(takes)))
                def _():
                    for copy in own_direct(k):
                        copy.wait_send()

                return carry

            lax.fori_loop(0, per, done, 0)

            def done_first(t, carry):
                relay_first(t)[-1].wait_send()
                return carry

            lax.fori_loop(0, (col_count - 1) * per, done_first, 0)

        @pl.when(jnp.logical_and(is_home, takes))
        def _():
            def done_second(t, carry):
                relay_second(t)[-1].wait_send()
                return carry

            lax.fori_loop(0, (col_count - 1) * fold, done_second, 0)

        @pl.when(jnp.logical_not(is_home))
        def _():
            def done(k, carry):
                for copy in own_relayed(k):
                    copy.wait_send()
                return carry

            lax.fori_loop(0, per, done, 0)

    if not last:

        def hold(k, carry):
            await_piece(k)
            return carry

        lax.fori_loop(0, fold, hold, 0)
        settle()
        return

    for q, ready in enumerate(arrived):

        @pl.when(lax.rem(place, chunks) == q)
        def _():
            fetch = pltpu.make_async_copy(ready, recv, self_sem.at[2])
            fetch.start()
            fetch.wait()

    proj, weight = gather_sums(0)
    theta = 2.0 * proj / weight
    diagonal_load.wait()

    piece = min(128, tile)

    def finish(k, carry):
        s = lax.rem(place - k + fold, fold)

        await_piece(k)

        def part(r, carry):
            squares, spread = carry
            rows = pl.ds(pl.multiple_of(r * piece, piece), piece)
            for h in range(2):
                cols = pl.ds(pl.multiple_of(s * tile + h * half, half), half)
                code = recv[s, h, pl.ds(half, 16), rows].astype(jnp.int32).astype(jnp.float32)[0:1]
                shrink = jnp.exp2(code * (1.0 / 128.0)) * (1.0 / 32767.0)
                value = recv[s, h, pl.ds(0, half), rows].astype(jnp.int32).astype(jnp.float32)
                turned = (value * shrink).T
                sigma = p_ref[rows, cols] + turned
                residual = sigma - theta * c_ref[rows, cols].astype(jnp.float32)
                update = residual / jnp.maximum(jnp.abs(out_ref[rows, cols] - theta), 1.0)
                out_ref[rows, cols] = update
                squares = squares + fold_sum(residual * residual)
                spread = spread + fold_sum(update * update)
            return squares, spread

        return lax.fori_loop(0, tile // piece, part, carry)

    squares, spread = lax.fori_loop(0, fold, finish, (zero, zero))
    mine[1, 0:8] = squares
    mine[1, 8:16] = spread
    exchange(1, True)
    squares, spread = gather_sums(1)
    stats_ref[0] = theta
    stats_ref[1] = squares / total
    stats_ref[2] = spread / total

    exchange(0, False)
    exchange(1, False)
    settle()


def turn(chunk, chunks, products, arrived, coeff, diagonal, strings):
    tile_rows, tile_cols = coeff.shape
    row_count = lax.axis_size("row")
    col_count = lax.axis_size("col")
    fold = row_count // col_count
    per = fold // chunks
    count = row_count * col_count
    tall = tile_rows // 2 + 16
    others = max(col_count - 1, 1)
    vmem = pl.BlockSpec(memory_space=pltpu.VMEM)
    anywhere = pl.BlockSpec(memory_space=pl.ANY)
    dma = pltpu.SemaphoreType.DMA
    last = chunk == chunks - 1
    arrival = (fold, 2, tall, tile_rows)
    scratch = [
        pltpu.VMEM((tile_rows, tile_cols if last else tile_cols // chunks), jnp.float32),
        pltpu.VMEM((per, 2, tall, tile_rows), jnp.int16),
        pltpu.VMEM((others, per, tall, tile_rows), jnp.int16),
        pltpu.VMEM((others * fold, tall, tile_rows), jnp.int16),
        dma((fold,)),
        dma((per, 2)),
        dma((fold, 2)),
        dma((others, per)),
        dma((others * fold,)),
        dma((others * per,)),
        dma((others * fold,)),
        dma((4,)),
    ]
    if last:
        operands = (*products, *arrived, diagonal, coeff)
        in_specs = [anywhere] * (2 * chunks) + [vmem]
        out_shape = (
            jax.ShapeDtypeStruct((tile_rows, tile_cols), jnp.float32),
            jax.ShapeDtypeStruct((3,), jnp.float32),
        )
        out_specs = (vmem, pl.BlockSpec(memory_space=pltpu.SMEM))
        scratch = [
            pltpu.VMEM(arrival, jnp.int16),
            *scratch,
            pltpu.VMEM((2, 16, 128), jnp.float32),
            pltpu.VMEM((2, count, 16, 128), jnp.float32),
            dma((2, count)),
            dma((2, count)),
        ]
    else:
        operands = (products[chunk],)
        in_specs = [anywhere]
        out_shape = jax.ShapeDtypeStruct(arrival, jnp.int16)
        out_specs = vmem
    return pl.pallas_call(
        functools.partial(turn_kernel, row_count, col_count, float(strings) * float(strings), chunk, chunks),
        out_shape=out_shape,
        in_specs=in_specs,
        out_specs=out_specs,
        scratch_shapes=scratch,
        compiler_params=pltpu.CompilerParams(
            collective_id=chunk, has_side_effects=True, vmem_limit_bytes=(60 if last else 24) * 1024 * 1024
        ),
        name=f"turn_{chunk}",
    )(*operands)


CHUNKS = 4


def body(ham, coeff, tile_mask, occupation, orbital_energy, coulomb):
    tile_rows, strings = ham.shape
    tile_cols = coeff.shape[1]
    mask_cols = tile_mask.shape[1]
    block_size = strings // mask_cols
    mask_rows = tile_rows // block_size
    weights = tile_mask.astype(jnp.bfloat16)[:, None, :, None]
    masked = (ham.reshape(mask_rows, block_size, mask_cols, block_size) * weights).reshape(
        tile_rows, strings
    )
    occ_float = occupation.astype(jnp.float32)
    occ_alpha = lax.dynamic_slice_in_dim(occ_float, lax.axis_index("row") * tile_rows, tile_rows, 1)
    occ_beta = lax.dynamic_slice_in_dim(occ_float, lax.axis_index("col") * tile_cols, tile_cols, 1)
    energy_alpha = jnp.dot(orbital_energy, occ_alpha, precision=HIGH)
    energy_beta = jnp.dot(orbital_energy, occ_beta, precision=HIGH)
    coupling = jnp.dot(jnp.dot(occ_alpha.T, coulomb, precision=HIGH), occ_beta, precision=HIGH)
    diagonal = energy_alpha[:, None] + energy_beta[None, :] + coupling
    fold = tile_cols // tile_rows
    chunks = math.gcd(CHUNKS, fold)
    products = []
    arrived = []
    for q in range(chunks):
        part = jnp.concatenate(
            [coeff[:, s * tile_rows : (s + 1) * tile_rows] for s in range(q, fold, chunks)], axis=1
        )
        gathered = with_layout_constraint(lax.all_gather(part, "row", axis=0, tiled=True), Layout((0, 1)))
        products.append(jnp.dot(masked, gathered, preferred_element_type=jnp.float32))
        result = turn(q, chunks, products, arrived, coeff, diagonal, strings)
        if q < chunks - 1:
            arrived.append(result)
    update, sums = result
    correction = update * lax.rsqrt(sums[2] + 1e-06)
    stats = jnp.stack([sums[0], jnp.sqrt(sums[1])])
    return (correction, stats)


def solution(mesh):
    in_specs = (P("row", None), P("row", "col"), P("row", None), P(), P(), P())
    out_specs = (P("row", "col"), P())
    return jax.shard_map(body, mesh=mesh, in_specs=in_specs, out_specs=out_specs, check_vma=False)
```

```python
import functools
import math

import jax
import jax.numpy as jnp
from jax import lax
from jax.experimental import pallas as pl
from jax.experimental.layout import Layout, with_layout_constraint
from jax.experimental.pallas import tpu as pltpu
from jax.sharding import PartitionSpec as P

MESH = pl.DeviceIdType.MESH
HIGH = lax.Precision.HIGHEST


def turn_kernel(row_count, col_count, total, chunk, chunks, *refs):
    last = chunk == chunks - 1
    if last:
        products, arrived = refs[:chunks], refs[chunks : 2 * chunks - 1]
        diagonal_ref, c_ref, out_ref, stats_ref, recv = refs[2 * chunks - 1 : 2 * chunks + 4]
        refs = refs[2 * chunks + 4 :]
        mine, sums, sum_send, sum_recv = refs[-4:]
    else:
        products = refs[:1]
        recv = refs[1]
        refs = refs[2:]
    p_ref, packed, relay_a, relay_b, load_sem, own_send, recv_sem, arrive_a, arrive_b, send_a, send_b, self_sem = refs[:12]
    row = lax.axis_index("row")
    col = lax.axis_index("col")
    tile = p_ref.shape[0]
    half = tile // 2
    fold = row_count // col_count
    per = fold // chunks
    home = lax.div(row, fold)
    place = lax.rem(row, fold)
    turn = lax.div(place, chunks)
    count = row_count * col_count
    me = row * col_count + col
    is_home = home == col
    takes = lax.rem(place, chunks) == chunk
    if last:
        loads = [
            pltpu.make_async_copy(
                product.at[:, pl.ds(k * tile, tile)],
                p_ref.at[:, pl.ds((q + chunks * k) * tile, tile)],
                load_sem.at[q * per + k],
            )
            for q, product in enumerate(products)
            for k in range(per)
        ]
    else:
        loads = [pltpu.make_async_copy(products[0], p_ref, load_sem.at[0])]
    for load in loads:
        load.start()
    if last:
        diagonal_load = pltpu.make_async_copy(diagonal_ref, out_ref, self_sem.at[3])
        diagonal_load.start()

    barrier = pltpu.get_barrier_semaphore()

    def greet(d, carry):
        other = lax.rem(me + d, count)
        pl.semaphore_signal(
            barrier,
            inc=1,
            device_id=(lax.div(other, col_count), lax.rem(other, col_count)),
            device_id_type=MESH,
        )
        return carry

    lax.fori_loop(1, count, greet, 0)
    pl.semaphore_wait(barrier, count - 1)
    for load in loads:
        load.wait()

    def columns(s):
        return pl.ds(pl.multiple_of(s * tile, tile), tile)

    def remote(src, dst, send, arrive, to_row, to_col):
        return pltpu.make_async_remote_copy(
            src_ref=src,
            dst_ref=dst,
            send_sem=send,
            recv_sem=arrive,
            device_id=(to_row, to_col),
            device_id_type=MESH,
        )

    def spot(k):
        kk = lax.rem(turn + k, per)
        return kk, chunk + chunks * kk

    def own_direct(k):
        kk, s = spot(k)
        near = col * fold + s
        return [
            remote(packed.at[kk, h], recv.at[place, h], own_send.at[kk, h], recv_sem.at[place, h], near, col)
            for h in range(2)
        ]

    def own_relayed(k):
        kk, s = spot(k)
        near = col * fold + s
        slot_a = col - (col > home).astype(jnp.int32)
        slot_b = row - fold * (home > col).astype(jnp.int32)
        return [
            remote(packed.at[kk, 0], relay_a.at[slot_a, kk], own_send.at[kk, 0], arrive_a.at[slot_a, kk], row, home),
            remote(packed.at[kk, 1], relay_b.at[slot_b], own_send.at[kk, 1], arrive_b.at[slot_b], near, col),
        ]

    def own_local():
        return [pltpu.make_async_copy(packed.at[turn, h], recv.at[place, h], self_sem.at[h]) for h in range(2)]

    def pack(k):
        kk, s = spot(k)
        cols = columns(s) if last else columns(kk)
        for h in range(2):
            peak = jnp.max(jnp.abs(p_ref[pl.ds(h * half, half), cols]), axis=0, keepdims=True)
            code = jnp.floor(jnp.log2(jnp.maximum(peak, 1e-30)) * 128.0) + 2.0
            grow = jnp.exp2(code * (-1.0 / 128.0)) * 32767.0
            packed[kk, h, pl.ds(half, 16)] = jnp.broadcast_to(code, (16, tile)).astype(jnp.int32).astype(jnp.int16)
            rows = min(64, half)
            for r in range(0, half, rows):
                value = p_ref[pl.ds(h * half + r, rows), cols] * grow
                packed[kk, h, pl.ds(r, rows)] = jnp.floor(value + 0.5).astype(jnp.int32).astype(jnp.int16)

    def exchange(phase, start):
        def one(d, carry):
            other = lax.rem(me + d, count)
            copy = remote(
                mine.at[phase],
                sums.at[phase, me],
                sum_send.at[phase, d],
                sum_recv.at[phase, me],
                lax.div(other, col_count),
                lax.rem(other, col_count),
            )
            if start:
                copy.start()
            else:
                copy.wait_send()
            return carry

        lax.fori_loop(1, count, one, 0)

    def gather_sums(phase):
        def one(d, carry):
            other = lax.rem(me + d, count)
            remote(
                mine.at[phase],
                sums.at[phase, other],
                sum_send.at[phase, d],
                sum_recv.at[phase, other],
                lax.div(other, col_count),
                lax.rem(other, col_count),
            ).wait_recv()
            return carry

        lax.fori_loop(1, count, one, 0)
        sums[phase, pl.ds(me, 1)] = mine[pl.ds(phase, 1)]
        every = jnp.sum(sums[phase], axis=0)
        return jnp.sum(every[0:8]), jnp.sum(every[8:16])

    def fold_sum(x):
        lanes = x.shape[1] // 128
        out = x[:, 0:128]
        for q in range(1, lanes):
            out = out + x[:, q * 128 : (q + 1) * 128]
        return jnp.sum(out.reshape(x.shape[0] // 8, 8, 128), axis=0)

    zero = jnp.zeros((8, 128), jnp.float32)
    if last:
        step_rows = min(32, tile)

        def early(r, carry):
            rows = pl.ds(pl.multiple_of(r * step_rows, step_rows), step_rows)
            c = c_ref[rows, :].astype(jnp.float32)
            return carry[0] + fold_sum(c * p_ref[rows, :]), carry[1] + fold_sum(c * c)

        proj, weight = lax.fori_loop(0, tile // step_rows, early, (zero, zero))
        mine[0, 0:8] = proj
        mine[0, 8:16] = weight
        exchange(0, True)

    def launch(k, carry):
        pack(k)

        @pl.when(jnp.logical_not(is_home))
        def _():
            for copy in own_relayed(k):
                copy.start()

        @pl.when(jnp.logical_and(is_home, jnp.logical_or(k > 0, jnp.logical_not(takes))))
        def _():
            for copy in own_direct(k):
                copy.start()

        return carry

    lax.fori_loop(0, per, launch, 0)

    @pl.when(jnp.logical_and(is_home, takes))
    def _():
        for copy in own_local():
            copy.start()
        for copy in own_local():
            copy.wait()

    def relay_first(t):
        slot = lax.div(t, per)
        group = slot + (slot >= col).astype(jnp.int32)
        kk, s = spot(lax.rem(t, per))
        return slot, kk, remote(
            relay_a.at[slot, kk], recv.at[place, 0], send_a.at[t], recv_sem.at[place, 0], group * fold + s, col
        )

    def relay_second(t):
        slot = lax.div(t, fold)
        group = slot + (slot >= col).astype(jnp.int32)
        far = lax.rem(place - lax.rem(t, fold) + fold, fold)
        slot_b = slot * fold + far
        return slot_b, remote(
            relay_b.at[slot_b], recv.at[far, 1], send_b.at[t], recv_sem.at[far, 1], row, group
        )

    @pl.when(is_home)
    def _():
        def step(t, carry):
            slot, kk, copy = relay_first(t)
            pltpu.make_async_copy(relay_a.at[slot, kk], relay_a.at[slot, kk], arrive_a.at[slot, kk]).wait()
            copy.start()
            return carry

        lax.fori_loop(0, (col_count - 1) * per, step, 0)

    @pl.when(jnp.logical_and(is_home, takes))
    def _():
        def step(t, carry):
            slot_b, copy = relay_second(t)
            pltpu.make_async_copy(relay_b.at[slot_b], relay_b.at[slot_b], arrive_b.at[slot_b]).wait()
            copy.start()
            return carry

        lax.fori_loop(0, (col_count - 1) * fold, step, 0)

    def await_piece(k):
        s = lax.rem(place - k + fold, fold)

        @pl.when(jnp.logical_and(takes, jnp.logical_not(jnp.logical_and(is_home, k == 0))))
        def _():
            for h in range(2):
                pltpu.make_async_copy(recv.at[s, h], recv.at[s, h], recv_sem.at[s, h]).wait()

    def settle():
        @pl.when(is_home)
        def _():
            def done(k, carry):
                @pl.when(jnp.logical_or(k > 0, jnp.logical_not(takes)))
                def _():
                    for copy in own_direct(k):
                        copy.wait_send()

                return carry

            lax.fori_loop(0, per, done, 0)

            def done_first(t, carry):
                relay_first(t)[-1].wait_send()
                return carry

            lax.fori_loop(0, (col_count - 1) * per, done_first, 0)

        @pl.when(jnp.logical_and(is_home, takes))
        def _():
            def done_second(t, carry):
                relay_second(t)[-1].wait_send()
                return carry

            lax.fori_loop(0, (col_count - 1) * fold, done_second, 0)

        @pl.when(jnp.logical_not(is_home))
        def _():
            def done(k, carry):
                for copy in own_relayed(k):
                    copy.wait_send()
                return carry

            lax.fori_loop(0, per, done, 0)

    if not last:

        def hold(k, carry):
            await_piece(k)
            return carry

        lax.fori_loop(0, fold, hold, 0)
        settle()
        return

    for q, ready in enumerate(arrived):

        @pl.when(lax.rem(place, chunks) == q)
        def _():
            fetch = pltpu.make_async_copy(ready, recv, self_sem.at[2])
            fetch.start()
            fetch.wait()

    proj, weight = gather_sums(0)
    theta = 2.0 * proj / weight
    diagonal_load.wait()

    piece = min(128, tile)

    def finish(k, carry):
        s = lax.rem(place - k + fold, fold)

        await_piece(k)

        def part(r, carry):
            squares, spread = carry
            rows = pl.ds(pl.multiple_of(r * piece, piece), piece)
            for h in range(2):
                cols = pl.ds(pl.multiple_of(s * tile + h * half, half), half)
                code = recv[s, h, pl.ds(half, 16), rows].astype(jnp.int32).astype(jnp.float32)[0:1]
                shrink = jnp.exp2(code * (1.0 / 128.0)) * (1.0 / 32767.0)
                value = recv[s, h, pl.ds(0, half), rows].astype(jnp.int32).astype(jnp.float32)
                turned = (value * shrink).T
                sigma = p_ref[rows, cols] + turned
                residual = sigma - theta * c_ref[rows, cols].astype(jnp.float32)
                update = residual / jnp.maximum(jnp.abs(out_ref[rows, cols] - theta), 1.0)
                out_ref[rows, cols] = update
                squares = squares + fold_sum(residual * residual)
                spread = spread + fold_sum(update * update)
            return squares, spread

        return lax.fori_loop(0, tile // piece, part, carry)

    squares, spread = lax.fori_loop(0, fold, finish, (zero, zero))
    mine[1, 0:8] = squares
    mine[1, 8:16] = spread
    exchange(1, True)
    squares, spread = gather_sums(1)
    stats_ref[0] = theta
    stats_ref[1] = squares / total
    stats_ref[2] = spread / total

    exchange(0, False)
    exchange(1, False)
    settle()


def turn(chunk, chunks, products, arrived, coeff, diagonal, strings):
    tile_rows, tile_cols = coeff.shape
    row_count = lax.axis_size("row")
    col_count = lax.axis_size("col")
    fold = row_count // col_count
    per = fold // chunks
    count = row_count * col_count
    tall = tile_rows // 2 + 16
    others = max(col_count - 1, 1)
    vmem = pl.BlockSpec(memory_space=pltpu.VMEM)
    anywhere = pl.BlockSpec(memory_space=pl.ANY)
    dma = pltpu.SemaphoreType.DMA
    last = chunk == chunks - 1
    arrival = (fold, 2, tall, tile_rows)
    scratch = [
        pltpu.VMEM((tile_rows, tile_cols if last else tile_cols // chunks), jnp.float32),
        pltpu.VMEM((per, 2, tall, tile_rows), jnp.int16),
        pltpu.VMEM((others, per, tall, tile_rows), jnp.int16),
        pltpu.VMEM((others * fold, tall, tile_rows), jnp.int16),
        dma((fold,)),
        dma((per, 2)),
        dma((fold, 2)),
        dma((others, per)),
        dma((others * fold,)),
        dma((others * per,)),
        dma((others * fold,)),
        dma((4,)),
    ]
    if last:
        operands = (*products, *arrived, diagonal, coeff)
        in_specs = [anywhere] * (2 * chunks) + [vmem]
        out_shape = (
            jax.ShapeDtypeStruct((tile_rows, tile_cols), jnp.float32),
            jax.ShapeDtypeStruct((3,), jnp.float32),
        )
        out_specs = (vmem, pl.BlockSpec(memory_space=pltpu.SMEM))
        scratch = [
            pltpu.VMEM(arrival, jnp.int16),
            *scratch,
            pltpu.VMEM((2, 16, 128), jnp.float32),
            pltpu.VMEM((2, count, 16, 128), jnp.float32),
            dma((2, count)),
            dma((2, count)),
        ]
    else:
        operands = (products[chunk],)
        in_specs = [anywhere]
        out_shape = jax.ShapeDtypeStruct(arrival, jnp.int16)
        out_specs = vmem
    return pl.pallas_call(
        functools.partial(turn_kernel, row_count, col_count, float(strings) * float(strings), chunk, chunks),
        out_shape=out_shape,
        in_specs=in_specs,
        out_specs=out_specs,
        scratch_shapes=scratch,
        compiler_params=pltpu.CompilerParams(
            collective_id=chunk, has_side_effects=True, vmem_limit_bytes=(60 if last else 24) * 1024 * 1024
        ),
        name=f"turn_{chunk}",
    )(*operands)


def gather_kernel(ham_ref, mask_ref, coeff_ref, ring_ref, acc_ref, wide, ring, m_ref, buf, load_sem, send_sem, wide_sem, ring_sem):
    rows, strings = ham_ref.shape
    half = coeff_ref.shape[1]
    quarter = rows // 4
    row = lax.axis_index("row")
    col = lax.axis_index("col")
    core = lax.rem(row, 2)
    x = lax.rem(lax.div(row, 2), 2)
    low = lax.rem(lax.div(row, 4), 2)
    high = lax.div(row, 8)
    diag = high == col
    mid = low != high
    fold = half // rows

    def device(h, l, a, k):
        return ((h * 2 + l) * 2 + a) * 2 + k

    targets = {
        "x": (device(high, low, 1 - x, core), col),
        "z": (device(high, 1 - low, x, core), col),
        "y": (row, 1 - col),
        "c": (device(high, low, x, 1 - core), col),
        "cut": (device(1 - high, 1 - low, x, core), col),
    }

    ham_load = pltpu.make_async_copy(ham_ref, m_ref, load_sem.at[0])
    ham_load.start()

    barrier = pltpu.get_barrier_semaphore()
    for target in targets.values():
        pl.semaphore_signal(barrier, inc=1, device_id=target, device_id_type=MESH)
    pl.semaphore_wait(barrier, len(targets))

    def spot(l, a, k):
        return (l * 2 + a) * 2 + k

    def part(ref, t, q):
        return ref.at[t, pl.ds(q * quarter, quarter)]

    sent = []

    def send(way, ref, sems, t, q, own=None):
        src = part(ref, t, q) if own is None else own.at[pl.ds(q * quarter, quarter)]
        copy = pltpu.make_async_remote_copy(
            src_ref=src,
            dst_ref=part(ref, t, q),
            send_sem=send_sem.at[len(sent)],
            recv_sem=sems.at[t, q],
            device_id=targets[way],
            device_id_type=MESH,
        )
        sent.append((copy, way == "cut"))
        if way == "cut":

            @pl.when(mid)
            def _():
                copy.start()
        else:
            copy.start()

    def settle():
        for copy, only_mid in sent:
            if only_mid:

                @pl.when(mid)
                def _():
                    copy.wait_send()
            else:
                copy.wait_send()
        sent.clear()

    def arrive(ref, sems, t, q):
        view = part(ref, t, q)
        pltpu.make_async_copy(view, view, sems.at[t, q]).wait()

    def pass_on(ref, sems, t, q, *ways):
        arrive(ref, sems, t, q)
        for way in ways:
            send(way, ref, sems, t, q)
        send("c", ref, sems, t, q)

    def load(ref, sems, l, a, width, own=None):
        mine, other = spot(l, a, core), spot(l, a, 1 - core)
        for q in range(4):
            arrive(ref, sems, other, q)
        src = ref.at[mine] if own is None else own
        first = pltpu.make_async_copy(
            src, buf.at[pl.ds(pl.multiple_of(core * rows, rows), rows), pl.ds(0, width)], load_sem.at[1]
        )
        second = pltpu.make_async_copy(
            ref.at[other],
            buf.at[pl.ds(pl.multiple_of((1 - core) * rows, rows), rows), pl.ds(0, width)],
            load_sem.at[2],
        )
        first.start()
        second.start()
        first.wait()
        second.wait()

    def block(n):
        return pl.ds(pl.multiple_of(n * rows, rows), rows)

    near = col * fold
    away = (1 - col) * fold

    def plain(l, a):
        base = spot(l, a, 0)
        left = pl.ds(pl.multiple_of((away + base) * rows, rows), 2 * rows)

        def one(n, carry):
            acc_ref[:, block(n)] += jnp.dot(m_ref[:, left], buf[:, block(n)], preferred_element_type=jnp.float32)
            return carry

        lax.fori_loop(0, fold, one, 0)

    def turned(l, a):
        base = spot(l, a, 0)

        def one(n, carry):
            total = jnp.zeros((rows, rows), jnp.float32)
            for k in range(0, fold, 2):
                left = pl.ds(pl.multiple_of((away + k) * rows, rows), 2 * rows)
                total = total + lax.dot_general(
                    m_ref[:, left],
                    buf[block(n), pl.ds(k * rows, 2 * rows)],
                    (((1,), (1,)), ((), ())),
                    preferred_element_type=jnp.float32,
                )
            acc_ref[:, block(base + n)] += total
            return carry

        lax.fori_loop(0, 2, one, 0)

    def mirrored(l, a):
        base = spot(l, a, 0)

        def lane(k, carry):
            t = base + k

            def one(d, inner):
                s = lax.rem(t + d, fold)
                tile = buf[block(k), block(d)]
                acc_ref[:, block(s)] += jnp.dot(
                    m_ref[:, block(near + t)], tile, preferred_element_type=jnp.float32
                )

                @pl.when(d > 0)
                def _():
                    acc_ref[:, block(t)] += lax.dot_general(
                        m_ref[:, block(near + s)],
                        tile,
                        (((1,), (1,)), ((), ())),
                        preferred_element_type=jnp.float32,
                    )

                return inner

            last = jnp.where(t < fold // 2, fold // 2 + 1, fold // 2)
            lax.fori_loop(0, last, one, 0)
            return carry

        lax.fori_loop(0, 2, lane, 0)

    def prepare():
        ham_load.wait()
        groups, blocks = mask_ref.shape
        size = strings // blocks
        step = min(1024, strings)
        pick = lax.broadcasted_iota(jnp.int32, (rows, groups), 0) // size == lax.broadcasted_iota(
            jnp.int32, (rows, groups), 1
        )
        tall = jnp.dot(
            pick.astype(jnp.bfloat16), mask_ref[...].astype(jnp.bfloat16), preferred_element_type=jnp.float32
        ).astype(jnp.bfloat16)

        def one(n, carry):
            cols = pl.ds(pl.multiple_of(n * step, step), step)
            spread = (n * step + lax.broadcasted_iota(jnp.int32, (blocks, step), 1)) // size == lax.broadcasted_iota(
                jnp.int32, (blocks, step), 0
            )
            weight = jnp.dot(tall, spread.astype(jnp.bfloat16), preferred_element_type=jnp.float32)
            m_ref[:, cols] = m_ref[:, cols] * weight.astype(jnp.bfloat16)
            acc_ref[:, pl.ds(pl.multiple_of(n * (step // 2), step // 2), step // 2)] = jnp.zeros(
                (rows, step // 2), jnp.float32
            )
            return carry

        lax.fori_loop(0, strings // step, one, 0)

    reach = ring.shape[2]
    W = (wide, wide_sem)
    R = (ring, ring_sem)
    own = spot(low, x, core)
    t_x = spot(low, 1 - x, core)
    t_z = spot(1 - low, x, core)
    t_d = spot(1 - low, 1 - x, core)

    @pl.when(diag)
    def _():
        def mine(q):
            for way in ("x", "z", "cut", "c"):
                send(way, *R, own, q, ring_ref)

        mine(0)
        mine(1)
        prepare()
        pass_on(*R, t_z, 0, "cut")
        pass_on(*R, t_x, 0, "z")
        pass_on(*W, own, 0, "z")
        mine(2)
        pass_on(*R, t_z, 1, "cut")
        pass_on(*R, t_x, 1, "z")
        pass_on(*W, t_x, 0, "z")
        pass_on(*W, t_z, 0, "y")
        mine(3)
        pass_on(*W, t_z, 2, "x")
        pass_on(*W, t_d, 0, "y")
        pass_on(*R, t_z, 2, "x", "cut")
        pass_on(*R, t_x, 2)
        pass_on(*W, own, 3, "x")
        pass_on(*W, t_d, 2, "y")
        pass_on(*R, t_z, 3, "x", "cut")
        pass_on(*R, t_x, 3)
        load(*R, low, x, reach, ring_ref)
        mirrored(low, x)
        pass_on(*W, t_x, 1, "z")
        pass_on(*W, t_x, 3, "y")
        load(*R, 1 - low, x, reach)
        mirrored(1 - low, x)
        pass_on(*W, t_z, 3, "x")
        pass_on(*W, t_d, 1, "y")
        for q in range(4):
            pass_on(*R, t_d, q)
        load(*R, low, 1 - x, reach)
        mirrored(low, 1 - x)
        pass_on(*W, own, 1, "z")
        pass_on(*W, t_d, 3, "y")
        load(*R, 1 - low, 1 - x, reach)
        mirrored(1 - low, 1 - x)
        pass_on(*W, own, 2, "x")
        load(*W, 1 - low, 1 - x, half)
        turned(1 - low, 1 - x)
        pass_on(*W, t_z, 1)
        pass_on(*W, t_x, 2)
        load(*W, low, x, half)
        turned(low, x)
        load(*W, 1 - low, x, half)
        turned(1 - low, x)
        load(*W, low, 1 - x, half)
        turned(low, 1 - x)
        settle()

    @pl.when(jnp.logical_not(diag))
    def _():
        def mine(way, q):
            send(way, *W, own, q, coeff_ref)

        mine("y", 0)
        mine("x", 0)
        mine("z", 2)
        mine("x", 1)
        mine("z", 3)
        mine("x", 2)
        mine("z", 1)
        for q in range(4):
            mine("c", q)
        pass_on(*W, t_x, 0, "y")
        pass_on(*W, t_z, 2, "y")
        mine("y", 3)
        prepare()
        pass_on(*W, t_x, 1, "y")
        pass_on(*W, t_z, 3, "y")
        mine("y", 1)
        mine("y", 2)
        front = 1 - col
        back = col
        a_own, b_own = spot(front, x, core), spot(back, x, core)
        a_far, b_far = spot(front, 1 - x, core), spot(back, 1 - x, core)

        def inward(t, q):
            arrive(*R, t, q)
            send("x", *R, t, q)
            copy = pltpu.make_async_remote_copy(
                src_ref=part(ring, t, q),
                dst_ref=part(ring, t, q),
                send_sem=send_sem.at[len(sent)],
                recv_sem=ring_sem.at[t, q],
                device_id=targets["z"],
                device_id_type=MESH,
            )
            sent.append((copy, True))

            @pl.when(mid)
            def _():
                copy.start()

            send("c", *R, t, q)

        load(*W, low, x, half, coeff_ref)
        plain(low, x)
        inward(a_own, 0)
        pass_on(*W, t_x, 2)
        pass_on(*W, t_z, 1)
        inward(b_own, 0)
        pass_on(*W, t_z, 0)
        inward(a_own, 1)
        inward(b_own, 1)
        pass_on(*W, t_d, 0)
        pass_on(*R, a_far, 0)
        pass_on(*W, t_d, 2)
        inward(a_own, 2)
        pass_on(*R, b_far, 0)
        inward(b_own, 2)
        load(*W, 1 - low, x, half)
        plain(1 - low, x)
        pass_on(*W, t_x, 3)
        pass_on(*R, a_far, 1)
        inward(a_own, 3)
        pass_on(*R, b_far, 1)
        load(*W, low, 1 - x, half)
        plain(low, 1 - x)
        pass_on(*W, t_d, 1)
        inward(b_own, 3)
        pass_on(*R, a_far, 2)
        load(*R, front, x, reach)
        mirrored(front, x)
        pass_on(*R, b_far, 2)
        pass_on(*W, t_d, 3)
        load(*R, back, x, reach)
        mirrored(back, x)
        pass_on(*R, a_far, 3)
        pass_on(*R, b_far, 3)
        load(*W, 1 - low, 1 - x, half)
        plain(1 - low, 1 - x)
        load(*R, front, 1 - x, reach)
        mirrored(front, 1 - x)
        load(*R, back, 1 - x, reach)
        mirrored(back, 1 - x)
        settle()


def gather_products(ham, tile_mask, coeff):
    rows, strings = ham.shape
    half = coeff.shape[1]
    fold = half // rows
    row = lax.axis_index("row")
    reach = (fold // 2 + 1) * rows
    start = jnp.where(lax.div(row, fold) == lax.axis_index("col"), lax.rem(row, fold) * rows, 0)
    doubled = jnp.concatenate([coeff, coeff[:, : reach - rows]], axis=1)
    ring = lax.dynamic_slice(doubled, (0, start), (rows, reach))
    anywhere = pl.BlockSpec(memory_space=pl.ANY)
    vmem = pl.BlockSpec(memory_space=pltpu.VMEM)
    dma = pltpu.SemaphoreType.DMA
    return pl.pallas_call(
        gather_kernel,
        out_shape=(
            jax.ShapeDtypeStruct((rows, half), jnp.float32),
            jax.ShapeDtypeStruct((fold, rows, half), jnp.bfloat16),
            jax.ShapeDtypeStruct((fold, rows, reach), jnp.bfloat16),
        ),
        in_specs=[anywhere, vmem, anywhere, anywhere],
        out_specs=(vmem, anywhere, anywhere),
        scratch_shapes=[
            pltpu.VMEM((rows, strings), jnp.bfloat16),
            pltpu.VMEM((2 * rows, half), jnp.bfloat16),
            dma((3,)),
            dma((80,)),
            dma((fold, 4)),
            dma((fold, 4)),
        ],
        compiler_params=pltpu.CompilerParams(
            collective_id=9, has_side_effects=True, vmem_limit_bytes=50 * 1024 * 1024
        ),
        name="gather_products",
    )(ham, tile_mask, coeff, ring)[0]


CHUNKS = 2


def body(ham, coeff, tile_mask, occupation, orbital_energy, coulomb):
    tile_rows, strings = ham.shape
    tile_cols = coeff.shape[1]
    fold = tile_cols // tile_rows
    direct = lax.axis_size("col") == 2 and lax.axis_size("row") == 16
    occ_float = occupation.astype(jnp.float32)
    occ_alpha = lax.dynamic_slice_in_dim(occ_float, lax.axis_index("row") * tile_rows, tile_rows, 1)
    occ_beta = lax.dynamic_slice_in_dim(occ_float, lax.axis_index("col") * tile_cols, tile_cols, 1)
    energy_alpha = jnp.dot(orbital_energy, occ_alpha, precision=HIGH)
    energy_beta = jnp.dot(orbital_energy, occ_beta, precision=HIGH)
    coupling = jnp.dot(jnp.dot(occ_alpha.T, coulomb, precision=HIGH), occ_beta, precision=HIGH)
    diagonal = energy_alpha[:, None] + energy_beta[None, :] + coupling
    if direct:
        result = turn(0, 1, [gather_products(ham, tile_mask, coeff)], [], coeff, diagonal, strings)
    else:
        mask_cols = tile_mask.shape[1]
        block_size = strings // mask_cols
        mask_rows = tile_rows // block_size
        weights = tile_mask.astype(jnp.bfloat16)[:, None, :, None]
        masked = (ham.reshape(mask_rows, block_size, mask_cols, block_size) * weights).reshape(tile_rows, strings)
        chunks = math.gcd(CHUNKS, fold)
        products = []
        arrived = []
        for q in range(chunks):
            part = jnp.concatenate(
                [coeff[:, s * tile_rows : (s + 1) * tile_rows] for s in range(q, fold, chunks)], axis=1
            )
            gathered = with_layout_constraint(lax.all_gather(part, "row", axis=0, tiled=True), Layout((0, 1)))
            products.append(jnp.dot(masked, gathered, preferred_element_type=jnp.float32))
            result = turn(q, chunks, products, arrived, coeff, diagonal, strings)
            if q < chunks - 1:
                arrived.append(result)
    update, sums = result
    correction = update * lax.rsqrt(sums[2] + 1e-06)
    stats = jnp.stack([sums[0], jnp.sqrt(sums[1])])
    return (correction, stats)


def solution(mesh):
    in_specs = (P("row", None), P("row", "col"), P("row", None), P(), P(), P())
    out_specs = (P("row", "col"), P())
    return jax.shard_map(body, mesh=mesh, in_specs=in_specs, out_specs=out_specs, check_vma=False)
```

```python
import functools
import math

import jax
import jax.numpy as jnp
from jax import lax
from jax.experimental import pallas as pl
from jax.experimental.layout import Layout, with_layout_constraint
from jax.experimental.pallas import tpu as pltpu
from jax.sharding import PartitionSpec as P

MESH = pl.DeviceIdType.MESH
HIGH = lax.Precision.HIGHEST


def turn_kernel(row_count, col_count, total, chunk, chunks, *refs):
    last = chunk == chunks - 1
    if last:
        products, arrived = refs[:chunks], refs[chunks : 2 * chunks - 1]
        diagonal_ref, c_ref, out_ref, stats_ref, recv = refs[2 * chunks - 1 : 2 * chunks + 4]
        refs = refs[2 * chunks + 4 :]
        mine, sums, sum_send, sum_recv = refs[-4:]
    else:
        products = refs[:1]
        recv = refs[1]
        refs = refs[2:]
    p_ref, packed, relay_a, relay_b, load_sem, own_send, recv_sem, arrive_a, arrive_b, send_a, send_b, self_sem = refs[:12]
    row = lax.axis_index("row")
    col = lax.axis_index("col")
    tile = p_ref.shape[0]
    half = tile // 2
    fold = row_count // col_count
    per = fold // chunks
    home = lax.div(row, fold)
    place = lax.rem(row, fold)
    turn = lax.div(place, chunks)
    count = row_count * col_count
    me = row * col_count + col
    is_home = home == col
    takes = lax.rem(place, chunks) == chunk
    if last:
        loads = [
            pltpu.make_async_copy(
                product.at[:, pl.ds(k * tile, tile)],
                p_ref.at[:, pl.ds((q + chunks * k) * tile, tile)],
                load_sem.at[q * per + k],
            )
            for q, product in enumerate(products)
            for k in range(per)
        ]
    else:
        loads = [pltpu.make_async_copy(products[0], p_ref, load_sem.at[0])]
    for load in loads:
        load.start()
    if last:
        diagonal_load = pltpu.make_async_copy(diagonal_ref, out_ref, self_sem.at[3])
        diagonal_load.start()

    barrier = pltpu.get_barrier_semaphore()

    def greet(d, carry):
        other = lax.rem(me + d, count)
        pl.semaphore_signal(
            barrier,
            inc=1,
            device_id=(lax.div(other, col_count), lax.rem(other, col_count)),
            device_id_type=MESH,
        )
        return carry

    lax.fori_loop(1, count, greet, 0)
    pl.semaphore_wait(barrier, count - 1)
    for load in loads:
        load.wait()

    def columns(s):
        return pl.ds(pl.multiple_of(s * tile, tile), tile)

    def remote(src, dst, send, arrive, to_row, to_col):
        return pltpu.make_async_remote_copy(
            src_ref=src,
            dst_ref=dst,
            send_sem=send,
            recv_sem=arrive,
            device_id=(to_row, to_col),
            device_id_type=MESH,
        )

    def spot(k):
        kk = lax.rem(turn + k, per)
        return kk, chunk + chunks * kk

    def own_direct(k):
        kk, s = spot(k)
        near = col * fold + s
        return [
            remote(packed.at[kk, h], recv.at[place, h], own_send.at[kk, h], recv_sem.at[place, h], near, col)
            for h in range(2)
        ]

    def own_relayed(k):
        kk, s = spot(k)
        near = col * fold + s
        slot_a = col - (col > home).astype(jnp.int32)
        slot_b = row - fold * (home > col).astype(jnp.int32)
        return [
            remote(packed.at[kk, 0], relay_a.at[slot_a, kk], own_send.at[kk, 0], arrive_a.at[slot_a, kk], row, home),
            remote(packed.at[kk, 1], relay_b.at[slot_b], own_send.at[kk, 1], arrive_b.at[slot_b], near, col),
        ]

    def own_local():
        return [pltpu.make_async_copy(packed.at[turn, h], recv.at[place, h], self_sem.at[h]) for h in range(2)]

    def pack(k):
        kk, s = spot(k)
        cols = columns(s) if last else columns(kk)
        for h in range(2):
            peak = jnp.max(jnp.abs(p_ref[pl.ds(h * half, half), cols]), axis=0, keepdims=True)
            code = jnp.floor(jnp.log2(jnp.maximum(peak, 1e-30)) * 128.0) + 2.0
            grow = jnp.exp2(code * (-1.0 / 128.0)) * 32767.0
            packed[kk, h, pl.ds(half, 16)] = jnp.broadcast_to(code, (16, tile)).astype(jnp.int32).astype(jnp.int16)
            rows = min(64, half)
            for r in range(0, half, rows):
                value = p_ref[pl.ds(h * half + r, rows), cols] * grow
                packed[kk, h, pl.ds(r, rows)] = jnp.floor(value + 0.5).astype(jnp.int32).astype(jnp.int16)

    def exchange(phase, start):
        def one(d, carry):
            other = lax.rem(me + d, count)
            copy = remote(
                mine.at[phase],
                sums.at[phase, me],
                sum_send.at[phase, d],
                sum_recv.at[phase, me],
                lax.div(other, col_count),
                lax.rem(other, col_count),
            )
            if start:
                copy.start()
            else:
                copy.wait_send()
            return carry

        lax.fori_loop(1, count, one, 0)

    def gather_sums(phase):
        def one(d, carry):
            other = lax.rem(me + d, count)
            remote(
                mine.at[phase],
                sums.at[phase, other],
                sum_send.at[phase, d],
                sum_recv.at[phase, other],
                lax.div(other, col_count),
                lax.rem(other, col_count),
            ).wait_recv()
            return carry

        lax.fori_loop(1, count, one, 0)
        sums[phase, pl.ds(me, 1)] = mine[pl.ds(phase, 1)]
        every = jnp.sum(sums[phase], axis=0)
        return jnp.sum(every[0:8]), jnp.sum(every[8:16])

    def fold_sum(x):
        lanes = x.shape[1] // 128
        out = x[:, 0:128]
        for q in range(1, lanes):
            out = out + x[:, q * 128 : (q + 1) * 128]
        return jnp.sum(out.reshape(x.shape[0] // 8, 8, 128), axis=0)

    zero = jnp.zeros((8, 128), jnp.float32)
    if last:
        step_rows = min(32, tile)

        def early(r, carry):
            rows = pl.ds(pl.multiple_of(r * step_rows, step_rows), step_rows)
            c = c_ref[rows, :].astype(jnp.float32)
            return carry[0] + fold_sum(c * p_ref[rows, :]), carry[1] + fold_sum(c * c)

        proj, weight = lax.fori_loop(0, tile // step_rows, early, (zero, zero))
        mine[0, 0:8] = proj
        mine[0, 8:16] = weight
        exchange(0, True)

    def launch(k, carry):
        pack(k)

        @pl.when(jnp.logical_not(is_home))
        def _():
            for copy in own_relayed(k):
                copy.start()

        @pl.when(jnp.logical_and(is_home, jnp.logical_or(k > 0, jnp.logical_not(takes))))
        def _():
            for copy in own_direct(k):
                copy.start()

        return carry

    lax.fori_loop(0, per, launch, 0)

    @pl.when(jnp.logical_and(is_home, takes))
    def _():
        for copy in own_local():
            copy.start()
        for copy in own_local():
            copy.wait()

    def relay_first(t):
        slot = lax.div(t, per)
        group = slot + (slot >= col).astype(jnp.int32)
        kk, s = spot(lax.rem(t, per))
        return slot, kk, remote(
            relay_a.at[slot, kk], recv.at[place, 0], send_a.at[t], recv_sem.at[place, 0], group * fold + s, col
        )

    def relay_second(t):
        slot = lax.div(t, fold)
        group = slot + (slot >= col).astype(jnp.int32)
        far = lax.rem(place - lax.rem(t, fold) + fold, fold)
        slot_b = slot * fold + far
        return slot_b, remote(
            relay_b.at[slot_b], recv.at[far, 1], send_b.at[t], recv_sem.at[far, 1], row, group
        )

    @pl.when(is_home)
    def _():
        def step(t, carry):
            slot, kk, copy = relay_first(t)
            pltpu.make_async_copy(relay_a.at[slot, kk], relay_a.at[slot, kk], arrive_a.at[slot, kk]).wait()
            copy.start()
            return carry

        lax.fori_loop(0, (col_count - 1) * per, step, 0)

    @pl.when(jnp.logical_and(is_home, takes))
    def _():
        def step(t, carry):
            slot_b, copy = relay_second(t)
            pltpu.make_async_copy(relay_b.at[slot_b], relay_b.at[slot_b], arrive_b.at[slot_b]).wait()
            copy.start()
            return carry

        lax.fori_loop(0, (col_count - 1) * fold, step, 0)

    def await_piece(k):
        s = lax.rem(place - k + fold, fold)

        @pl.when(jnp.logical_and(takes, jnp.logical_not(jnp.logical_and(is_home, k == 0))))
        def _():
            for h in range(2):
                pltpu.make_async_copy(recv.at[s, h], recv.at[s, h], recv_sem.at[s, h]).wait()

    def settle():
        @pl.when(is_home)
        def _():
            def done(k, carry):
                @pl.when(jnp.logical_or(k > 0, jnp.logical_not(takes)))
                def _():
                    for copy in own_direct(k):
                        copy.wait_send()

                return carry

            lax.fori_loop(0, per, done, 0)

            def done_first(t, carry):
                relay_first(t)[-1].wait_send()
                return carry

            lax.fori_loop(0, (col_count - 1) * per, done_first, 0)

        @pl.when(jnp.logical_and(is_home, takes))
        def _():
            def done_second(t, carry):
                relay_second(t)[-1].wait_send()
                return carry

            lax.fori_loop(0, (col_count - 1) * fold, done_second, 0)

        @pl.when(jnp.logical_not(is_home))
        def _():
            def done(k, carry):
                for copy in own_relayed(k):
                    copy.wait_send()
                return carry

            lax.fori_loop(0, per, done, 0)

    if not last:

        def hold(k, carry):
            await_piece(k)
            return carry

        lax.fori_loop(0, fold, hold, 0)
        settle()
        return

    for q, ready in enumerate(arrived):

        @pl.when(lax.rem(place, chunks) == q)
        def _():
            fetch = pltpu.make_async_copy(ready, recv, self_sem.at[2])
            fetch.start()
            fetch.wait()

    proj, weight = gather_sums(0)
    theta = 2.0 * proj / weight
    diagonal_load.wait()

    piece = min(128, tile)

    def finish(k, carry):
        s = lax.rem(place - k + fold, fold)

        await_piece(k)

        def part(r, carry):
            squares, spread = carry
            rows = pl.ds(pl.multiple_of(r * piece, piece), piece)
            for h in range(2):
                cols = pl.ds(pl.multiple_of(s * tile + h * half, half), half)
                code = recv[s, h, pl.ds(half, 16), rows].astype(jnp.int32).astype(jnp.float32)[0:1]
                shrink = jnp.exp2(code * (1.0 / 128.0)) * (1.0 / 32767.0)
                value = recv[s, h, pl.ds(0, half), rows].astype(jnp.int32).astype(jnp.float32)
                turned = (value * shrink).T
                sigma = p_ref[rows, cols] + turned
                residual = sigma - theta * c_ref[rows, cols].astype(jnp.float32)
                update = residual / jnp.maximum(jnp.abs(out_ref[rows, cols] - theta), 1.0)
                out_ref[rows, cols] = update
                squares = squares + fold_sum(residual * residual)
                spread = spread + fold_sum(update * update)
            return squares, spread

        return lax.fori_loop(0, tile // piece, part, carry)

    squares, spread = lax.fori_loop(0, fold, finish, (zero, zero))
    mine[1, 0:8] = squares
    mine[1, 8:16] = spread
    exchange(1, True)
    squares, spread = gather_sums(1)
    stats_ref[0] = theta
    stats_ref[1] = squares / total
    stats_ref[2] = spread / total

    exchange(0, False)
    exchange(1, False)
    settle()


def turn(chunk, chunks, products, arrived, coeff, diagonal, strings):
    tile_rows, tile_cols = coeff.shape
    row_count = lax.axis_size("row")
    col_count = lax.axis_size("col")
    fold = row_count // col_count
    per = fold // chunks
    count = row_count * col_count
    tall = tile_rows // 2 + 16
    others = max(col_count - 1, 1)
    vmem = pl.BlockSpec(memory_space=pltpu.VMEM)
    anywhere = pl.BlockSpec(memory_space=pl.ANY)
    dma = pltpu.SemaphoreType.DMA
    last = chunk == chunks - 1
    arrival = (fold, 2, tall, tile_rows)
    scratch = [
        pltpu.VMEM((tile_rows, tile_cols if last else tile_cols // chunks), jnp.float32),
        pltpu.VMEM((per, 2, tall, tile_rows), jnp.int16),
        pltpu.VMEM((others, per, tall, tile_rows), jnp.int16),
        pltpu.VMEM((others * fold, tall, tile_rows), jnp.int16),
        dma((fold,)),
        dma((per, 2)),
        dma((fold, 2)),
        dma((others, per)),
        dma((others * fold,)),
        dma((others * per,)),
        dma((others * fold,)),
        dma((4,)),
    ]
    if last:
        operands = (*products, *arrived, diagonal, coeff)
        in_specs = [anywhere] * (2 * chunks) + [vmem]
        out_shape = (
            jax.ShapeDtypeStruct((tile_rows, tile_cols), jnp.float32),
            jax.ShapeDtypeStruct((3,), jnp.float32),
        )
        out_specs = (vmem, pl.BlockSpec(memory_space=pltpu.SMEM))
        scratch = [
            pltpu.VMEM(arrival, jnp.int16),
            *scratch,
            pltpu.VMEM((2, 16, 128), jnp.float32),
            pltpu.VMEM((2, count, 16, 128), jnp.float32),
            dma((2, count)),
            dma((2, count)),
        ]
    else:
        operands = (products[chunk],)
        in_specs = [anywhere]
        out_shape = jax.ShapeDtypeStruct(arrival, jnp.int16)
        out_specs = vmem
    return pl.pallas_call(
        functools.partial(turn_kernel, row_count, col_count, float(strings) * float(strings), chunk, chunks),
        out_shape=out_shape,
        in_specs=in_specs,
        out_specs=out_specs,
        scratch_shapes=scratch,
        compiler_params=pltpu.CompilerParams(
            collective_id=chunk, has_side_effects=True, vmem_limit_bytes=(60 if last else 24) * 1024 * 1024
        ),
        name=f"turn_{chunk}",
    )(*operands)


def gather_kernel(
    ham_ref,
    mask_ref,
    coeff_ref,
    ring_ref,
    couple_ref,
    occ_ref,
    alpha_ref,
    beta_ref,
    acc_ref,
    wide,
    ring,
    diagonal_ref,
    m_ref,
    buf,
    load_sem,
    send_sem,
    wide_sem,
    ring_sem,
):
    rows, strings = ham_ref.shape
    half = coeff_ref.shape[1]
    quarter = rows // 4
    row = lax.axis_index("row")
    col = lax.axis_index("col")
    core = lax.rem(row, 2)
    x = lax.rem(lax.div(row, 2), 2)
    low = lax.rem(lax.div(row, 4), 2)
    high = lax.div(row, 8)
    diag = high == col
    mid = low != high
    fold = half // rows

    def device(h, l, a, k):
        return ((h * 2 + l) * 2 + a) * 2 + k

    targets = {
        "x": (device(high, low, 1 - x, core), col),
        "z": (device(high, 1 - low, x, core), col),
        "y": (row, 1 - col),
        "c": (device(high, low, x, 1 - core), col),
        "cut": (device(1 - high, 1 - low, x, core), col),
    }

    ham_load = pltpu.make_async_copy(ham_ref, m_ref, load_sem.at[0])
    ham_load.start()

    barrier = pltpu.get_barrier_semaphore()
    for target in targets.values():
        pl.semaphore_signal(barrier, inc=1, device_id=target, device_id_type=MESH)
    pl.semaphore_wait(barrier, len(targets))

    def spot(l, a, k):
        return (l * 2 + a) * 2 + k

    def part(ref, t, q):
        return ref.at[t, pl.ds(q * quarter, quarter)]

    end = jnp.logical_not(mid)
    sent = []

    def send(way, ref, sems, t, q, own=None, when=None):
        src = part(ref, t, q) if own is None else own.at[pl.ds(q * quarter, quarter)]
        if way == "cut":
            when = mid
        copy = pltpu.make_async_remote_copy(
            src_ref=src,
            dst_ref=part(ref, t, q),
            send_sem=send_sem.at[len(sent)],
            recv_sem=sems.at[t, q],
            device_id=targets[way],
            device_id_type=MESH,
        )
        sent.append((copy, when))
        if when is None:
            copy.start()
        else:

            @pl.when(when)
            def _():
                copy.start()

    def settle():
        for copy, when in sent:
            if when is None:
                copy.wait_send()
            else:

                @pl.when(when)
                def _():
                    copy.wait_send()

        sent.clear()

    def arrive(ref, sems, t, q):
        view = part(ref, t, q)
        pltpu.make_async_copy(view, view, sems.at[t, q]).wait()

    def pass_on(ref, sems, t, q, *ways):
        arrive(ref, sems, t, q)
        for way in ways:
            send(way, ref, sems, t, q)
        send("c", ref, sems, t, q)

    def load(ref, sems, l, a, width, own=None):
        mine, other = spot(l, a, core), spot(l, a, 1 - core)
        for q in range(4):
            arrive(ref, sems, other, q)
        src = ref.at[mine] if own is None else own
        first = pltpu.make_async_copy(
            src, buf.at[pl.ds(pl.multiple_of(core * rows, rows), rows), pl.ds(0, width)], load_sem.at[1]
        )
        second = pltpu.make_async_copy(
            ref.at[other],
            buf.at[pl.ds(pl.multiple_of((1 - core) * rows, rows), rows), pl.ds(0, width)],
            load_sem.at[2],
        )
        first.start()
        second.start()
        first.wait()
        second.wait()

    def block(n):
        return pl.ds(pl.multiple_of(n * rows, rows), rows)

    near = col * fold
    away = (1 - col) * fold

    def plain(l, a):
        base = spot(l, a, 0)
        left = pl.ds(pl.multiple_of((away + base) * rows, rows), 2 * rows)

        def one(n, carry):
            acc_ref[:, block(n)] += jnp.dot(m_ref[:, left], buf[:, block(n)], preferred_element_type=jnp.float32)
            return carry

        lax.fori_loop(0, fold, one, 0)

    def turned(l, a):
        base = spot(l, a, 0)

        def one(n, carry):
            total = jnp.zeros((rows, rows), jnp.float32)
            for k in range(0, fold, 2):
                left = pl.ds(pl.multiple_of((away + k) * rows, rows), 2 * rows)
                total = total + lax.dot_general(
                    m_ref[:, left],
                    buf[block(n), pl.ds(k * rows, 2 * rows)],
                    (((1,), (1,)), ((), ())),
                    preferred_element_type=jnp.float32,
                )
            acc_ref[:, block(base + n)] += total
            return carry

        lax.fori_loop(0, 2, one, 0)

    def mirrored(l, a):
        base = spot(l, a, 0)

        def lane(k, carry):
            t = base + k

            def one(d, inner):
                s = lax.rem(t + d, fold)
                tile = buf[block(k), block(d)]
                acc_ref[:, block(s)] += jnp.dot(
                    m_ref[:, block(near + t)], tile, preferred_element_type=jnp.float32
                )

                @pl.when(d > 0)
                def _():
                    acc_ref[:, block(t)] += lax.dot_general(
                        m_ref[:, block(near + s)],
                        tile,
                        (((1,), (1,)), ((), ())),
                        preferred_element_type=jnp.float32,
                    )

                return inner

            last = jnp.where(t < fold // 2, fold // 2 + 1, fold // 2)
            lax.fori_loop(0, last, one, 0)
            return carry

        lax.fori_loop(0, 2, lane, 0)

    def prepare():
        ham_load.wait()
        groups, blocks = mask_ref.shape
        size = strings // blocks
        step = min(1024, strings)
        pick = lax.broadcasted_iota(jnp.int32, (rows, groups), 0) // size == lax.broadcasted_iota(
            jnp.int32, (rows, groups), 1
        )
        tall = jnp.dot(
            pick.astype(jnp.bfloat16), mask_ref[...].astype(jnp.bfloat16), preferred_element_type=jnp.float32
        ).astype(jnp.bfloat16)

        def one(n, carry):
            cols = pl.ds(pl.multiple_of(n * step, step), step)
            spread = (n * step + lax.broadcasted_iota(jnp.int32, (blocks, step), 1)) // size == lax.broadcasted_iota(
                jnp.int32, (blocks, step), 0
            )
            weight = jnp.dot(tall, spread.astype(jnp.bfloat16), preferred_element_type=jnp.float32)
            m_ref[:, cols] = m_ref[:, cols] * weight.astype(jnp.bfloat16)
            acc_ref[:, pl.ds(pl.multiple_of(n * (step // 2), step // 2), step // 2)] = jnp.zeros(
                (rows, step // 2), jnp.float32
            )
            return carry

        lax.fori_loop(0, strings // step, one, 0)

    def energies():
        def one(n, carry):
            diagonal_ref[:, block(n)] = (
                jnp.dot(couple_ref[...], occ_ref[:, block(n)], precision=HIGH, preferred_element_type=jnp.float32)
                + alpha_ref[...]
                + beta_ref[:, block(n)]
            )
            return carry

        lax.fori_loop(0, fold, one, 0)

    reach = ring.shape[2]
    W = (wide, wide_sem)
    R = (ring, ring_sem)
    own = spot(low, x, core)
    t_x = spot(low, 1 - x, core)
    t_z = spot(1 - low, x, core)
    t_d = spot(1 - low, 1 - x, core)

    @pl.when(diag)
    def _():
        def mine(way, q):
            send(way, *R, own, q, ring_ref)

        for q in range(4):
            mine("cut", q)
            mine("x", q)
            if q < 2:
                mine("z", q)
            mine("c", q)
        prepare()
        pass_on(*R, t_z, 0, "cut")
        pass_on(*W, own, 0, "z")
        pass_on(*R, t_z, 1, "cut")
        pass_on(*W, t_x, 0, "z")
        mine("z", 2)
        mine("z", 3)
        pass_on(*W, t_z, 0, "y")
        pass_on(*R, t_x, 0, "z")
        pass_on(*R, t_x, 1, "z")
        pass_on(*W, t_z, 2, "x")
        pass_on(*W, t_d, 0, "y")
        pass_on(*R, t_x, 2)
        pass_on(*R, t_x, 3)
        pass_on(*R, t_z, 2, "x", "cut")
        pass_on(*W, own, 3, "x")
        pass_on(*R, t_z, 3, "x", "cut")
        pass_on(*W, t_d, 2, "y")
        load(*R, low, x, reach, ring_ref)
        mirrored(low, x)
        pass_on(*W, t_x, 1, "z")
        pass_on(*W, t_x, 3, "y")
        energies()
        load(*R, low, 1 - x, reach)
        mirrored(low, 1 - x)
        pass_on(*W, t_z, 3, "x")
        pass_on(*W, t_d, 1, "y")
        load(*R, 1 - low, x, reach)
        mirrored(1 - low, x)
        pass_on(*W, own, 1, "z")
        for q in range(4):
            pass_on(*R, t_d, q)
        pass_on(*W, t_d, 3, "y")
        load(*R, 1 - low, 1 - x, reach)
        mirrored(1 - low, 1 - x)
        pass_on(*W, own, 2, "x")
        load(*W, 1 - low, 1 - x, half)
        turned(1 - low, 1 - x)
        load(*W, low, x, half)
        turned(low, x)
        pass_on(*W, t_z, 1)
        pass_on(*W, t_x, 2)
        load(*W, 1 - low, x, half)
        turned(1 - low, x)
        load(*W, low, 1 - x, half)
        turned(low, 1 - x)
        settle()

    @pl.when(jnp.logical_not(diag))
    def _():
        def mine(way, q, when=None):
            send(way, *W, own, q, coeff_ref, when)

        mine("y", 0)
        mine("x", 0)
        mine("z", 2)
        mine("x", 1)
        mine("z", 3)
        mine("x", 2)
        mine("z", 1, end)
        for q in range(4):
            mine("c", q)
        pass_on(*W, t_x, 0, "y")
        pass_on(*W, t_z, 2, "y")
        mine("y", 3)
        front = 1 - col
        back = col
        a_own, b_own = spot(front, x, core), spot(back, x, core)
        a_far, b_far = spot(front, 1 - x, core), spot(back, 1 - x, core)

        def inward(t, q):
            arrive(*R, t, q)
            send("x", *R, t, q)
            send("z", *R, t, q, None, mid)
            send("c", *R, t, q)

        prepare()
        pass_on(*W, t_x, 1, "y")
        pass_on(*W, t_z, 3, "y")
        mine("y", 1)
        mine("y", 2)
        inward(a_own, 0)
        inward(a_own, 1)
        load(*W, low, x, half, coeff_ref)
        plain(low, x)
        inward(a_own, 2)
        inward(a_own, 3)
        pass_on(*W, t_x, 2)
        pass_on(*W, t_z, 0)
        inward(b_own, 0)
        pass_on(*W, t_d, 0)
        inward(b_own, 1)
        energies()
        for q in range(4):
            pass_on(*R, a_far, q)
        load(*R, front, x, reach)
        mirrored(front, x)
        pass_on(*W, t_d, 2)
        inward(b_own, 2)
        load(*R, front, 1 - x, reach)
        mirrored(front, 1 - x)
        inward(b_own, 3)
        mine("z", 1, mid)
        pass_on(*W, t_x, 3)
        load(*W, low, 1 - x, half)
        plain(low, 1 - x)
        load(*R, back, x, reach)
        mirrored(back, x)
        pass_on(*W, t_d, 1)
        for q in range(4):
            pass_on(*R, b_far, q)
        pass_on(*W, t_z, 1)
        load(*W, 1 - low, x, half)
        plain(1 - low, x)
        pass_on(*W, t_d, 3)
        load(*R, back, 1 - x, reach)
        mirrored(back, 1 - x)
        load(*W, 1 - low, 1 - x, half)
        plain(1 - low, 1 - x)
        settle()


def gather_products(ham, tile_mask, coeff, couple, occ_beta, energy_alpha, energy_beta):
    rows, strings = ham.shape
    half = coeff.shape[1]
    fold = half // rows
    row = lax.axis_index("row")
    reach = (fold // 2 + 1) * rows
    start = jnp.where(lax.div(row, fold) == lax.axis_index("col"), lax.rem(row, fold) * rows, 0)
    doubled = jnp.concatenate([coeff, coeff[:, : reach - rows]], axis=1)
    ring = lax.dynamic_slice(doubled, (0, start), (rows, reach))
    anywhere = pl.BlockSpec(memory_space=pl.ANY)
    vmem = pl.BlockSpec(memory_space=pltpu.VMEM)
    dma = pltpu.SemaphoreType.DMA
    return pl.pallas_call(
        gather_kernel,
        out_shape=(
            jax.ShapeDtypeStruct((rows, half), jnp.float32),
            jax.ShapeDtypeStruct((fold, rows, half), jnp.bfloat16),
            jax.ShapeDtypeStruct((fold, rows, reach), jnp.bfloat16),
            jax.ShapeDtypeStruct((rows, half), jnp.float32),
        ),
        in_specs=[anywhere, vmem, anywhere, anywhere, vmem, vmem, vmem, vmem],
        out_specs=(vmem, anywhere, anywhere, vmem),
        scratch_shapes=[
            pltpu.VMEM((rows, strings), jnp.bfloat16),
            pltpu.VMEM((2 * rows, half), jnp.bfloat16),
            dma((3,)),
            dma((80,)),
            dma((fold, 4)),
            dma((fold, 4)),
        ],
        compiler_params=pltpu.CompilerParams(
            collective_id=9, has_side_effects=True, vmem_limit_bytes=50 * 1024 * 1024
        ),
        name="gather_products",
    )(ham, tile_mask, coeff, ring, couple, occ_beta, energy_alpha[:, None], energy_beta[None, :])


CHUNKS = 2


def body(ham, coeff, tile_mask, occupation, orbital_energy, coulomb):
    tile_rows, strings = ham.shape
    tile_cols = coeff.shape[1]
    fold = tile_cols // tile_rows
    direct = lax.axis_size("col") == 2 and lax.axis_size("row") == 16
    occ_float = occupation.astype(jnp.float32)
    occ_alpha = lax.dynamic_slice_in_dim(occ_float, lax.axis_index("row") * tile_rows, tile_rows, 1)
    occ_beta = lax.dynamic_slice_in_dim(occ_float, lax.axis_index("col") * tile_cols, tile_cols, 1)
    energy_alpha = jnp.dot(orbital_energy, occ_alpha, precision=HIGH)
    energy_beta = jnp.dot(orbital_energy, occ_beta, precision=HIGH)
    couple = jnp.dot(occ_alpha.T, coulomb, precision=HIGH)
    if direct:
        product, _, _, diagonal = gather_products(
            ham, tile_mask, coeff, couple, occ_beta, energy_alpha, energy_beta
        )
        result = turn(0, 1, [product], [], coeff, diagonal, strings)
    else:
        diagonal = energy_alpha[:, None] + energy_beta[None, :] + jnp.dot(couple, occ_beta, precision=HIGH)
        mask_cols = tile_mask.shape[1]
        block_size = strings // mask_cols
        mask_rows = tile_rows // block_size
        weights = tile_mask.astype(jnp.bfloat16)[:, None, :, None]
        masked = (ham.reshape(mask_rows, block_size, mask_cols, block_size) * weights).reshape(tile_rows, strings)
        chunks = math.gcd(CHUNKS, fold)
        products = []
        arrived = []
        for q in range(chunks):
            part = jnp.concatenate(
                [coeff[:, s * tile_rows : (s + 1) * tile_rows] for s in range(q, fold, chunks)], axis=1
            )
            gathered = with_layout_constraint(lax.all_gather(part, "row", axis=0, tiled=True), Layout((0, 1)))
            products.append(jnp.dot(masked, gathered, preferred_element_type=jnp.float32))
            result = turn(q, chunks, products, arrived, coeff, diagonal, strings)
            if q < chunks - 1:
                arrived.append(result)
    update, sums = result
    correction = update * lax.rsqrt(sums[2] + 1e-06)
    stats = jnp.stack([sums[0], jnp.sqrt(sums[1])])
    return (correction, stats)


def solution(mesh):
    in_specs = (P("row", None), P("row", "col"), P("row", None), P(), P(), P())
    out_specs = (P("row", "col"), P())
    return jax.shard_map(body, mesh=mesh, in_specs=in_specs, out_specs=out_specs, check_vma=False)
```

```python
import functools
import math

import jax
import jax.numpy as jnp
from jax import lax
from jax.experimental import pallas as pl
from jax.experimental.layout import Layout, with_layout_constraint
from jax.experimental.pallas import tpu as pltpu
from jax.sharding import PartitionSpec as P

MESH = pl.DeviceIdType.MESH
HIGH = lax.Precision.HIGHEST


def turn_kernel(row_count, col_count, total, chunk, chunks, *refs):
    last = chunk == chunks - 1
    if last:
        products, arrived = refs[:chunks], refs[chunks : 2 * chunks - 1]
        diagonal_ref, c_ref, out_ref, stats_ref, recv = refs[2 * chunks - 1 : 2 * chunks + 4]
        refs = refs[2 * chunks + 4 :]
        mine, sums, sum_send, sum_recv = refs[-4:]
    else:
        products = refs[:1]
        recv = refs[1]
        refs = refs[2:]
    p_ref, packed, relay_a, relay_b, load_sem, own_send, recv_sem, arrive_a, arrive_b, send_a, send_b, self_sem = refs[:12]
    row = lax.axis_index("row")
    col = lax.axis_index("col")
    tile = p_ref.shape[0]
    half = tile // 2
    fold = row_count // col_count
    per = fold // chunks
    home = lax.div(row, fold)
    place = lax.rem(row, fold)
    turn = lax.div(place, chunks)
    count = row_count * col_count
    me = row * col_count + col
    is_home = home == col
    takes = lax.rem(place, chunks) == chunk
    if last:
        loads = [
            pltpu.make_async_copy(
                product.at[:, pl.ds(k * tile, tile)],
                p_ref.at[:, pl.ds((q + chunks * k) * tile, tile)],
                load_sem.at[q * per + k],
            )
            for q, product in enumerate(products)
            for k in range(per)
        ]
    else:
        loads = [pltpu.make_async_copy(products[0], p_ref, load_sem.at[0])]
    for load in loads:
        load.start()
    if last:
        diagonal_load = pltpu.make_async_copy(diagonal_ref, out_ref, self_sem.at[3])
        diagonal_load.start()

    barrier = pltpu.get_barrier_semaphore()

    def greet(d, carry):
        other = lax.rem(me + d, count)
        pl.semaphore_signal(
            barrier,
            inc=1,
            device_id=(lax.div(other, col_count), lax.rem(other, col_count)),
            device_id_type=MESH,
        )
        return carry

    lax.fori_loop(1, count, greet, 0)
    pl.semaphore_wait(barrier, count - 1)
    for load in loads:
        load.wait()

    def columns(s):
        return pl.ds(pl.multiple_of(s * tile, tile), tile)

    def remote(src, dst, send, arrive, to_row, to_col):
        return pltpu.make_async_remote_copy(
            src_ref=src,
            dst_ref=dst,
            send_sem=send,
            recv_sem=arrive,
            device_id=(to_row, to_col),
            device_id_type=MESH,
        )

    def spot(k):
        kk = lax.rem(turn + k, per)
        return kk, chunk + chunks * kk

    def own_direct(k):
        kk, s = spot(k)
        near = col * fold + s
        return [
            remote(packed.at[kk, h], recv.at[place, h], own_send.at[kk, h], recv_sem.at[place, h], near, col)
            for h in range(2)
        ]

    def own_relayed(k):
        kk, s = spot(k)
        near = col * fold + s
        slot_a = col - (col > home).astype(jnp.int32)
        slot_b = row - fold * (home > col).astype(jnp.int32)
        return [
            remote(packed.at[kk, 0], relay_a.at[slot_a, kk], own_send.at[kk, 0], arrive_a.at[slot_a, kk], row, home),
            remote(packed.at[kk, 1], relay_b.at[slot_b], own_send.at[kk, 1], arrive_b.at[slot_b], near, col),
        ]

    def own_local():
        return [pltpu.make_async_copy(packed.at[turn, h], recv.at[place, h], self_sem.at[h]) for h in range(2)]

    def pack(k):
        kk, s = spot(k)
        cols = columns(s) if last else columns(kk)
        for h in range(2):
            peak = jnp.max(jnp.abs(p_ref[pl.ds(h * half, half), cols]), axis=0, keepdims=True)
            code = jnp.floor(jnp.log2(jnp.maximum(peak, 1e-30)) * 128.0) + 2.0
            grow = jnp.exp2(code * (-1.0 / 128.0)) * 32767.0
            packed[kk, h, pl.ds(half, 16)] = jnp.broadcast_to(code, (16, tile)).astype(jnp.int32).astype(jnp.int16)
            rows = min(64, half)
            for r in range(0, half, rows):
                value = p_ref[pl.ds(h * half + r, rows), cols] * grow
                packed[kk, h, pl.ds(r, rows)] = jnp.floor(value + 0.5).astype(jnp.int32).astype(jnp.int16)

    def exchange(phase, start):
        def one(d, carry):
            other = lax.rem(me + d, count)
            copy = remote(
                mine.at[phase],
                sums.at[phase, me],
                sum_send.at[phase, d],
                sum_recv.at[phase, me],
                lax.div(other, col_count),
                lax.rem(other, col_count),
            )
            if start:
                copy.start()
            else:
                copy.wait_send()
            return carry

        lax.fori_loop(1, count, one, 0)

    def gather_sums(phase):
        def one(d, carry):
            other = lax.rem(me + d, count)
            remote(
                mine.at[phase],
                sums.at[phase, other],
                sum_send.at[phase, d],
                sum_recv.at[phase, other],
                lax.div(other, col_count),
                lax.rem(other, col_count),
            ).wait_recv()
            return carry

        lax.fori_loop(1, count, one, 0)
        sums[phase, pl.ds(me, 1)] = mine[pl.ds(phase, 1)]
        every = jnp.sum(sums[phase], axis=0)
        return jnp.sum(every[0:8]), jnp.sum(every[8:16])

    def fold_sum(x):
        lanes = x.shape[1] // 128
        out = x[:, 0:128]
        for q in range(1, lanes):
            out = out + x[:, q * 128 : (q + 1) * 128]
        return jnp.sum(out.reshape(x.shape[0] // 8, 8, 128), axis=0)

    zero = jnp.zeros((8, 128), jnp.float32)
    if last:
        step_rows = min(32, tile)

        def early(r, carry):
            rows = pl.ds(pl.multiple_of(r * step_rows, step_rows), step_rows)
            c = c_ref[rows, :].astype(jnp.float32)
            return carry[0] + fold_sum(c * p_ref[rows, :]), carry[1] + fold_sum(c * c)

        proj, weight = lax.fori_loop(0, tile // step_rows, early, (zero, zero))
        mine[0, 0:8] = proj
        mine[0, 8:16] = weight
        exchange(0, True)

    def launch(k, carry):
        pack(k)

        @pl.when(jnp.logical_not(is_home))
        def _():
            for copy in own_relayed(k):
                copy.start()

        @pl.when(jnp.logical_and(is_home, jnp.logical_or(k > 0, jnp.logical_not(takes))))
        def _():
            for copy in own_direct(k):
                copy.start()

        return carry

    lax.fori_loop(0, per, launch, 0)

    @pl.when(jnp.logical_and(is_home, takes))
    def _():
        for copy in own_local():
            copy.start()
        for copy in own_local():
            copy.wait()

    def relay_first(t):
        slot = lax.div(t, per)
        group = slot + (slot >= col).astype(jnp.int32)
        kk, s = spot(lax.rem(t, per))
        return slot, kk, remote(
            relay_a.at[slot, kk], recv.at[place, 0], send_a.at[t], recv_sem.at[place, 0], group * fold + s, col
        )

    def relay_second(t):
        slot = lax.div(t, fold)
        group = slot + (slot >= col).astype(jnp.int32)
        far = lax.rem(place - lax.rem(t, fold) + fold, fold)
        slot_b = slot * fold + far
        return slot_b, remote(
            relay_b.at[slot_b], recv.at[far, 1], send_b.at[t], recv_sem.at[far, 1], row, group
        )

    @pl.when(is_home)
    def _():
        def step(t, carry):
            slot, kk, copy = relay_first(t)
            pltpu.make_async_copy(relay_a.at[slot, kk], relay_a.at[slot, kk], arrive_a.at[slot, kk]).wait()
            copy.start()
            return carry

        lax.fori_loop(0, (col_count - 1) * per, step, 0)

    @pl.when(jnp.logical_and(is_home, takes))
    def _():
        def step(t, carry):
            slot_b, copy = relay_second(t)
            pltpu.make_async_copy(relay_b.at[slot_b], relay_b.at[slot_b], arrive_b.at[slot_b]).wait()
            copy.start()
            return carry

        lax.fori_loop(0, (col_count - 1) * fold, step, 0)

    def await_piece(k):
        s = lax.rem(place - k + fold, fold)

        @pl.when(jnp.logical_and(takes, jnp.logical_not(jnp.logical_and(is_home, k == 0))))
        def _():
            for h in range(2):
                pltpu.make_async_copy(recv.at[s, h], recv.at[s, h], recv_sem.at[s, h]).wait()

    def settle():
        @pl.when(is_home)
        def _():
            def done(k, carry):
                @pl.when(jnp.logical_or(k > 0, jnp.logical_not(takes)))
                def _():
                    for copy in own_direct(k):
                        copy.wait_send()

                return carry

            lax.fori_loop(0, per, done, 0)

            def done_first(t, carry):
                relay_first(t)[-1].wait_send()
                return carry

            lax.fori_loop(0, (col_count - 1) * per, done_first, 0)

        @pl.when(jnp.logical_and(is_home, takes))
        def _():
            def done_second(t, carry):
                relay_second(t)[-1].wait_send()
                return carry

            lax.fori_loop(0, (col_count - 1) * fold, done_second, 0)

        @pl.when(jnp.logical_not(is_home))
        def _():
            def done(k, carry):
                for copy in own_relayed(k):
                    copy.wait_send()
                return carry

            lax.fori_loop(0, per, done, 0)

    if not last:

        def hold(k, carry):
            await_piece(k)
            return carry

        lax.fori_loop(0, fold, hold, 0)
        settle()
        return

    for q, ready in enumerate(arrived):

        @pl.when(lax.rem(place, chunks) == q)
        def _():
            fetch = pltpu.make_async_copy(ready, recv, self_sem.at[2])
            fetch.start()
            fetch.wait()

    proj, weight = gather_sums(0)
    theta = 2.0 * proj / weight
    diagonal_load.wait()

    piece = min(128, tile)

    def finish(k, carry):
        s = lax.rem(place - k + fold, fold)

        await_piece(k)

        def part(r, carry):
            squares, spread = carry
            rows = pl.ds(pl.multiple_of(r * piece, piece), piece)
            for h in range(2):
                cols = pl.ds(pl.multiple_of(s * tile + h * half, half), half)
                code = recv[s, h, pl.ds(half, 16), rows].astype(jnp.int32).astype(jnp.float32)[0:1]
                shrink = jnp.exp2(code * (1.0 / 128.0)) * (1.0 / 32767.0)
                value = recv[s, h, pl.ds(0, half), rows].astype(jnp.int32).astype(jnp.float32)
                turned = (value * shrink).T
                sigma = p_ref[rows, cols] + turned
                residual = sigma - theta * c_ref[rows, cols].astype(jnp.float32)
                update = residual / jnp.maximum(jnp.abs(out_ref[rows, cols] - theta), 1.0)
                out_ref[rows, cols] = update
                squares = squares + fold_sum(residual * residual)
                spread = spread + fold_sum(update * update)
            return squares, spread

        return lax.fori_loop(0, tile // piece, part, carry)

    squares, spread = lax.fori_loop(0, fold, finish, (zero, zero))
    mine[1, 0:8] = squares
    mine[1, 8:16] = spread
    exchange(1, True)
    squares, spread = gather_sums(1)
    stats_ref[0] = theta
    stats_ref[1] = squares / total
    stats_ref[2] = spread / total

    exchange(0, False)
    exchange(1, False)
    settle()


def turn(chunk, chunks, products, arrived, coeff, diagonal, strings):
    tile_rows, tile_cols = coeff.shape
    row_count = lax.axis_size("row")
    col_count = lax.axis_size("col")
    fold = row_count // col_count
    per = fold // chunks
    count = row_count * col_count
    tall = tile_rows // 2 + 16
    others = max(col_count - 1, 1)
    vmem = pl.BlockSpec(memory_space=pltpu.VMEM)
    anywhere = pl.BlockSpec(memory_space=pl.ANY)
    dma = pltpu.SemaphoreType.DMA
    last = chunk == chunks - 1
    arrival = (fold, 2, tall, tile_rows)
    scratch = [
        pltpu.VMEM((tile_rows, tile_cols if last else tile_cols // chunks), jnp.float32),
        pltpu.VMEM((per, 2, tall, tile_rows), jnp.int16),
        pltpu.VMEM((others, per, tall, tile_rows), jnp.int16),
        pltpu.VMEM((others * fold, tall, tile_rows), jnp.int16),
        dma((fold,)),
        dma((per, 2)),
        dma((fold, 2)),
        dma((others, per)),
        dma((others * fold,)),
        dma((others * per,)),
        dma((others * fold,)),
        dma((4,)),
    ]
    if last:
        operands = (*products, *arrived, diagonal, coeff)
        in_specs = [anywhere] * (2 * chunks) + [vmem]
        out_shape = (
            jax.ShapeDtypeStruct((tile_rows, tile_cols), jnp.float32),
            jax.ShapeDtypeStruct((3,), jnp.float32),
        )
        out_specs = (vmem, pl.BlockSpec(memory_space=pltpu.SMEM))
        scratch = [
            pltpu.VMEM(arrival, jnp.int16),
            *scratch,
            pltpu.VMEM((2, 16, 128), jnp.float32),
            pltpu.VMEM((2, count, 16, 128), jnp.float32),
            dma((2, count)),
            dma((2, count)),
        ]
    else:
        operands = (products[chunk],)
        in_specs = [anywhere]
        out_shape = jax.ShapeDtypeStruct(arrival, jnp.int16)
        out_specs = vmem
    return pl.pallas_call(
        functools.partial(turn_kernel, row_count, col_count, float(strings) * float(strings), chunk, chunks),
        out_shape=out_shape,
        in_specs=in_specs,
        out_specs=out_specs,
        scratch_shapes=scratch,
        compiler_params=pltpu.CompilerParams(
            collective_id=chunk,
            has_side_effects=True,
            vmem_limit_bytes=(24 if not last else 60 if chunks == 1 else 60) * 1024 * 1024,
        ),
        name=f"turn_{chunk}",
    )(*operands)


def step_kernel(
    total,
    ham_ref,
    mask_ref,
    coeff_ref,
    ring_ref,
    occ_ref,
    level_ref,
    coulomb_ref,
    out_ref,
    wide,
    ring,
    stats_ref,
    acc_ref,
    m_ref,
    buf,
    c_ref,
    packed,
    relay_a,
    relay_b,
    recv,
    mine_sums,
    sums,
    load_sem,
    send_sem,
    wide_sem,
    ring_sem,
    own_send,
    recv_sem,
    arrive_a,
    arrive_b,
    send_a,
    send_b,
    self_sem,
    sum_send,
    sum_recv,
):
    rows, strings = ham_ref.shape
    half = coeff_ref.shape[1]
    quarter = rows // 4
    row = lax.axis_index("row")
    col = lax.axis_index("col")
    core = lax.rem(row, 2)
    x = lax.rem(lax.div(row, 2), 2)
    low = lax.rem(lax.div(row, 4), 2)
    high = lax.div(row, 8)
    diag = high == col
    mid = low != high
    fold = half // rows

    def device(h, l, a, k):
        return ((h * 2 + l) * 2 + a) * 2 + k

    targets = {
        "x": (device(high, low, 1 - x, core), col),
        "z": (device(high, 1 - low, x, core), col),
        "y": (row, 1 - col),
        "c": (device(high, low, x, 1 - core), col),
        "cut": (device(1 - high, 1 - low, x, core), col),
    }

    ham_load = pltpu.make_async_copy(ham_ref, m_ref, load_sem.at[0])
    ham_load.start()
    coeff_load = pltpu.make_async_copy(coeff_ref, c_ref, load_sem.at[3])
    coeff_load.start()

    count = sums.shape[1]
    me = row * 2 + col

    def remote(src, dst, send_one, arrive_one, to_row, to_col):
        return pltpu.make_async_remote_copy(
            src_ref=src,
            dst_ref=dst,
            send_sem=send_one,
            recv_sem=arrive_one,
            device_id=(to_row, to_col),
            device_id_type=MESH,
        )

    barrier = pltpu.get_barrier_semaphore()

    def greet(d, carry):
        other = lax.rem(me + d, count)
        pl.semaphore_signal(
            barrier, inc=1, device_id=(lax.div(other, 2), lax.rem(other, 2)), device_id_type=MESH
        )
        return carry

    lax.fori_loop(1, count, greet, 0)
    pl.semaphore_wait(barrier, count - 1)

    def spot(l, a, k):
        return (l * 2 + a) * 2 + k

    def part(ref, t, q):
        return ref.at[t, pl.ds(q * quarter, quarter)]

    end = jnp.logical_not(mid)
    sent = []

    def send(way, ref, sems, t, q, own=None, when=None):
        src = part(ref, t, q) if own is None else own.at[pl.ds(q * quarter, quarter)]
        if way == "cut":
            when = mid
        copy = pltpu.make_async_remote_copy(
            src_ref=src,
            dst_ref=part(ref, t, q),
            send_sem=send_sem.at[len(sent)],
            recv_sem=sems.at[t, q],
            device_id=targets[way],
            device_id_type=MESH,
        )
        sent.append((copy, when))
        if when is None:
            copy.start()
        else:

            @pl.when(when)
            def _():
                copy.start()

    def settle():
        for copy, when in sent:
            if when is None:
                copy.wait_send()
            else:

                @pl.when(when)
                def _():
                    copy.wait_send()

        sent.clear()

    def arrive(ref, sems, t, q):
        view = part(ref, t, q)
        pltpu.make_async_copy(view, view, sems.at[t, q]).wait()

    def pass_on(ref, sems, t, q, *ways):
        arrive(ref, sems, t, q)
        for way in ways:
            send(way, ref, sems, t, q)
        send("c", ref, sems, t, q)

    def load(ref, sems, l, a, width, own=None):
        mine, other = spot(l, a, core), spot(l, a, 1 - core)
        for q in range(4):
            arrive(ref, sems, other, q)
        src = ref.at[mine] if own is None else own
        first = pltpu.make_async_copy(
            src, buf.at[pl.ds(pl.multiple_of(core * rows, rows), rows), pl.ds(0, width)], load_sem.at[1]
        )
        second = pltpu.make_async_copy(
            ref.at[other],
            buf.at[pl.ds(pl.multiple_of((1 - core) * rows, rows), rows), pl.ds(0, width)],
            load_sem.at[2],
        )
        first.start()
        second.start()
        first.wait()
        second.wait()

    def block(n):
        return pl.ds(pl.multiple_of(n * rows, rows), rows)

    near = col * fold
    away = (1 - col) * fold

    def plain(l, a):
        base = spot(l, a, 0)
        left = pl.ds(pl.multiple_of((away + base) * rows, rows), 2 * rows)

        def one(n, carry):
            acc_ref[:, block(n)] += jnp.dot(m_ref[:, left], buf[:, block(n)], preferred_element_type=jnp.float32)
            return carry

        lax.fori_loop(0, fold, one, 0)

    def turned(l, a):
        base = spot(l, a, 0)

        def one(n, carry):
            total = jnp.zeros((rows, rows), jnp.float32)
            for k in range(0, fold, 2):
                left = pl.ds(pl.multiple_of((away + k) * rows, rows), 2 * rows)
                total = total + lax.dot_general(
                    m_ref[:, left],
                    buf[block(n), pl.ds(k * rows, 2 * rows)],
                    (((1,), (1,)), ((), ())),
                    preferred_element_type=jnp.float32,
                )
            acc_ref[:, block(base + n)] += total
            return carry

        lax.fori_loop(0, 2, one, 0)

    def mirrored(l, a):
        base = spot(l, a, 0)

        def lane(k, carry):
            t = base + k

            def one(d, inner):
                s = lax.rem(t + d, fold)
                tile = buf[block(k), block(d)]
                acc_ref[:, block(s)] += jnp.dot(
                    m_ref[:, block(near + t)], tile, preferred_element_type=jnp.float32
                )

                @pl.when(d > 0)
                def _():
                    acc_ref[:, block(t)] += lax.dot_general(
                        m_ref[:, block(near + s)],
                        tile,
                        (((1,), (1,)), ((), ())),
                        preferred_element_type=jnp.float32,
                    )

                return inner

            last = jnp.where(t < fold // 2, fold // 2 + 1, fold // 2)
            lax.fori_loop(0, last, one, 0)
            return carry

        lax.fori_loop(0, 2, lane, 0)

    def prepare():
        ham_load.wait()
        groups, blocks = mask_ref.shape
        size = strings // blocks
        step = min(1024, strings)
        pick = lax.broadcasted_iota(jnp.int32, (rows, groups), 0) // size == lax.broadcasted_iota(
            jnp.int32, (rows, groups), 1
        )
        tall = jnp.dot(
            pick.astype(jnp.bfloat16), mask_ref[...].astype(jnp.bfloat16), preferred_element_type=jnp.float32
        ).astype(jnp.bfloat16)

        def one(n, carry):
            cols = pl.ds(pl.multiple_of(n * step, step), step)
            spread = (n * step + lax.broadcasted_iota(jnp.int32, (blocks, step), 1)) // size == lax.broadcasted_iota(
                jnp.int32, (blocks, step), 0
            )
            weight = jnp.dot(tall, spread.astype(jnp.bfloat16), preferred_element_type=jnp.float32)
            m_ref[:, cols] = m_ref[:, cols] * weight.astype(jnp.bfloat16)
            acc_ref[:, pl.ds(pl.multiple_of(n * (step // 2), step // 2), step // 2)] = jnp.zeros(
                (rows, step // 2), jnp.float32
            )
            return carry

        lax.fori_loop(0, strings // step, one, 0)

    def energies():
        alpha = occ_ref[:, block(row)].astype(jnp.float32).T
        couple = jnp.dot(alpha, coulomb_ref[...], precision=HIGH, preferred_element_type=jnp.float32)
        energy = jnp.sum(alpha * level_ref[...], axis=1, keepdims=True)

        def one(n, carry):
            beta = occ_ref[:, block(near + n)].astype(jnp.float32)
            out_ref[:, block(n)] = (
                jnp.dot(couple, beta, precision=HIGH, preferred_element_type=jnp.float32)
                + energy
                + jnp.dot(level_ref[...], beta, precision=HIGH, preferred_element_type=jnp.float32)
            )
            return carry

        lax.fori_loop(0, fold, one, 0)

    reach = ring.shape[2]
    W = (wide, wide_sem)
    R = (ring, ring_sem)
    own = spot(low, x, core)
    t_x = spot(low, 1 - x, core)
    t_z = spot(1 - low, x, core)
    t_d = spot(1 - low, 1 - x, core)

    @pl.when(diag)
    def _():
        def mine(way, q):
            send(way, *R, own, q, ring_ref)

        for q in range(4):
            mine("cut", q)
            mine("x", q)
            if q < 2:
                mine("z", q)
            mine("c", q)
        prepare()
        pass_on(*R, t_z, 0, "cut")
        pass_on(*W, own, 0, "z")
        pass_on(*R, t_z, 1, "cut")
        pass_on(*W, t_x, 0, "z")
        mine("z", 2)
        mine("z", 3)
        pass_on(*W, t_z, 0, "y")
        pass_on(*R, t_x, 0, "z")
        pass_on(*R, t_x, 1, "z")
        pass_on(*W, t_z, 2, "x")
        pass_on(*W, t_d, 0, "y")
        pass_on(*R, t_x, 2)
        pass_on(*R, t_x, 3)
        pass_on(*R, t_z, 2, "x", "cut")
        pass_on(*W, own, 3, "x")
        pass_on(*R, t_z, 3, "x", "cut")
        pass_on(*W, t_d, 2, "y")
        load(*R, low, x, reach, ring_ref)
        mirrored(low, x)
        pass_on(*W, t_x, 1, "z")
        pass_on(*W, t_x, 3, "y")
        energies()
        load(*R, low, 1 - x, reach)
        mirrored(low, 1 - x)
        pass_on(*W, t_z, 3, "x")
        pass_on(*W, t_d, 1, "y")
        load(*R, 1 - low, x, reach)
        mirrored(1 - low, x)
        pass_on(*W, own, 1, "z")
        for q in range(4):
            pass_on(*R, t_d, q)
        pass_on(*W, t_d, 3, "y")
        load(*R, 1 - low, 1 - x, reach)
        mirrored(1 - low, 1 - x)
        pass_on(*W, own, 2, "x")
        load(*W, 1 - low, 1 - x, half)
        turned(1 - low, 1 - x)
        load(*W, low, x, half)
        turned(low, x)
        pass_on(*W, t_z, 1)
        pass_on(*W, t_x, 2)
        load(*W, 1 - low, x, half)
        turned(1 - low, x)
        load(*W, low, 1 - x, half)
        turned(low, 1 - x)
        settle()

    @pl.when(jnp.logical_not(diag))
    def _():
        def mine(way, q, when=None):
            send(way, *W, own, q, coeff_ref, when)

        mine("y", 0)
        mine("x", 0)
        mine("z", 2)
        mine("x", 1)
        mine("z", 3)
        mine("x", 2)
        mine("z", 1, end)
        for q in range(4):
            mine("c", q)
        pass_on(*W, t_x, 0, "y")
        pass_on(*W, t_z, 2, "y")
        mine("y", 3)
        front = 1 - col
        back = col
        a_own, b_own = spot(front, x, core), spot(back, x, core)
        a_far, b_far = spot(front, 1 - x, core), spot(back, 1 - x, core)

        def inward(t, q):
            arrive(*R, t, q)
            send("x", *R, t, q)
            send("z", *R, t, q, None, mid)
            send("c", *R, t, q)

        prepare()
        pass_on(*W, t_x, 1, "y")
        pass_on(*W, t_z, 3, "y")
        mine("y", 1)
        mine("y", 2)
        inward(a_own, 0)
        inward(a_own, 1)
        load(*W, low, x, half, coeff_ref)
        plain(low, x)
        inward(a_own, 2)
        inward(a_own, 3)
        pass_on(*W, t_x, 2)
        pass_on(*W, t_z, 0)
        inward(b_own, 0)
        pass_on(*W, t_d, 0)
        inward(b_own, 1)
        energies()
        for q in range(4):
            pass_on(*R, a_far, q)
        load(*R, front, x, reach)
        mirrored(front, x)
        pass_on(*W, t_d, 2)
        inward(b_own, 2)
        load(*R, front, 1 - x, reach)
        mirrored(front, 1 - x)
        inward(b_own, 3)
        mine("z", 1, mid)
        pass_on(*W, t_x, 3)
        load(*W, low, 1 - x, half)
        plain(low, 1 - x)
        load(*R, back, x, reach)
        mirrored(back, x)
        pass_on(*W, t_d, 1)
        for q in range(4):
            pass_on(*R, b_far, q)
        pass_on(*W, t_z, 1)
        load(*W, 1 - low, x, half)
        plain(1 - low, x)
        pass_on(*W, t_d, 3)
        load(*R, back, 1 - x, reach)
        mirrored(back, 1 - x)
        load(*W, 1 - low, 1 - x, half)
        plain(1 - low, 1 - x)
        settle()

    place = lax.rem(row, fold)
    far_col = 1 - col
    piece_half = rows // 2

    def own_direct(k):
        s = lax.rem(place + k, fold)
        return [
            remote(packed.at[s, h], recv.at[place, h], own_send.at[s, h], recv_sem.at[place, h], near + s, col)
            for h in range(2)
        ]

    def own_relayed(k):
        s = lax.rem(place + k, fold)
        return [
            remote(packed.at[s, 0], relay_a.at[s], own_send.at[s, 0], arrive_a.at[s], row, far_col),
            remote(packed.at[s, 1], relay_b.at[place], own_send.at[s, 1], arrive_b.at[place], near + s, col),
        ]

    def own_local():
        return [pltpu.make_async_copy(packed.at[place, h], recv.at[place, h], self_sem.at[h]) for h in range(2)]

    def pack(k):
        s = lax.rem(place + k, fold)
        for h in range(2):
            peak = jnp.max(jnp.abs(acc_ref[pl.ds(h * piece_half, piece_half), block(s)]), axis=0, keepdims=True)
            code = jnp.floor(jnp.log2(jnp.maximum(peak, 1e-30)) * 128.0) + 2.0
            grow = jnp.exp2(code * (-1.0 / 128.0)) * 32767.0
            packed[s, h, pl.ds(piece_half, 16)] = (
                jnp.broadcast_to(code, (16, rows)).astype(jnp.int32).astype(jnp.int16)
            )
            for r in range(0, piece_half, 64):
                value = acc_ref[pl.ds(h * piece_half + r, 64), block(s)] * grow
                packed[s, h, pl.ds(r, 64)] = jnp.floor(value + 0.5).astype(jnp.int32).astype(jnp.int16)

    def exchange(phase, start):
        def one(d, carry):
            other = lax.rem(me + d, count)
            copy = remote(
                mine_sums.at[phase],
                sums.at[phase, me],
                sum_send.at[phase, d],
                sum_recv.at[phase, me],
                lax.div(other, 2),
                lax.rem(other, 2),
            )
            if start:
                copy.start()
            else:
                copy.wait_send()
            return carry

        lax.fori_loop(1, count, one, 0)

    def gather_sums(phase):
        def one(d, carry):
            other = lax.rem(me + d, count)
            view = sums.at[phase, other]
            pltpu.make_async_copy(view, view, sum_recv.at[phase, other]).wait()
            return carry

        lax.fori_loop(1, count, one, 0)
        sums[phase, pl.ds(me, 1)] = mine_sums[pl.ds(phase, 1)]
        every = jnp.sum(sums[phase], axis=0)
        return jnp.sum(every[0:8]), jnp.sum(every[8:16])

    def fold_sum(v):
        out = v[:, 0:128]
        for q in range(1, v.shape[1] // 128):
            out = out + v[:, q * 128 : (q + 1) * 128]
        return jnp.sum(out.reshape(v.shape[0] // 8, 8, 128), axis=0)

    def launch(k, carry):
        pack(k)

        @pl.when(jnp.logical_not(diag))
        def _():
            for copy in own_relayed(k):
                copy.start()

        @pl.when(jnp.logical_and(diag, k > 0))
        def _():
            for copy in own_direct(k):
                copy.start()

        return carry

    lax.fori_loop(0, fold, launch, 0)

    zero = jnp.zeros((8, 128), jnp.float32)
    step_rows = min(32, rows)
    coeff_load.wait()

    def early(r, carry):
        band = pl.ds(pl.multiple_of(r * step_rows, step_rows), step_rows)
        c = c_ref[band, :].astype(jnp.float32)
        return carry[0] + fold_sum(c * acc_ref[band, :]), carry[1] + fold_sum(c * c)

    proj, weight = lax.fori_loop(0, rows // step_rows, early, (zero, zero))
    mine_sums[0, 0:8] = proj
    mine_sums[0, 8:16] = weight
    exchange(0, True)

    @pl.when(diag)
    def _():
        for copy in own_local():
            copy.start()
        for copy in own_local():
            copy.wait()

    def relay_first(t):
        s = lax.rem(place + t, fold)
        return s, remote(
            relay_a.at[s], recv.at[place, 0], send_a.at[t], recv_sem.at[place, 0], far_col * fold + s, col
        )

    def relay_second(t):
        far = lax.rem(place - t + fold, fold)
        return far, remote(relay_b.at[far], recv.at[far, 1], send_b.at[t], recv_sem.at[far, 1], row, far_col)

    @pl.when(diag)
    def _():
        def relay(t, carry):
            s, copy = relay_first(t)
            pltpu.make_async_copy(relay_a.at[s], relay_a.at[s], arrive_a.at[s]).wait()
            copy.start()
            far, copy = relay_second(t)
            pltpu.make_async_copy(relay_b.at[far], relay_b.at[far], arrive_b.at[far]).wait()
            copy.start()
            return carry

        lax.fori_loop(0, fold, relay, 0)

    def await_piece(k):
        s = lax.rem(place - k + fold, fold)

        @pl.when(jnp.logical_not(jnp.logical_and(diag, k == 0)))
        def _():
            for h in range(2):
                pltpu.make_async_copy(recv.at[s, h], recv.at[s, h], recv_sem.at[s, h]).wait()

    proj, weight = gather_sums(0)
    theta = 2.0 * proj / weight
    piece = min(128, rows)

    def finish(k, carry):
        s = lax.rem(place - k + fold, fold)
        await_piece(k)

        def part_of(r, inner):
            squares, spread = inner
            band = pl.ds(pl.multiple_of(r * piece, piece), piece)
            for h in range(2):
                cols = pl.ds(pl.multiple_of(s * rows + h * piece_half, piece_half), piece_half)
                code = recv[s, h, pl.ds(piece_half, 16), band].astype(jnp.int32).astype(jnp.float32)[0:1]
                shrink = jnp.exp2(code * (1.0 / 128.0)) * (1.0 / 32767.0)
                value = recv[s, h, pl.ds(0, piece_half), band].astype(jnp.int32).astype(jnp.float32)
                sigma = acc_ref[band, cols] + (value * shrink).T
                residual = sigma - theta * c_ref[band, cols].astype(jnp.float32)
                update = residual / jnp.maximum(jnp.abs(out_ref[band, cols] - theta), 1.0)
                out_ref[band, cols] = update
                squares = squares + fold_sum(residual * residual)
                spread = spread + fold_sum(update * update)
            return squares, spread

        return lax.fori_loop(0, rows // piece, part_of, carry)

    squares, spread = lax.fori_loop(0, fold, finish, (zero, zero))
    mine_sums[1, 0:8] = squares
    mine_sums[1, 8:16] = spread
    exchange(1, True)
    squares, spread = gather_sums(1)
    stats_ref[0] = theta
    stats_ref[1] = squares / total
    stats_ref[2] = spread / total

    exchange(0, False)
    exchange(1, False)

    @pl.when(diag)
    def _():
        def done(t, carry):
            @pl.when(t > 0)
            def _():
                for copy in own_direct(t):
                    copy.wait_send()

            relay_first(t)[1].wait_send()
            relay_second(t)[1].wait_send()
            return carry

        lax.fori_loop(0, fold, done, 0)

    @pl.when(jnp.logical_not(diag))
    def _():
        def done(t, carry):
            for copy in own_relayed(t):
                copy.wait_send()
            return carry

        lax.fori_loop(0, fold, done, 0)


def whole_step(ham, tile_mask, coeff, occupation, orbital_energy, coulomb):
    rows, strings = ham.shape
    half = coeff.shape[1]
    fold = half // rows
    count = lax.axis_size("row") * lax.axis_size("col")
    row = lax.axis_index("row")
    reach = (fold // 2 + 1) * rows
    start = jnp.where(lax.div(row, fold) == lax.axis_index("col"), lax.rem(row, fold) * rows, 0)
    doubled = jnp.concatenate([coeff, coeff[:, : reach - rows]], axis=1)
    ring = lax.dynamic_slice(doubled, (0, start), (rows, reach))
    tall = rows // 2 + 16
    anywhere = pl.BlockSpec(memory_space=pl.ANY)
    vmem = pl.BlockSpec(memory_space=pltpu.VMEM)
    dma = pltpu.SemaphoreType.DMA
    update, _, _, sums = pl.pallas_call(
        functools.partial(step_kernel, float(strings) * float(strings)),
        out_shape=(
            jax.ShapeDtypeStruct((rows, half), jnp.float32),
            jax.ShapeDtypeStruct((fold, rows, half), jnp.bfloat16),
            jax.ShapeDtypeStruct((fold, rows, reach), jnp.bfloat16),
            jax.ShapeDtypeStruct((3,), jnp.float32),
        ),
        in_specs=[anywhere, vmem, anywhere, anywhere, vmem, vmem, vmem],
        out_specs=(vmem, anywhere, anywhere, pl.BlockSpec(memory_space=pltpu.SMEM)),
        scratch_shapes=[
            pltpu.VMEM((rows, half), jnp.float32),
            pltpu.VMEM((rows, strings), jnp.bfloat16),
            pltpu.VMEM((2 * rows, half), jnp.bfloat16),
            pltpu.VMEM((rows, half), jnp.bfloat16),
            pltpu.VMEM((fold, 2, tall, rows), jnp.int16),
            pltpu.VMEM((fold, tall, rows), jnp.int16),
            pltpu.VMEM((fold, tall, rows), jnp.int16),
            pltpu.VMEM((fold, 2, tall, rows), jnp.int16),
            pltpu.VMEM((2, 16, 128), jnp.float32),
            pltpu.VMEM((2, count, 16, 128), jnp.float32),
            dma((4,)),
            dma((80,)),
            dma((fold, 4)),
            dma((fold, 4)),
            dma((fold, 2)),
            dma((fold, 2)),
            dma((fold,)),
            dma((fold,)),
            dma((fold,)),
            dma((fold,)),
            dma((2,)),
            dma((2, count)),
            dma((2, count)),
        ],
        compiler_params=pltpu.CompilerParams(
            collective_id=9, has_side_effects=True, vmem_limit_bytes=62 * 1024 * 1024
        ),
        name="whole_step",
    )(ham, tile_mask, coeff, ring, occupation, orbital_energy[None, :], coulomb)
    return update, sums


CHUNKS = 2


def body(ham, coeff, tile_mask, occupation, orbital_energy, coulomb):
    tile_rows, strings = ham.shape
    tile_cols = coeff.shape[1]
    fold = tile_cols // tile_rows
    direct = lax.axis_size("col") == 2 and lax.axis_size("row") == 16
    if direct:
        result = whole_step(ham, tile_mask, coeff, occupation, orbital_energy, coulomb)
    else:
        occ_float = occupation.astype(jnp.float32)
        occ_alpha = lax.dynamic_slice_in_dim(occ_float, lax.axis_index("row") * tile_rows, tile_rows, 1)
        occ_beta = lax.dynamic_slice_in_dim(occ_float, lax.axis_index("col") * tile_cols, tile_cols, 1)
        energy_alpha = jnp.dot(orbital_energy, occ_alpha, precision=HIGH)
        energy_beta = jnp.dot(orbital_energy, occ_beta, precision=HIGH)
        couple = jnp.dot(occ_alpha.T, coulomb, precision=HIGH)
        diagonal = energy_alpha[:, None] + energy_beta[None, :] + jnp.dot(couple, occ_beta, precision=HIGH)
        mask_cols = tile_mask.shape[1]
        block_size = strings // mask_cols
        mask_rows = tile_rows // block_size
        weights = tile_mask.astype(jnp.bfloat16)[:, None, :, None]
        masked = (ham.reshape(mask_rows, block_size, mask_cols, block_size) * weights).reshape(tile_rows, strings)
        chunks = math.gcd(CHUNKS, fold)
        products = []
        arrived = []
        for q in range(chunks):
            part = jnp.concatenate(
                [coeff[:, s * tile_rows : (s + 1) * tile_rows] for s in range(q, fold, chunks)], axis=1
            )
            gathered = with_layout_constraint(lax.all_gather(part, "row", axis=0, tiled=True), Layout((0, 1)))
            products.append(jnp.dot(masked, gathered, preferred_element_type=jnp.float32))
            result = turn(q, chunks, products, arrived, coeff, diagonal, strings)
            if q < chunks - 1:
                arrived.append(result)
    update, sums = result
    correction = update * lax.rsqrt(sums[2] + 1e-06)
    stats = jnp.stack([sums[0], jnp.sqrt(sums[1])])
    return (correction, stats)


def solution(mesh):
    in_specs = (P("row", None), P("row", "col"), P("row", None), P(), P(), P())
    out_specs = (P("row", "col"), P())
    return jax.shard_map(body, mesh=mesh, in_specs=in_specs, out_specs=out_specs, check_vma=False)
```

```python
import functools
import math

import jax
import jax.numpy as jnp
from jax import lax
from jax.experimental import pallas as pl
from jax.experimental.layout import Layout, with_layout_constraint
from jax.experimental.pallas import tpu as pltpu
from jax.sharding import PartitionSpec as P

MESH = pl.DeviceIdType.MESH
HIGH = lax.Precision.HIGHEST


def turn_kernel(row_count, col_count, total, chunk, chunks, *refs):
    last = chunk == chunks - 1
    if last:
        products, arrived = refs[:chunks], refs[chunks : 2 * chunks - 1]
        diagonal_ref, c_ref, out_ref, stats_ref, recv = refs[2 * chunks - 1 : 2 * chunks + 4]
        refs = refs[2 * chunks + 4 :]
        mine, sums, sum_send, sum_recv = refs[-4:]
    else:
        products = refs[:1]
        recv = refs[1]
        refs = refs[2:]
    p_ref, packed, relay_a, relay_b, load_sem, own_send, recv_sem, arrive_a, arrive_b, send_a, send_b, self_sem = refs[:12]
    row = lax.axis_index("row")
    col = lax.axis_index("col")
    tile = p_ref.shape[0]
    half = tile // 2
    fold = row_count // col_count
    per = fold // chunks
    home = lax.div(row, fold)
    place = lax.rem(row, fold)
    turn = lax.div(place, chunks)
    count = row_count * col_count
    me = row * col_count + col
    is_home = home == col
    takes = lax.rem(place, chunks) == chunk
    if last:
        loads = [
            pltpu.make_async_copy(
                product.at[:, pl.ds(k * tile, tile)],
                p_ref.at[:, pl.ds((q + chunks * k) * tile, tile)],
                load_sem.at[q * per + k],
            )
            for q, product in enumerate(products)
            for k in range(per)
        ]
    else:
        loads = [pltpu.make_async_copy(products[0], p_ref, load_sem.at[0])]
    for load in loads:
        load.start()
    if last:
        diagonal_load = pltpu.make_async_copy(diagonal_ref, out_ref, self_sem.at[3])
        diagonal_load.start()

    barrier = pltpu.get_barrier_semaphore()

    def greet(d, carry):
        other = lax.rem(me + d, count)
        pl.semaphore_signal(
            barrier,
            inc=1,
            device_id=(lax.div(other, col_count), lax.rem(other, col_count)),
            device_id_type=MESH,
        )
        return carry

    lax.fori_loop(1, count, greet, 0)
    pl.semaphore_wait(barrier, count - 1)
    for load in loads:
        load.wait()

    def columns(s):
        return pl.ds(pl.multiple_of(s * tile, tile), tile)

    def remote(src, dst, send, arrive, to_row, to_col):
        return pltpu.make_async_remote_copy(
            src_ref=src,
            dst_ref=dst,
            send_sem=send,
            recv_sem=arrive,
            device_id=(to_row, to_col),
            device_id_type=MESH,
        )

    def spot(k):
        kk = lax.rem(turn + k, per)
        return kk, chunk + chunks * kk

    def own_direct(k):
        kk, s = spot(k)
        near = col * fold + s
        return [
            remote(packed.at[kk, h], recv.at[place, h], own_send.at[kk, h], recv_sem.at[place, h], near, col)
            for h in range(2)
        ]

    def own_relayed(k):
        kk, s = spot(k)
        near = col * fold + s
        slot_a = col - (col > home).astype(jnp.int32)
        slot_b = row - fold * (home > col).astype(jnp.int32)
        return [
            remote(packed.at[kk, 0], relay_a.at[slot_a, kk], own_send.at[kk, 0], arrive_a.at[slot_a, kk], row, home),
            remote(packed.at[kk, 1], relay_b.at[slot_b], own_send.at[kk, 1], arrive_b.at[slot_b], near, col),
        ]

    def own_local():
        return [pltpu.make_async_copy(packed.at[turn, h], recv.at[place, h], self_sem.at[h]) for h in range(2)]

    def pack(k):
        kk, s = spot(k)
        cols = columns(s) if last else columns(kk)
        for h in range(2):
            peak = jnp.max(jnp.abs(p_ref[pl.ds(h * half, half), cols]), axis=0, keepdims=True)
            code = jnp.floor(jnp.log2(jnp.maximum(peak, 1e-30)) * 128.0) + 2.0
            grow = jnp.exp2(code * (-1.0 / 128.0)) * 32767.0
            packed[kk, h, pl.ds(half, 16)] = jnp.broadcast_to(code, (16, tile)).astype(jnp.int32).astype(jnp.int16)
            rows = min(64, half)
            for r in range(0, half, rows):
                value = p_ref[pl.ds(h * half + r, rows), cols] * grow
                packed[kk, h, pl.ds(r, rows)] = jnp.floor(value + 0.5).astype(jnp.int32).astype(jnp.int16)

    def exchange(phase, start):
        def one(d, carry):
            other = lax.rem(me + d, count)
            copy = remote(
                mine.at[phase],
                sums.at[phase, me],
                sum_send.at[phase, d],
                sum_recv.at[phase, me],
                lax.div(other, col_count),
                lax.rem(other, col_count),
            )
            if start:
                copy.start()
            else:
                copy.wait_send()
            return carry

        lax.fori_loop(1, count, one, 0)

    def gather_sums(phase):
        def one(d, carry):
            other = lax.rem(me + d, count)
            remote(
                mine.at[phase],
                sums.at[phase, other],
                sum_send.at[phase, d],
                sum_recv.at[phase, other],
                lax.div(other, col_count),
                lax.rem(other, col_count),
            ).wait_recv()
            return carry

        lax.fori_loop(1, count, one, 0)
        sums[phase, pl.ds(me, 1)] = mine[pl.ds(phase, 1)]
        every = jnp.sum(sums[phase], axis=0)
        return jnp.sum(every[0:8]), jnp.sum(every[8:16])

    def fold_sum(x):
        lanes = x.shape[1] // 128
        out = x[:, 0:128]
        for q in range(1, lanes):
            out = out + x[:, q * 128 : (q + 1) * 128]
        return jnp.sum(out.reshape(x.shape[0] // 8, 8, 128), axis=0)

    zero = jnp.zeros((8, 128), jnp.float32)
    if last:
        step_rows = min(32, tile)

        def early(r, carry):
            rows = pl.ds(pl.multiple_of(r * step_rows, step_rows), step_rows)
            c = c_ref[rows, :].astype(jnp.float32)
            return carry[0] + fold_sum(c * p_ref[rows, :]), carry[1] + fold_sum(c * c)

        proj, weight = lax.fori_loop(0, tile // step_rows, early, (zero, zero))
        mine[0, 0:8] = proj
        mine[0, 8:16] = weight
        exchange(0, True)

    def launch(k, carry):
        pack(k)

        @pl.when(jnp.logical_not(is_home))
        def _():
            for copy in own_relayed(k):
                copy.start()

        @pl.when(jnp.logical_and(is_home, jnp.logical_or(k > 0, jnp.logical_not(takes))))
        def _():
            for copy in own_direct(k):
                copy.start()

        return carry

    lax.fori_loop(0, per, launch, 0)

    @pl.when(jnp.logical_and(is_home, takes))
    def _():
        for copy in own_local():
            copy.start()
        for copy in own_local():
            copy.wait()

    def relay_first(t):
        slot = lax.div(t, per)
        group = slot + (slot >= col).astype(jnp.int32)
        kk, s = spot(lax.rem(t, per))
        return slot, kk, remote(
            relay_a.at[slot, kk], recv.at[place, 0], send_a.at[t], recv_sem.at[place, 0], group * fold + s, col
        )

    def relay_second(t):
        slot = lax.div(t, fold)
        group = slot + (slot >= col).astype(jnp.int32)
        far = lax.rem(place - lax.rem(t, fold) + fold, fold)
        slot_b = slot * fold + far
        return slot_b, remote(
            relay_b.at[slot_b], recv.at[far, 1], send_b.at[t], recv_sem.at[far, 1], row, group
        )

    @pl.when(is_home)
    def _():
        def step(t, carry):
            slot, kk, copy = relay_first(t)
            pltpu.make_async_copy(relay_a.at[slot, kk], relay_a.at[slot, kk], arrive_a.at[slot, kk]).wait()
            copy.start()
            return carry

        lax.fori_loop(0, (col_count - 1) * per, step, 0)

    @pl.when(jnp.logical_and(is_home, takes))
    def _():
        def step(t, carry):
            slot_b, copy = relay_second(t)
            pltpu.make_async_copy(relay_b.at[slot_b], relay_b.at[slot_b], arrive_b.at[slot_b]).wait()
            copy.start()
            return carry

        lax.fori_loop(0, (col_count - 1) * fold, step, 0)

    def await_piece(k):
        s = lax.rem(place - k + fold, fold)

        @pl.when(jnp.logical_and(takes, jnp.logical_not(jnp.logical_and(is_home, k == 0))))
        def _():
            for h in range(2):
                pltpu.make_async_copy(recv.at[s, h], recv.at[s, h], recv_sem.at[s, h]).wait()

    def settle():
        @pl.when(is_home)
        def _():
            def done(k, carry):
                @pl.when(jnp.logical_or(k > 0, jnp.logical_not(takes)))
                def _():
                    for copy in own_direct(k):
                        copy.wait_send()

                return carry

            lax.fori_loop(0, per, done, 0)

            def done_first(t, carry):
                relay_first(t)[-1].wait_send()
                return carry

            lax.fori_loop(0, (col_count - 1) * per, done_first, 0)

        @pl.when(jnp.logical_and(is_home, takes))
        def _():
            def done_second(t, carry):
                relay_second(t)[-1].wait_send()
                return carry

            lax.fori_loop(0, (col_count - 1) * fold, done_second, 0)

        @pl.when(jnp.logical_not(is_home))
        def _():
            def done(k, carry):
                for copy in own_relayed(k):
                    copy.wait_send()
                return carry

            lax.fori_loop(0, per, done, 0)

    if not last:

        def hold(k, carry):
            await_piece(k)
            return carry

        lax.fori_loop(0, fold, hold, 0)
        settle()
        return

    for q, ready in enumerate(arrived):

        @pl.when(lax.rem(place, chunks) == q)
        def _():
            fetch = pltpu.make_async_copy(ready, recv, self_sem.at[2])
            fetch.start()
            fetch.wait()

    proj, weight = gather_sums(0)
    theta = 2.0 * proj / weight
    diagonal_load.wait()

    piece = min(128, tile)

    def finish(k, carry):
        s = lax.rem(place - k + fold, fold)

        await_piece(k)

        def part(r, carry):
            squares, spread = carry
            rows = pl.ds(pl.multiple_of(r * piece, piece), piece)
            for h in range(2):
                cols = pl.ds(pl.multiple_of(s * tile + h * half, half), half)
                code = recv[s, h, pl.ds(half, 16), rows].astype(jnp.int32).astype(jnp.float32)[0:1]
                shrink = jnp.exp2(code * (1.0 / 128.0)) * (1.0 / 32767.0)
                value = recv[s, h, pl.ds(0, half), rows].astype(jnp.int32).astype(jnp.float32)
                turned = (value * shrink).T
                sigma = p_ref[rows, cols] + turned
                residual = sigma - theta * c_ref[rows, cols].astype(jnp.float32)
                update = residual / jnp.maximum(jnp.abs(out_ref[rows, cols] - theta), 1.0)
                out_ref[rows, cols] = update
                squares = squares + fold_sum(residual * residual)
                spread = spread + fold_sum(update * update)
            return squares, spread

        return lax.fori_loop(0, tile // piece, part, carry)

    squares, spread = lax.fori_loop(0, fold, finish, (zero, zero))
    mine[1, 0:8] = squares
    mine[1, 8:16] = spread
    exchange(1, True)
    squares, spread = gather_sums(1)
    stats_ref[0] = theta
    stats_ref[1] = squares / total
    stats_ref[2] = spread / total

    exchange(0, False)
    exchange(1, False)
    settle()


def turn(chunk, chunks, products, arrived, coeff, diagonal, strings):
    tile_rows, tile_cols = coeff.shape
    row_count = lax.axis_size("row")
    col_count = lax.axis_size("col")
    fold = row_count // col_count
    per = fold // chunks
    count = row_count * col_count
    tall = tile_rows // 2 + 16
    others = max(col_count - 1, 1)
    vmem = pl.BlockSpec(memory_space=pltpu.VMEM)
    anywhere = pl.BlockSpec(memory_space=pl.ANY)
    dma = pltpu.SemaphoreType.DMA
    last = chunk == chunks - 1
    arrival = (fold, 2, tall, tile_rows)
    scratch = [
        pltpu.VMEM((tile_rows, tile_cols if last else tile_cols // chunks), jnp.float32),
        pltpu.VMEM((per, 2, tall, tile_rows), jnp.int16),
        pltpu.VMEM((others, per, tall, tile_rows), jnp.int16),
        pltpu.VMEM((others * fold, tall, tile_rows), jnp.int16),
        dma((fold,)),
        dma((per, 2)),
        dma((fold, 2)),
        dma((others, per)),
        dma((others * fold,)),
        dma((others * per,)),
        dma((others * fold,)),
        dma((4,)),
    ]
    if last:
        operands = (*products, *arrived, diagonal, coeff)
        in_specs = [anywhere] * (2 * chunks) + [vmem]
        out_shape = (
            jax.ShapeDtypeStruct((tile_rows, tile_cols), jnp.float32),
            jax.ShapeDtypeStruct((3,), jnp.float32),
        )
        out_specs = (vmem, pl.BlockSpec(memory_space=pltpu.SMEM))
        scratch = [
            pltpu.VMEM(arrival, jnp.int16),
            *scratch,
            pltpu.VMEM((2, 16, 128), jnp.float32),
            pltpu.VMEM((2, count, 16, 128), jnp.float32),
            dma((2, count)),
            dma((2, count)),
        ]
    else:
        operands = (products[chunk],)
        in_specs = [anywhere]
        out_shape = jax.ShapeDtypeStruct(arrival, jnp.int16)
        out_specs = vmem
    return pl.pallas_call(
        functools.partial(turn_kernel, row_count, col_count, float(strings) * float(strings), chunk, chunks),
        out_shape=out_shape,
        in_specs=in_specs,
        out_specs=out_specs,
        scratch_shapes=scratch,
        compiler_params=pltpu.CompilerParams(
            collective_id=chunk,
            has_side_effects=True,
            vmem_limit_bytes=(24 if not last else 60 if chunks == 1 else 60) * 1024 * 1024,
        ),
        name=f"turn_{chunk}",
    )(*operands)


def step_kernel(
    total,
    ham_ref,
    mask_ref,
    coeff_ref,
    occ_ref,
    level_ref,
    coulomb_ref,
    out_ref,
    wide,
    ring,
    stats_ref,
    acc_ref,
    m_ref,
    buf,
    ring_ref,
    c_ref,
    packed,
    relay_a,
    relay_b,
    recv,
    mine_sums,
    sums,
    load_sem,
    send_sem,
    wide_sem,
    ring_sem,
    own_send,
    recv_sem,
    arrive_a,
    arrive_b,
    send_a,
    send_b,
    self_sem,
    sum_send,
    sum_recv,
    ring_load,
):
    rows, strings = ham_ref.shape
    half = coeff_ref.shape[1]
    quarter = rows // 4
    row = lax.axis_index("row")
    col = lax.axis_index("col")
    core = lax.rem(row, 2)
    x = lax.rem(lax.div(row, 2), 2)
    low = lax.rem(lax.div(row, 4), 2)
    high = lax.div(row, 8)
    diag = high == col
    mid = low != high
    fold = half // rows

    def device(h, l, a, k):
        return ((h * 2 + l) * 2 + a) * 2 + k

    targets = {
        "x": (device(high, low, 1 - x, core), col),
        "z": (device(high, 1 - low, x, core), col),
        "y": (row, 1 - col),
        "c": (device(high, low, x, 1 - core), col),
        "cut": (device(1 - high, 1 - low, x, core), col),
    }

    ham_load = pltpu.make_async_copy(ham_ref, m_ref, load_sem.at[0])
    ham_load.start()
    coeff_load = pltpu.make_async_copy(coeff_ref, c_ref, load_sem.at[3])
    coeff_load.start()

    ring_loads = [
        pltpu.make_async_copy(
            coeff_ref.at[:, pl.ds(pl.multiple_of(lax.rem(row + d, fold) * rows, rows), rows)],
            ring_ref.at[:, pl.ds(d * rows, rows)],
            ring_load.at[d],
        )
        for d in range(fold // 2 + 1)
    ]

    @pl.when(diag)
    def _():
        for copy in ring_loads:
            copy.start()

    count = sums.shape[1]
    me = row * 2 + col

    def remote(src, dst, send_one, arrive_one, to_row, to_col):
        return pltpu.make_async_remote_copy(
            src_ref=src,
            dst_ref=dst,
            send_sem=send_one,
            recv_sem=arrive_one,
            device_id=(to_row, to_col),
            device_id_type=MESH,
        )

    barrier = pltpu.get_barrier_semaphore()

    def greet(d, carry):
        other = lax.rem(me + d, count)
        pl.semaphore_signal(
            barrier, inc=1, device_id=(lax.div(other, 2), lax.rem(other, 2)), device_id_type=MESH
        )
        return carry

    lax.fori_loop(1, count, greet, 0)
    pl.semaphore_wait(barrier, count - 1)

    def spot(l, a, k):
        return (l * 2 + a) * 2 + k

    def part(ref, t, q):
        return ref.at[t, pl.ds(q * quarter, quarter)]

    end = jnp.logical_not(mid)
    sent = []

    def send(way, ref, sems, t, q, own=None, when=None):
        src = part(ref, t, q) if own is None else own.at[pl.ds(q * quarter, quarter)]
        if way == "cut":
            when = mid
        copy = pltpu.make_async_remote_copy(
            src_ref=src,
            dst_ref=part(ref, t, q),
            send_sem=send_sem.at[len(sent)],
            recv_sem=sems.at[t, q],
            device_id=targets[way],
            device_id_type=MESH,
        )
        sent.append((copy, when))
        if when is None:
            copy.start()
        else:

            @pl.when(when)
            def _():
                copy.start()

    def settle():
        for copy, when in sent:
            if when is None:
                copy.wait_send()
            else:

                @pl.when(when)
                def _():
                    copy.wait_send()

        sent.clear()

    def arrive(ref, sems, t, q):
        view = part(ref, t, q)
        pltpu.make_async_copy(view, view, sems.at[t, q]).wait()

    def pass_on(ref, sems, t, q, *ways):
        arrive(ref, sems, t, q)
        for way in ways:
            send(way, ref, sems, t, q)
        send("c", ref, sems, t, q)

    def load(ref, sems, l, a, width, own=None):
        mine, other = spot(l, a, core), spot(l, a, 1 - core)
        for q in range(4):
            arrive(ref, sems, other, q)
        src = ref.at[mine] if own is None else own
        first = pltpu.make_async_copy(
            src, buf.at[pl.ds(pl.multiple_of(core * rows, rows), rows), pl.ds(0, width)], load_sem.at[1]
        )
        second = pltpu.make_async_copy(
            ref.at[other],
            buf.at[pl.ds(pl.multiple_of((1 - core) * rows, rows), rows), pl.ds(0, width)],
            load_sem.at[2],
        )
        first.start()
        second.start()
        first.wait()
        second.wait()

    def block(n):
        return pl.ds(pl.multiple_of(n * rows, rows), rows)

    near = col * fold
    away = (1 - col) * fold

    def plain(l, a):
        base = spot(l, a, 0)
        left = pl.ds(pl.multiple_of((away + base) * rows, rows), 2 * rows)

        def one(n, carry):
            acc_ref[:, block(n)] += jnp.dot(m_ref[:, left], buf[:, block(n)], preferred_element_type=jnp.float32)
            return carry

        lax.fori_loop(0, fold, one, 0)

    def turned(l, a):
        base = spot(l, a, 0)

        def one(n, carry):
            total = jnp.zeros((rows, rows), jnp.float32)
            for k in range(0, fold, 2):
                left = pl.ds(pl.multiple_of((away + k) * rows, rows), 2 * rows)
                total = total + lax.dot_general(
                    m_ref[:, left],
                    buf[block(n), pl.ds(k * rows, 2 * rows)],
                    (((1,), (1,)), ((), ())),
                    preferred_element_type=jnp.float32,
                )
            acc_ref[:, block(base + n)] += total
            return carry

        lax.fori_loop(0, 2, one, 0)

    def mirrored(l, a):
        base = spot(l, a, 0)

        def lane(k, carry):
            t = base + k

            def one(d, inner):
                s = lax.rem(t + d, fold)
                tile = buf[block(k), block(d)]
                acc_ref[:, block(s)] += jnp.dot(
                    m_ref[:, block(near + t)], tile, preferred_element_type=jnp.float32
                )

                @pl.when(d > 0)
                def _():
                    acc_ref[:, block(t)] += lax.dot_general(
                        m_ref[:, block(near + s)],
                        tile,
                        (((1,), (1,)), ((), ())),
                        preferred_element_type=jnp.float32,
                    )

                return inner

            last = jnp.where(t < fold // 2, fold // 2 + 1, fold // 2)
            lax.fori_loop(0, last, one, 0)
            return carry

        lax.fori_loop(0, 2, lane, 0)

    def prepare():
        ham_load.wait()
        groups, blocks = mask_ref.shape
        size = strings // blocks
        step = min(1024, strings)
        pick = lax.broadcasted_iota(jnp.int32, (rows, groups), 0) // size == lax.broadcasted_iota(
            jnp.int32, (rows, groups), 1
        )
        tall = jnp.dot(
            pick.astype(jnp.bfloat16), mask_ref[...].astype(jnp.bfloat16), preferred_element_type=jnp.float32
        ).astype(jnp.bfloat16)

        def one(n, carry):
            cols = pl.ds(pl.multiple_of(n * step, step), step)
            spread = (n * step + lax.broadcasted_iota(jnp.int32, (blocks, step), 1)) // size == lax.broadcasted_iota(
                jnp.int32, (blocks, step), 0
            )
            weight = jnp.dot(tall, spread.astype(jnp.bfloat16), preferred_element_type=jnp.float32)
            m_ref[:, cols] = m_ref[:, cols] * weight.astype(jnp.bfloat16)
            acc_ref[:, pl.ds(pl.multiple_of(n * (step // 2), step // 2), step // 2)] = jnp.zeros(
                (rows, step // 2), jnp.float32
            )
            return carry

        lax.fori_loop(0, strings // step, one, 0)

    def energies():
        alpha = occ_ref[:, block(row)].astype(jnp.float32).T
        couple = jnp.dot(alpha, coulomb_ref[...], precision=HIGH, preferred_element_type=jnp.float32)
        energy = jnp.sum(alpha * level_ref[...], axis=1, keepdims=True)

        def one(n, carry):
            beta = occ_ref[:, block(near + n)].astype(jnp.float32)
            out_ref[:, block(n)] = (
                jnp.dot(couple, beta, precision=HIGH, preferred_element_type=jnp.float32)
                + energy
                + jnp.dot(level_ref[...], beta, precision=HIGH, preferred_element_type=jnp.float32)
            )
            return carry

        lax.fori_loop(0, fold, one, 0)

    reach = ring.shape[2]
    W = (wide, wide_sem)
    R = (ring, ring_sem)
    own = spot(low, x, core)
    t_x = spot(low, 1 - x, core)
    t_z = spot(1 - low, x, core)
    t_d = spot(1 - low, 1 - x, core)

    @pl.when(diag)
    def _():
        def mine(way, q):
            send(way, *R, own, q, ring_ref)

        for copy in ring_loads:
            copy.wait()
        for q in range(4):
            mine("cut", q)
            mine("x", q)
            if q < 2:
                mine("z", q)
            mine("c", q)
        prepare()
        pass_on(*R, t_z, 0, "cut")
        pass_on(*W, own, 0, "z")
        pass_on(*R, t_z, 1, "cut")
        pass_on(*W, t_x, 0, "z")
        mine("z", 2)
        mine("z", 3)
        pass_on(*W, t_z, 0, "y")
        pass_on(*R, t_x, 0, "z")
        pass_on(*R, t_x, 1, "z")
        pass_on(*W, t_z, 2, "x")
        pass_on(*W, t_d, 0, "y")
        pass_on(*R, t_x, 2)
        pass_on(*R, t_x, 3)
        pass_on(*R, t_z, 2, "x", "cut")
        pass_on(*W, own, 3, "x")
        pass_on(*R, t_z, 3, "x", "cut")
        pass_on(*W, t_d, 2, "y")
        load(*R, low, x, reach, ring_ref)
        mirrored(low, x)
        pass_on(*W, t_x, 1, "z")
        pass_on(*W, t_x, 3, "y")
        energies()
        load(*R, low, 1 - x, reach)
        mirrored(low, 1 - x)
        pass_on(*W, t_z, 3, "x")
        pass_on(*W, t_d, 1, "y")
        load(*R, 1 - low, x, reach)
        mirrored(1 - low, x)
        pass_on(*W, own, 1, "z")
        for q in range(4):
            pass_on(*R, t_d, q)
        pass_on(*W, t_d, 3, "y")
        load(*R, 1 - low, 1 - x, reach)
        mirrored(1 - low, 1 - x)
        pass_on(*W, own, 2, "x")
        load(*W, 1 - low, 1 - x, half)
        turned(1 - low, 1 - x)
        load(*W, low, x, half)
        turned(low, x)
        pass_on(*W, t_z, 1)
        pass_on(*W, t_x, 2)
        load(*W, 1 - low, x, half)
        turned(1 - low, x)
        load(*W, low, 1 - x, half)
        turned(low, 1 - x)
        settle()

    @pl.when(jnp.logical_not(diag))
    def _():
        def mine(way, q, when=None):
            send(way, *W, own, q, coeff_ref, when)

        mine("y", 0)
        mine("x", 0)
        mine("z", 2)
        mine("x", 1)
        mine("z", 3)
        mine("x", 2)
        mine("z", 1, end)
        for q in range(4):
            mine("c", q)
        pass_on(*W, t_x, 0, "y")
        pass_on(*W, t_z, 2, "y")
        mine("y", 3)
        front = 1 - col
        back = col
        a_own, b_own = spot(front, x, core), spot(back, x, core)
        a_far, b_far = spot(front, 1 - x, core), spot(back, 1 - x, core)

        def inward(t, q):
            arrive(*R, t, q)
            send("x", *R, t, q)
            send("z", *R, t, q, None, mid)
            send("c", *R, t, q)

        prepare()
        pass_on(*W, t_x, 1, "y")
        pass_on(*W, t_z, 3, "y")
        mine("y", 1)
        mine("y", 2)
        inward(a_own, 0)
        inward(a_own, 1)
        load(*W, low, x, half, coeff_ref)
        plain(low, x)
        inward(a_own, 2)
        inward(a_own, 3)
        pass_on(*W, t_x, 2)
        pass_on(*W, t_z, 0)
        inward(b_own, 0)
        pass_on(*W, t_d, 0)
        inward(b_own, 1)
        energies()
        for q in range(4):
            pass_on(*R, a_far, q)
        load(*R, front, x, reach)
        mirrored(front, x)
        pass_on(*W, t_d, 2)
        inward(b_own, 2)
        load(*R, front, 1 - x, reach)
        mirrored(front, 1 - x)
        inward(b_own, 3)
        mine("z", 1, mid)
        pass_on(*W, t_x, 3)
        load(*W, low, 1 - x, half)
        plain(low, 1 - x)
        load(*R, back, x, reach)
        mirrored(back, x)
        pass_on(*W, t_d, 1)
        for q in range(4):
            pass_on(*R, b_far, q)
        pass_on(*W, t_z, 1)
        load(*W, 1 - low, x, half)
        plain(1 - low, x)
        pass_on(*W, t_d, 3)
        load(*R, back, 1 - x, reach)
        mirrored(back, 1 - x)
        load(*W, 1 - low, 1 - x, half)
        plain(1 - low, 1 - x)
        settle()

    place = lax.rem(row, fold)
    far_col = 1 - col
    piece_half = rows // 2

    def own_direct(k):
        s = lax.rem(place + k, fold)
        return [
            remote(packed.at[s, h], recv.at[place, h], own_send.at[s, h], recv_sem.at[place, h], near + s, col)
            for h in range(2)
        ]

    def own_relayed(k):
        s = lax.rem(place + k, fold)
        return [
            remote(packed.at[s, 0], relay_a.at[s], own_send.at[s, 0], arrive_a.at[s], row, far_col),
            remote(packed.at[s, 1], relay_b.at[place], own_send.at[s, 1], arrive_b.at[place], near + s, col),
        ]

    def own_local():
        return [pltpu.make_async_copy(packed.at[place, h], recv.at[place, h], self_sem.at[h]) for h in range(2)]

    def pack(k):
        s = lax.rem(place + k, fold)
        for h in range(2):
            peak = jnp.max(jnp.abs(acc_ref[pl.ds(h * piece_half, piece_half), block(s)]), axis=0, keepdims=True)
            code = jnp.floor(jnp.log2(jnp.maximum(peak, 1e-30)) * 128.0) + 2.0
            grow = jnp.exp2(code * (-1.0 / 128.0)) * 32767.0
            packed[s, h, pl.ds(piece_half, 16)] = (
                jnp.broadcast_to(code, (16, rows)).astype(jnp.int32).astype(jnp.int16)
            )
            for r in range(0, piece_half, 64):
                value = acc_ref[pl.ds(h * piece_half + r, 64), block(s)] * grow
                packed[s, h, pl.ds(r, 64)] = jnp.floor(value + 0.5).astype(jnp.int32).astype(jnp.int16)

    def exchange(phase, start):
        def one(d, carry):
            other = lax.rem(me + d, count)
            copy = remote(
                mine_sums.at[phase],
                sums.at[phase, me],
                sum_send.at[phase, d],
                sum_recv.at[phase, me],
                lax.div(other, 2),
                lax.rem(other, 2),
            )
            if start:
                copy.start()
            else:
                copy.wait_send()
            return carry

        lax.fori_loop(1, count, one, 0)

    def gather_sums(phase):
        def one(d, carry):
            other = lax.rem(me + d, count)
            view = sums.at[phase, other]
            pltpu.make_async_copy(view, view, sum_recv.at[phase, other]).wait()
            return carry

        lax.fori_loop(1, count, one, 0)
        sums[phase, pl.ds(me, 1)] = mine_sums[pl.ds(phase, 1)]
        every = jnp.sum(sums[phase], axis=0)
        return jnp.sum(every[0:8]), jnp.sum(every[8:16])

    def fold_sum(v):
        out = v[:, 0:128]
        for q in range(1, v.shape[1] // 128):
            out = out + v[:, q * 128 : (q + 1) * 128]
        return jnp.sum(out.reshape(v.shape[0] // 8, 8, 128), axis=0)

    zero = jnp.zeros((8, 128), jnp.float32)
    step_rows = min(32, rows)
    coeff_load.wait()

    def early(r, carry):
        band = pl.ds(pl.multiple_of(r * step_rows, step_rows), step_rows)
        c = c_ref[band, :].astype(jnp.float32)
        return carry[0] + fold_sum(c * acc_ref[band, :]), carry[1] + fold_sum(c * c)

    proj, weight = lax.fori_loop(0, rows // step_rows, early, (zero, zero))
    mine_sums[0, 0:8] = proj
    mine_sums[0, 8:16] = weight
    exchange(0, True)

    def relay_first(t):
        s = lax.rem(place + t, fold)
        return s, remote(
            relay_a.at[s], recv.at[place, 0], send_a.at[t], recv_sem.at[place, 0], far_col * fold + s, col
        )

    def relay_second(t):
        far = lax.rem(place - t + fold, fold)
        return far, remote(relay_b.at[far], recv.at[far, 1], send_b.at[t], recv_sem.at[far, 1], row, far_col)

    def launch(k, carry):
        @pl.when(diag)
        def _():
            s, copy = relay_first(k)
            pltpu.make_async_copy(relay_a.at[s], relay_a.at[s], arrive_a.at[s]).wait()
            copy.start()

        pack(k)

        @pl.when(jnp.logical_not(diag))
        def _():
            for copy in own_relayed(k):
                copy.start()

        @pl.when(jnp.logical_and(diag, k > 0))
        def _():
            for copy in own_direct(k):
                copy.start()

        return carry

    lax.fori_loop(0, fold, launch, 0)

    @pl.when(diag)
    def _():
        for copy in own_local():
            copy.start()
        for copy in own_local():
            copy.wait()

    @pl.when(diag)
    def _():
        def relay(t, carry):
            far, copy = relay_second(t)
            pltpu.make_async_copy(relay_b.at[far], relay_b.at[far], arrive_b.at[far]).wait()
            copy.start()
            return carry

        lax.fori_loop(0, fold, relay, 0)

    def await_piece(k):
        s = lax.rem(place - k + fold, fold)

        @pl.when(jnp.logical_not(jnp.logical_and(diag, k == 0)))
        def _():
            for h in range(2):
                pltpu.make_async_copy(recv.at[s, h], recv.at[s, h], recv_sem.at[s, h]).wait()

    proj, weight = gather_sums(0)
    theta = 2.0 * proj / weight
    piece = min(128, rows)

    def finish(k, carry):
        s = lax.rem(place - k + fold, fold)
        await_piece(k)

        def part_of(r, inner):
            squares, spread = inner
            band = pl.ds(pl.multiple_of(r * piece, piece), piece)
            for h in range(2):
                cols = pl.ds(pl.multiple_of(s * rows + h * piece_half, piece_half), piece_half)
                code = recv[s, h, pl.ds(piece_half, 16), band].astype(jnp.int32).astype(jnp.float32)[0:1]
                shrink = jnp.exp2(code * (1.0 / 128.0)) * (1.0 / 32767.0)
                value = recv[s, h, pl.ds(0, piece_half), band].astype(jnp.int32).astype(jnp.float32)
                sigma = acc_ref[band, cols] + (value * shrink).T
                residual = sigma - theta * c_ref[band, cols].astype(jnp.float32)
                update = residual / jnp.maximum(jnp.abs(out_ref[band, cols] - theta), 1.0)
                out_ref[band, cols] = update
                squares = squares + fold_sum(residual * residual)
                spread = spread + fold_sum(update * update)
            return squares, spread

        return lax.fori_loop(0, rows // piece, part_of, carry)

    squares, spread = lax.fori_loop(0, fold, finish, (zero, zero))
    mine_sums[1, 0:8] = squares
    mine_sums[1, 8:16] = spread
    exchange(1, True)
    squares, spread = gather_sums(1)
    stats_ref[0] = theta
    stats_ref[1] = squares / total
    stats_ref[2] = spread / total

    exchange(0, False)
    exchange(1, False)

    @pl.when(diag)
    def _():
        def done(t, carry):
            @pl.when(t > 0)
            def _():
                for copy in own_direct(t):
                    copy.wait_send()

            relay_first(t)[1].wait_send()
            relay_second(t)[1].wait_send()
            return carry

        lax.fori_loop(0, fold, done, 0)

    @pl.when(jnp.logical_not(diag))
    def _():
        def done(t, carry):
            for copy in own_relayed(t):
                copy.wait_send()
            return carry

        lax.fori_loop(0, fold, done, 0)


def whole_step(ham, tile_mask, coeff, occupation, orbital_energy, coulomb):
    rows, strings = ham.shape
    half = coeff.shape[1]
    fold = half // rows
    count = lax.axis_size("row") * lax.axis_size("col")
    reach = (fold // 2 + 1) * rows
    tall = rows // 2 + 16
    anywhere = pl.BlockSpec(memory_space=pl.ANY)
    vmem = pl.BlockSpec(memory_space=pltpu.VMEM)
    dma = pltpu.SemaphoreType.DMA
    update, _, _, sums = pl.pallas_call(
        functools.partial(step_kernel, float(strings) * float(strings)),
        out_shape=(
            jax.ShapeDtypeStruct((rows, half), jnp.float32),
            jax.ShapeDtypeStruct((fold, rows, half), jnp.bfloat16),
            jax.ShapeDtypeStruct((fold, rows, reach), jnp.bfloat16),
            jax.ShapeDtypeStruct((3,), jnp.float32),
        ),
        in_specs=[anywhere, vmem, anywhere, vmem, vmem, vmem],
        out_specs=(vmem, anywhere, anywhere, pl.BlockSpec(memory_space=pltpu.SMEM)),
        scratch_shapes=[
            pltpu.VMEM((rows, half), jnp.float32),
            pltpu.VMEM((rows, strings), jnp.bfloat16),
            pltpu.VMEM((2 * rows, half), jnp.bfloat16),
            pltpu.VMEM((rows, reach), jnp.bfloat16),
            pltpu.VMEM((rows, half), jnp.bfloat16),
            pltpu.VMEM((fold, 2, tall, rows), jnp.int16),
            pltpu.VMEM((fold, tall, rows), jnp.int16),
            pltpu.VMEM((fold, tall, rows), jnp.int16),
            pltpu.VMEM((fold, 2, tall, rows), jnp.int16),
            pltpu.VMEM((2, 16, 128), jnp.float32),
            pltpu.VMEM((2, count, 16, 128), jnp.float32),
            dma((4,)),
            dma((80,)),
            dma((fold, 4)),
            dma((fold, 4)),
            dma((fold, 2)),
            dma((fold, 2)),
            dma((fold,)),
            dma((fold,)),
            dma((fold,)),
            dma((fold,)),
            dma((2,)),
            dma((2, count)),
            dma((2, count)),
            dma((fold // 2 + 1,)),
        ],
        compiler_params=pltpu.CompilerParams(
            collective_id=9, has_side_effects=True, vmem_limit_bytes=62 * 1024 * 1024
        ),
        name="whole_step",
    )(ham, tile_mask, coeff, occupation, orbital_energy[None, :], coulomb)
    return update, sums


CHUNKS = 2


def body(ham, coeff, tile_mask, occupation, orbital_energy, coulomb):
    tile_rows, strings = ham.shape
    tile_cols = coeff.shape[1]
    fold = tile_cols // tile_rows
    direct = lax.axis_size("col") == 2 and lax.axis_size("row") == 16
    if direct:
        result = whole_step(ham, tile_mask, coeff, occupation, orbital_energy, coulomb)
    else:
        occ_float = occupation.astype(jnp.float32)
        occ_alpha = lax.dynamic_slice_in_dim(occ_float, lax.axis_index("row") * tile_rows, tile_rows, 1)
        occ_beta = lax.dynamic_slice_in_dim(occ_float, lax.axis_index("col") * tile_cols, tile_cols, 1)
        energy_alpha = jnp.dot(orbital_energy, occ_alpha, precision=HIGH)
        energy_beta = jnp.dot(orbital_energy, occ_beta, precision=HIGH)
        couple = jnp.dot(occ_alpha.T, coulomb, precision=HIGH)
        diagonal = energy_alpha[:, None] + energy_beta[None, :] + jnp.dot(couple, occ_beta, precision=HIGH)
        mask_cols = tile_mask.shape[1]
        block_size = strings // mask_cols
        mask_rows = tile_rows // block_size
        weights = tile_mask.astype(jnp.bfloat16)[:, None, :, None]
        masked = (ham.reshape(mask_rows, block_size, mask_cols, block_size) * weights).reshape(tile_rows, strings)
        chunks = math.gcd(CHUNKS, fold)
        products = []
        arrived = []
        for q in range(chunks):
            part = jnp.concatenate(
                [coeff[:, s * tile_rows : (s + 1) * tile_rows] for s in range(q, fold, chunks)], axis=1
            )
            gathered = with_layout_constraint(lax.all_gather(part, "row", axis=0, tiled=True), Layout((0, 1)))
            products.append(jnp.dot(masked, gathered, preferred_element_type=jnp.float32))
            result = turn(q, chunks, products, arrived, coeff, diagonal, strings)
            if q < chunks - 1:
                arrived.append(result)
    update, sums = result
    correction = update * lax.rsqrt(sums[2] + 1e-06)
    stats = jnp.stack([sums[0], jnp.sqrt(sums[1])])
    return (correction, stats)


def solution(mesh):
    in_specs = (P("row", None), P("row", "col"), P("row", None), P(), P(), P())
    out_specs = (P("row", "col"), P())
    return jax.shard_map(body, mesh=mesh, in_specs=in_specs, out_specs=out_specs, check_vma=False)
```

```python
import functools
import math

import jax
import jax.numpy as jnp
from jax import lax
from jax.experimental import pallas as pl
from jax.experimental.layout import Layout, with_layout_constraint
from jax.experimental.pallas import tpu as pltpu
from jax.sharding import PartitionSpec as P

MESH = pl.DeviceIdType.MESH
HIGH = lax.Precision.HIGHEST


def turn_kernel(row_count, col_count, total, chunk, chunks, *refs):
    last = chunk == chunks - 1
    if last:
        products, arrived = refs[:chunks], refs[chunks : 2 * chunks - 1]
        diagonal_ref, c_ref, out_ref, stats_ref, recv = refs[2 * chunks - 1 : 2 * chunks + 4]
        refs = refs[2 * chunks + 4 :]
        mine, sums, sum_send, sum_recv = refs[-4:]
    else:
        products = refs[:1]
        recv = refs[1]
        refs = refs[2:]
    p_ref, packed, relay_a, relay_b, load_sem, own_send, recv_sem, arrive_a, arrive_b, send_a, send_b, self_sem = refs[:12]
    row = lax.axis_index("row")
    col = lax.axis_index("col")
    tile = p_ref.shape[0]
    half = tile // 2
    fold = row_count // col_count
    per = fold // chunks
    home = lax.div(row, fold)
    place = lax.rem(row, fold)
    turn = lax.div(place, chunks)
    count = row_count * col_count
    me = row * col_count + col
    is_home = home == col
    takes = lax.rem(place, chunks) == chunk
    if last:
        loads = [
            pltpu.make_async_copy(
                product.at[:, pl.ds(k * tile, tile)],
                p_ref.at[:, pl.ds((q + chunks * k) * tile, tile)],
                load_sem.at[q * per + k],
            )
            for q, product in enumerate(products)
            for k in range(per)
        ]
    else:
        loads = [pltpu.make_async_copy(products[0], p_ref, load_sem.at[0])]
    for load in loads:
        load.start()
    if last:
        diagonal_load = pltpu.make_async_copy(diagonal_ref, out_ref, self_sem.at[3])
        diagonal_load.start()

    barrier = pltpu.get_barrier_semaphore()

    def greet(d, carry):
        other = lax.rem(me + d, count)
        pl.semaphore_signal(
            barrier,
            inc=1,
            device_id=(lax.div(other, col_count), lax.rem(other, col_count)),
            device_id_type=MESH,
        )
        return carry

    lax.fori_loop(1, count, greet, 0)
    pl.semaphore_wait(barrier, count - 1)
    for load in loads:
        load.wait()

    def columns(s):
        return pl.ds(pl.multiple_of(s * tile, tile), tile)

    def remote(src, dst, send, arrive, to_row, to_col):
        return pltpu.make_async_remote_copy(
            src_ref=src,
            dst_ref=dst,
            send_sem=send,
            recv_sem=arrive,
            device_id=(to_row, to_col),
            device_id_type=MESH,
        )

    def spot(k):
        kk = lax.rem(turn + k, per)
        return kk, chunk + chunks * kk

    def own_direct(k):
        kk, s = spot(k)
        near = col * fold + s
        return [
            remote(packed.at[kk, h], recv.at[place, h], own_send.at[kk, h], recv_sem.at[place, h], near, col)
            for h in range(2)
        ]

    def own_relayed(k):
        kk, s = spot(k)
        near = col * fold + s
        slot_a = col - (col > home).astype(jnp.int32)
        slot_b = row - fold * (home > col).astype(jnp.int32)
        return [
            remote(packed.at[kk, 0], relay_a.at[slot_a, kk], own_send.at[kk, 0], arrive_a.at[slot_a, kk], row, home),
            remote(packed.at[kk, 1], relay_b.at[slot_b], own_send.at[kk, 1], arrive_b.at[slot_b], near, col),
        ]

    def own_local():
        return [pltpu.make_async_copy(packed.at[turn, h], recv.at[place, h], self_sem.at[h]) for h in range(2)]

    def pack(k):
        kk, s = spot(k)
        cols = columns(s) if last else columns(kk)
        for h in range(2):
            peak = jnp.max(jnp.abs(p_ref[pl.ds(h * half, half), cols]), axis=0, keepdims=True)
            code = jnp.floor(jnp.log2(jnp.maximum(peak, 1e-30)) * 128.0) + 2.0
            grow = jnp.exp2(code * (-1.0 / 128.0)) * 32767.0
            packed[kk, h, pl.ds(half, 16)] = jnp.broadcast_to(code, (16, tile)).astype(jnp.int32).astype(jnp.int16)
            rows = min(64, half)
            for r in range(0, half, rows):
                value = p_ref[pl.ds(h * half + r, rows), cols] * grow
                packed[kk, h, pl.ds(r, rows)] = jnp.floor(value + 0.5).astype(jnp.int32).astype(jnp.int16)

    def exchange(phase, start):
        def one(d, carry):
            other = lax.rem(me + d, count)
            copy = remote(
                mine.at[phase],
                sums.at[phase, me],
                sum_send.at[phase, d],
                sum_recv.at[phase, me],
                lax.div(other, col_count),
                lax.rem(other, col_count),
            )
            if start:
                copy.start()
            else:
                copy.wait_send()
            return carry

        lax.fori_loop(1, count, one, 0)

    def gather_sums(phase):
        def one(d, carry):
            other = lax.rem(me + d, count)
            remote(
                mine.at[phase],
                sums.at[phase, other],
                sum_send.at[phase, d],
                sum_recv.at[phase, other],
                lax.div(other, col_count),
                lax.rem(other, col_count),
            ).wait_recv()
            return carry

        lax.fori_loop(1, count, one, 0)
        sums[phase, pl.ds(me, 1)] = mine[pl.ds(phase, 1)]
        every = jnp.sum(sums[phase], axis=0)
        return jnp.sum(every[0:8]), jnp.sum(every[8:16])

    def fold_sum(x):
        lanes = x.shape[1] // 128
        out = x[:, 0:128]
        for q in range(1, lanes):
            out = out + x[:, q * 128 : (q + 1) * 128]
        return jnp.sum(out.reshape(x.shape[0] // 8, 8, 128), axis=0)

    zero = jnp.zeros((8, 128), jnp.float32)
    if last:
        step_rows = min(32, tile)

        def early(r, carry):
            rows = pl.ds(pl.multiple_of(r * step_rows, step_rows), step_rows)
            c = c_ref[rows, :].astype(jnp.float32)
            return carry[0] + fold_sum(c * p_ref[rows, :]), carry[1] + fold_sum(c * c)

        proj, weight = lax.fori_loop(0, tile // step_rows, early, (zero, zero))
        mine[0, 0:8] = proj
        mine[0, 8:16] = weight
        exchange(0, True)

    def launch(k, carry):
        pack(k)

        @pl.when(jnp.logical_not(is_home))
        def _():
            for copy in own_relayed(k):
                copy.start()

        @pl.when(jnp.logical_and(is_home, jnp.logical_or(k > 0, jnp.logical_not(takes))))
        def _():
            for copy in own_direct(k):
                copy.start()

        return carry

    lax.fori_loop(0, per, launch, 0)

    @pl.when(jnp.logical_and(is_home, takes))
    def _():
        for copy in own_local():
            copy.start()
        for copy in own_local():
            copy.wait()

    def relay_first(t):
        slot = lax.div(t, per)
        group = slot + (slot >= col).astype(jnp.int32)
        kk, s = spot(lax.rem(t, per))
        return slot, kk, remote(
            relay_a.at[slot, kk], recv.at[place, 0], send_a.at[t], recv_sem.at[place, 0], group * fold + s, col
        )

    def relay_second(t):
        slot = lax.div(t, fold)
        group = slot + (slot >= col).astype(jnp.int32)
        far = lax.rem(place - lax.rem(t, fold) + fold, fold)
        slot_b = slot * fold + far
        return slot_b, remote(
            relay_b.at[slot_b], recv.at[far, 1], send_b.at[t], recv_sem.at[far, 1], row, group
        )

    @pl.when(is_home)
    def _():
        def step(t, carry):
            slot, kk, copy = relay_first(t)
            pltpu.make_async_copy(relay_a.at[slot, kk], relay_a.at[slot, kk], arrive_a.at[slot, kk]).wait()
            copy.start()
            return carry

        lax.fori_loop(0, (col_count - 1) * per, step, 0)

    @pl.when(jnp.logical_and(is_home, takes))
    def _():
        def step(t, carry):
            slot_b, copy = relay_second(t)
            pltpu.make_async_copy(relay_b.at[slot_b], relay_b.at[slot_b], arrive_b.at[slot_b]).wait()
            copy.start()
            return carry

        lax.fori_loop(0, (col_count - 1) * fold, step, 0)

    def await_piece(k):
        s = lax.rem(place - k + fold, fold)

        @pl.when(jnp.logical_and(takes, jnp.logical_not(jnp.logical_and(is_home, k == 0))))
        def _():
            for h in range(2):
                pltpu.make_async_copy(recv.at[s, h], recv.at[s, h], recv_sem.at[s, h]).wait()

    def settle():
        @pl.when(is_home)
        def _():
            def done(k, carry):
                @pl.when(jnp.logical_or(k > 0, jnp.logical_not(takes)))
                def _():
                    for copy in own_direct(k):
                        copy.wait_send()

                return carry

            lax.fori_loop(0, per, done, 0)

            def done_first(t, carry):
                relay_first(t)[-1].wait_send()
                return carry

            lax.fori_loop(0, (col_count - 1) * per, done_first, 0)

        @pl.when(jnp.logical_and(is_home, takes))
        def _():
            def done_second(t, carry):
                relay_second(t)[-1].wait_send()
                return carry

            lax.fori_loop(0, (col_count - 1) * fold, done_second, 0)

        @pl.when(jnp.logical_not(is_home))
        def _():
            def done(k, carry):
                for copy in own_relayed(k):
                    copy.wait_send()
                return carry

            lax.fori_loop(0, per, done, 0)

    if not last:

        def hold(k, carry):
            await_piece(k)
            return carry

        lax.fori_loop(0, fold, hold, 0)
        settle()
        return

    for q, ready in enumerate(arrived):

        @pl.when(lax.rem(place, chunks) == q)
        def _():
            fetch = pltpu.make_async_copy(ready, recv, self_sem.at[2])
            fetch.start()
            fetch.wait()

    proj, weight = gather_sums(0)
    theta = 2.0 * proj / weight
    diagonal_load.wait()

    piece = min(128, tile)

    def finish(k, carry):
        s = lax.rem(place - k + fold, fold)

        await_piece(k)

        def part(r, carry):
            squares, spread = carry
            rows = pl.ds(pl.multiple_of(r * piece, piece), piece)
            for h in range(2):
                cols = pl.ds(pl.multiple_of(s * tile + h * half, half), half)
                code = recv[s, h, pl.ds(half, 16), rows].astype(jnp.int32).astype(jnp.float32)[0:1]
                shrink = jnp.exp2(code * (1.0 / 128.0)) * (1.0 / 32767.0)
                value = recv[s, h, pl.ds(0, half), rows].astype(jnp.int32).astype(jnp.float32)
                turned = (value * shrink).T
                sigma = p_ref[rows, cols] + turned
                residual = sigma - theta * c_ref[rows, cols].astype(jnp.float32)
                update = residual / jnp.maximum(jnp.abs(out_ref[rows, cols] - theta), 1.0)
                out_ref[rows, cols] = update
                squares = squares + fold_sum(residual * residual)
                spread = spread + fold_sum(update * update)
            return squares, spread

        return lax.fori_loop(0, tile // piece, part, carry)

    squares, spread = lax.fori_loop(0, fold, finish, (zero, zero))
    mine[1, 0:8] = squares
    mine[1, 8:16] = spread
    exchange(1, True)
    squares, spread = gather_sums(1)
    stats_ref[0] = theta
    stats_ref[1] = squares / total
    stats_ref[2] = spread / total

    exchange(0, False)
    exchange(1, False)
    settle()


def turn(chunk, chunks, products, arrived, coeff, diagonal, strings):
    tile_rows, tile_cols = coeff.shape
    row_count = lax.axis_size("row")
    col_count = lax.axis_size("col")
    fold = row_count // col_count
    per = fold // chunks
    count = row_count * col_count
    tall = tile_rows // 2 + 16
    others = max(col_count - 1, 1)
    vmem = pl.BlockSpec(memory_space=pltpu.VMEM)
    anywhere = pl.BlockSpec(memory_space=pl.ANY)
    dma = pltpu.SemaphoreType.DMA
    last = chunk == chunks - 1
    arrival = (fold, 2, tall, tile_rows)
    scratch = [
        pltpu.VMEM((tile_rows, tile_cols if last else tile_cols // chunks), jnp.float32),
        pltpu.VMEM((per, 2, tall, tile_rows), jnp.int16),
        pltpu.VMEM((others, per, tall, tile_rows), jnp.int16),
        pltpu.VMEM((others * fold, tall, tile_rows), jnp.int16),
        dma((fold,)),
        dma((per, 2)),
        dma((fold, 2)),
        dma((others, per)),
        dma((others * fold,)),
        dma((others * per,)),
        dma((others * fold,)),
        dma((4,)),
    ]
    if last:
        operands = (*products, *arrived, diagonal, coeff)
        in_specs = [anywhere] * (2 * chunks) + [vmem]
        out_shape = (
            jax.ShapeDtypeStruct((tile_rows, tile_cols), jnp.float32),
            jax.ShapeDtypeStruct((3,), jnp.float32),
        )
        out_specs = (vmem, pl.BlockSpec(memory_space=pltpu.SMEM))
        scratch = [
            pltpu.VMEM(arrival, jnp.int16),
            *scratch,
            pltpu.VMEM((2, 16, 128), jnp.float32),
            pltpu.VMEM((2, count, 16, 128), jnp.float32),
            dma((2, count)),
            dma((2, count)),
        ]
    else:
        operands = (products[chunk],)
        in_specs = [anywhere]
        out_shape = jax.ShapeDtypeStruct(arrival, jnp.int16)
        out_specs = vmem
    return pl.pallas_call(
        functools.partial(turn_kernel, row_count, col_count, float(strings) * float(strings), chunk, chunks),
        out_shape=out_shape,
        in_specs=in_specs,
        out_specs=out_specs,
        scratch_shapes=scratch,
        compiler_params=pltpu.CompilerParams(
            collective_id=chunk,
            has_side_effects=True,
            vmem_limit_bytes=(24 if not last else 60 if chunks == 1 else 60) * 1024 * 1024,
        ),
        name=f"turn_{chunk}",
    )(*operands)


def step_kernel(
    total,
    ham_ref,
    mask_ref,
    coeff_ref,
    occ_ref,
    level_ref,
    coulomb_ref,
    out_ref,
    wide,
    ring,
    stats_ref,
    scale_ref,
    acc_ref,
    m_ref,
    buf,
    ring_ref,
    c_ref,
    packed,
    relay_a,
    relay_b,
    recv,
    mine_sums,
    sums,
    load_sem,
    send_sem,
    wide_sem,
    ring_sem,
    own_send,
    recv_sem,
    arrive_a,
    arrive_b,
    send_a,
    send_b,
    self_sem,
    sum_send,
    sum_recv,
    ring_load,
):
    rows, strings = ham_ref.shape
    half = coeff_ref.shape[1]
    quarter = rows // 4
    row = lax.axis_index("row")
    col = lax.axis_index("col")
    core = lax.rem(row, 2)
    x = lax.rem(lax.div(row, 2), 2)
    low = lax.rem(lax.div(row, 4), 2)
    high = lax.div(row, 8)
    diag = high == col
    mid = low != high
    fold = half // rows

    def device(h, l, a, k):
        return ((h * 2 + l) * 2 + a) * 2 + k

    targets = {
        "x": (device(high, low, 1 - x, core), col),
        "z": (device(high, 1 - low, x, core), col),
        "y": (row, 1 - col),
        "c": (device(high, low, x, 1 - core), col),
        "cut": (device(1 - high, 1 - low, x, core), col),
    }

    ham_load = pltpu.make_async_copy(ham_ref, m_ref, load_sem.at[0])
    ham_load.start()
    coeff_load = pltpu.make_async_copy(coeff_ref, c_ref, load_sem.at[3])
    coeff_load.start()

    ring_loads = [
        pltpu.make_async_copy(
            coeff_ref.at[:, pl.ds(pl.multiple_of(lax.rem(row + d, fold) * rows, rows), rows)],
            ring_ref.at[:, pl.ds(d * rows, rows)],
            ring_load.at[d],
        )
        for d in range(fold // 2 + 1)
    ]

    @pl.when(diag)
    def _():
        for copy in ring_loads:
            copy.start()

    count = sums.shape[1]
    me = row * 2 + col

    def remote(src, dst, send_one, arrive_one, to_row, to_col):
        return pltpu.make_async_remote_copy(
            src_ref=src,
            dst_ref=dst,
            send_sem=send_one,
            recv_sem=arrive_one,
            device_id=(to_row, to_col),
            device_id_type=MESH,
        )

    barrier = pltpu.get_barrier_semaphore()

    def greet(d, carry):
        other = lax.rem(me + d, count)
        pl.semaphore_signal(
            barrier, inc=1, device_id=(lax.div(other, 2), lax.rem(other, 2)), device_id_type=MESH
        )
        return carry

    lax.fori_loop(1, count, greet, 0)
    pl.semaphore_wait(barrier, count - 1)

    def spot(l, a, k):
        return (l * 2 + a) * 2 + k

    def cuts(ref, q):
        return 2 if ref is wide and q in (1, 2) else 1

    def span(ref, q, sub):
        size = quarter // cuts(ref, q)
        return pl.ds(q * quarter + sub * size, size)

    end = jnp.logical_not(mid)
    sent = []

    def send(way, ref, sems, t, q, own=None, when=None, sub=None):
        if sub is None:
            for one in range(cuts(ref, q)):
                send(way, ref, sems, t, q, own, when, one)
            return
        src = ref.at[t] if own is None else own
        if way == "cut":
            when = mid
        copy = pltpu.make_async_remote_copy(
            src_ref=src.at[span(ref, q, sub)],
            dst_ref=ref.at[t, span(ref, q, sub)],
            send_sem=send_sem.at[len(sent)],
            recv_sem=sems.at[t, q, sub],
            device_id=targets[way],
            device_id_type=MESH,
        )
        sent.append((copy, when))
        if when is None:
            copy.start()
        else:

            @pl.when(when)
            def _():
                copy.start()

    def settle():
        for copy, when in sent:
            if when is None:
                copy.wait_send()
            else:

                @pl.when(when)
                def _():
                    copy.wait_send()

        sent.clear()

    def arrive(ref, sems, t, q, sub):
        view = ref.at[t, span(ref, q, sub)]
        pltpu.make_async_copy(view, view, sems.at[t, q, sub]).wait()

    def pass_on(ref, sems, t, q, *ways):
        for sub in range(cuts(ref, q)):
            arrive(ref, sems, t, q, sub)
            for way in ways:
                send(way, ref, sems, t, q, sub=sub)
            send("c", ref, sems, t, q, sub=sub)

    short = rows // 2

    def load(ref, sems, l, a, width, own=None, side=None):
        mine, other = spot(l, a, core), spot(l, a, 1 - core)
        first_row, size = (0, rows) if side is None else (side * short, short)
        for q in range(first_row // quarter, (first_row + size) // quarter):
            for sub in range(cuts(ref, q)):
                arrive(ref, sems, other, q, sub)
        src = ref.at[mine] if own is None else own
        copies = [
            pltpu.make_async_copy(
                one.at[pl.ds(first_row, size)],
                buf.at[pl.ds(pl.multiple_of(k * rows + first_row, short), size), pl.ds(0, width)],
                load_sem.at[n],
            )
            for n, one, k in ((1, src, core), (2, ref.at[other], 1 - core))
        ]
        for copy in copies:
            copy.start()
        for copy in copies:
            copy.wait()

    def piece_of(n, side):
        if side is None:
            return block(n)
        return pl.ds(pl.multiple_of(n * rows + side * short, short), short)

    def block(n):
        return pl.ds(pl.multiple_of(n * rows, rows), rows)

    near = col * fold
    away = (1 - col) * fold

    def plain(l, a, side=None):
        base = spot(l, a, 0)

        def one(n, carry):
            if side is None:
                left = pl.ds(pl.multiple_of((away + base) * rows, rows), 2 * rows)
                total = jnp.dot(m_ref[:, left], buf[:, block(n)], preferred_element_type=jnp.float32)
            else:
                total = sum(
                    jnp.dot(
                        m_ref[:, piece_of(away + base + k, side)],
                        buf[piece_of(k, side), block(n)],
                        preferred_element_type=jnp.float32,
                    )
                    for k in range(2)
                )
            acc_ref[:, block(n)] += total
            return carry

        lax.fori_loop(0, fold, one, 0)

    def turned(l, a, side=None):
        base = spot(l, a, 0)

        def one(n, carry):
            total = 0.0
            for k in range(0, fold, 2):
                left = pl.ds(pl.multiple_of((away + k) * rows, rows), 2 * rows)
                total = total + lax.dot_general(
                    m_ref[:, left],
                    buf[piece_of(n, side), pl.ds(k * rows, 2 * rows)],
                    (((1,), (1,)), ((), ())),
                    preferred_element_type=jnp.float32,
                )
            acc_ref[:, piece_of(base + n, side)] += total
            return carry

        lax.fori_loop(0, 2, one, 0)

    def mirrored(l, a, side=None):
        base = spot(l, a, 0)

        def lane(k, carry):
            t = base + k

            def one(d, inner):
                s = lax.rem(t + d, fold)
                tile = buf[piece_of(k, side), block(d)]
                acc_ref[:, block(s)] += jnp.dot(
                    m_ref[:, piece_of(near + t, side)], tile, preferred_element_type=jnp.float32
                )

                @pl.when(d > 0)
                def _():
                    acc_ref[:, piece_of(t, side)] += lax.dot_general(
                        m_ref[:, block(near + s)],
                        tile,
                        (((1,), (1,)), ((), ())),
                        preferred_element_type=jnp.float32,
                    )

                return inner

            last = jnp.where(t < fold // 2, fold // 2 + 1, fold // 2)
            lax.fori_loop(0, last, one, 0)
            return carry

        lax.fori_loop(0, 2, lane, 0)

    def prepare():
        ham_load.wait()
        groups, blocks = mask_ref.shape
        size = strings // blocks
        step = min(1024, strings)
        pick = lax.broadcasted_iota(jnp.int32, (rows, groups), 0) // size == lax.broadcasted_iota(
            jnp.int32, (rows, groups), 1
        )
        tall = jnp.dot(
            pick.astype(jnp.bfloat16), mask_ref[...].astype(jnp.bfloat16), preferred_element_type=jnp.float32
        ).astype(jnp.bfloat16)

        def one(n, carry):
            cols = pl.ds(pl.multiple_of(n * step, step), step)
            spread = (n * step + lax.broadcasted_iota(jnp.int32, (blocks, step), 1)) // size == lax.broadcasted_iota(
                jnp.int32, (blocks, step), 0
            )
            weight = jnp.dot(tall, spread.astype(jnp.bfloat16), preferred_element_type=jnp.float32)
            m_ref[:, cols] = m_ref[:, cols] * weight.astype(jnp.bfloat16)
            acc_ref[:, pl.ds(pl.multiple_of(n * (step // 2), step // 2), step // 2)] = jnp.zeros(
                (rows, step // 2), jnp.float32
            )
            return carry

        lax.fori_loop(0, strings // step, one, 0)

    def energies():
        alpha = occ_ref[:, block(row)].astype(jnp.float32).T
        couple = jnp.dot(alpha, coulomb_ref[...], precision=HIGH, preferred_element_type=jnp.float32)
        energy = jnp.sum(alpha * level_ref[...], axis=1, keepdims=True)

        def one(n, carry):
            beta = occ_ref[:, block(near + n)].astype(jnp.float32)
            out_ref[:, block(n)] = (
                jnp.dot(couple, beta, precision=HIGH, preferred_element_type=jnp.float32)
                + energy
                + jnp.dot(level_ref[...], beta, precision=HIGH, preferred_element_type=jnp.float32)
            )
            return carry

        lax.fori_loop(0, fold, one, 0)

    reach = ring.shape[2]
    W = (wide, wide_sem)
    R = (ring, ring_sem)
    own = spot(low, x, core)
    t_x = spot(low, 1 - x, core)
    t_z = spot(1 - low, x, core)
    t_d = spot(1 - low, 1 - x, core)

    @pl.when(diag)
    def _():
        def mine(way, q):
            send(way, *R, own, q, ring_ref)

        for copy in ring_loads:
            copy.wait()
        for q in range(4):
            mine("cut", q)
            mine("x", q)
            if q < 2:
                mine("z", q)
            mine("c", q)
        prepare()
        pass_on(*R, t_z, 0, "cut")
        pass_on(*W, own, 0, "z")
        pass_on(*R, t_z, 1, "cut")
        pass_on(*W, t_x, 0, "z")
        mine("z", 2)
        mine("z", 3)
        pass_on(*W, t_z, 0, "y")
        pass_on(*R, t_x, 0, "z")
        pass_on(*R, t_x, 1, "z")
        pass_on(*W, t_z, 2, "x")
        pass_on(*W, t_d, 0, "y")
        pass_on(*R, t_x, 2)
        pass_on(*R, t_x, 3)
        pass_on(*R, t_z, 2, "x", "cut")
        pass_on(*W, own, 3, "x")
        pass_on(*R, t_z, 3, "x", "cut")
        pass_on(*W, t_d, 2, "y")
        load(*R, low, x, reach, ring_ref)
        mirrored(low, x)
        pass_on(*W, t_x, 1, "z")
        pass_on(*W, t_x, 3, "y")
        energies()
        load(*R, low, 1 - x, reach)
        mirrored(low, 1 - x)
        pass_on(*W, t_z, 3, "x")
        pass_on(*W, t_d, 1, "y")
        load(*R, 1 - low, x, reach)
        mirrored(1 - low, x)
        pass_on(*W, own, 1, "z")
        for q in range(4):
            pass_on(*R, t_d, q)
        pass_on(*W, t_d, 3, "y")
        load(*R, 1 - low, 1 - x, reach)
        mirrored(1 - low, 1 - x)
        pass_on(*W, own, 2, "x")
        load(*W, 1 - low, 1 - x, half)
        turned(1 - low, 1 - x)
        load(*W, low, x, half)
        turned(low, x)
        pass_on(*W, t_z, 1)
        pass_on(*W, t_x, 2)
        load(*W, 1 - low, x, half)
        turned(1 - low, x)
        load(*W, low, 1 - x, half)
        turned(low, 1 - x)
        settle()

    @pl.when(jnp.logical_not(diag))
    def _():
        def mine(way, q, when=None):
            send(way, *W, own, q, coeff_ref, when)

        mine("y", 0)
        mine("x", 0)
        mine("z", 2)
        mine("x", 1)
        mine("z", 3)
        mine("x", 2)
        mine("z", 1, end)
        for q in range(4):
            mine("c", q)
        pass_on(*W, t_x, 0, "y")
        pass_on(*W, t_z, 2, "y")
        mine("y", 3)
        front = 1 - col
        back = col
        a_own, b_own = spot(front, x, core), spot(back, x, core)
        a_far, b_far = spot(front, 1 - x, core), spot(back, 1 - x, core)

        def inward(t, q):
            arrive(*R, t, q, 0)
            send("x", *R, t, q)
            send("z", *R, t, q, None, mid)
            send("c", *R, t, q)

        prepare()
        pass_on(*W, t_x, 1, "y")
        pass_on(*W, t_z, 3, "y")
        mine("y", 1)
        mine("y", 2)
        inward(a_own, 0)
        inward(a_own, 1)
        load(*W, low, x, half, coeff_ref)
        plain(low, x)
        inward(a_own, 2)
        inward(a_own, 3)
        pass_on(*W, t_x, 2)
        pass_on(*W, t_z, 0)
        inward(b_own, 0)
        pass_on(*W, t_d, 0)
        inward(b_own, 1)
        energies()
        for q in range(4):
            pass_on(*R, a_far, q)
        load(*R, front, x, reach)
        mirrored(front, x)
        pass_on(*W, t_d, 2)
        inward(b_own, 2)
        load(*R, front, 1 - x, reach)
        mirrored(front, 1 - x)
        inward(b_own, 3)
        mine("z", 1, mid)
        pass_on(*W, t_x, 3)
        load(*W, low, 1 - x, half)
        plain(low, 1 - x)
        load(*R, back, x, reach)
        mirrored(back, x)
        pass_on(*W, t_d, 1)
        for q in range(4):
            pass_on(*R, b_far, q)
        pass_on(*W, t_z, 1)
        load(*W, 1 - low, x, half)
        plain(1 - low, x)
        pass_on(*W, t_d, 3)
        load(*R, back, 1 - x, reach)
        mirrored(back, 1 - x)
        load(*W, 1 - low, 1 - x, half)
        plain(1 - low, 1 - x)
        settle()

    place = lax.rem(row, fold)
    far_col = 1 - col
    piece_half = rows // 2

    def own_direct(k):
        s = lax.rem(place + k, fold)
        return [
            remote(packed.at[s, h], recv.at[place, h], own_send.at[s, h], recv_sem.at[place, h], near + s, col)
            for h in range(2)
        ]

    def own_relayed(k):
        s = lax.rem(place + k, fold)
        return [
            remote(packed.at[s, 0], relay_a.at[s], own_send.at[s, 0], arrive_a.at[s], row, far_col),
            remote(packed.at[s, 1], relay_b.at[place], own_send.at[s, 1], arrive_b.at[place], near + s, col),
        ]

    def own_local():
        return [pltpu.make_async_copy(packed.at[place, h], recv.at[place, h], self_sem.at[h]) for h in range(2)]

    def pack(k):
        s = lax.rem(place + k, fold)
        for h in range(2):
            peak = jnp.max(jnp.abs(acc_ref[pl.ds(h * piece_half, piece_half), block(s)]), axis=0, keepdims=True)
            code = jnp.floor(jnp.log2(jnp.maximum(peak, 1e-30)) * 128.0) + 2.0
            grow = jnp.exp2(code * (-1.0 / 128.0)) * 32767.0
            packed[s, h, pl.ds(piece_half, 16)] = (
                jnp.broadcast_to(code, (16, rows)).astype(jnp.int32).astype(jnp.int16)
            )
            for r in range(0, piece_half, 64):
                value = acc_ref[pl.ds(h * piece_half + r, 64), block(s)] * grow
                packed[s, h, pl.ds(r, 64)] = jnp.floor(value + 0.5).astype(jnp.int32).astype(jnp.int16)

    def exchange(phase, start):
        def one(d, carry):
            other = lax.rem(me + d, count)
            copy = remote(
                mine_sums.at[phase],
                sums.at[phase, me],
                sum_send.at[phase, d],
                sum_recv.at[phase, me],
                lax.div(other, 2),
                lax.rem(other, 2),
            )
            if start:
                copy.start()
            else:
                copy.wait_send()
            return carry

        lax.fori_loop(1, count, one, 0)

    def gather_sums(phase):
        def one(d, carry):
            other = lax.rem(me + d, count)
            view = sums.at[phase, other]
            pltpu.make_async_copy(view, view, sum_recv.at[phase, other]).wait()
            return carry

        lax.fori_loop(1, count, one, 0)
        sums[phase, pl.ds(me, 1)] = mine_sums[pl.ds(phase, 1)]
        every = jnp.sum(sums[phase], axis=0)
        return jnp.sum(every[0:8]), jnp.sum(every[8:16])

    def fold_sum(v):
        out = v[:, 0:128]
        for q in range(1, v.shape[1] // 128):
            out = out + v[:, q * 128 : (q + 1) * 128]
        return jnp.sum(out.reshape(v.shape[0] // 8, 8, 128), axis=0)

    zero = jnp.zeros((8, 128), jnp.float32)
    step_rows = min(32, rows)
    coeff_load.wait()

    def early(r, carry):
        band = pl.ds(pl.multiple_of(r * step_rows, step_rows), step_rows)
        c = c_ref[band, :].astype(jnp.float32)
        return carry[0] + fold_sum(c * acc_ref[band, :]), carry[1] + fold_sum(c * c)

    proj, weight = lax.fori_loop(0, rows // step_rows, early, (zero, zero))
    mine_sums[0, 0:8] = proj
    mine_sums[0, 8:16] = weight
    exchange(0, True)

    def relay_first(t):
        s = lax.rem(place + t, fold)
        return s, remote(
            relay_a.at[s], recv.at[place, 0], send_a.at[t], recv_sem.at[place, 0], far_col * fold + s, col
        )

    def relay_second(t):
        far = lax.rem(place - t + fold, fold)
        return far, remote(relay_b.at[far], recv.at[far, 1], send_b.at[t], recv_sem.at[far, 1], row, far_col)

    def launch(k, carry):
        @pl.when(diag)
        def _():
            s, copy = relay_first(k)
            pltpu.make_async_copy(relay_a.at[s], relay_a.at[s], arrive_a.at[s]).wait()
            copy.start()

        pack(k)

        @pl.when(jnp.logical_not(diag))
        def _():
            for copy in own_relayed(k):
                copy.start()

        @pl.when(jnp.logical_and(diag, k > 0))
        def _():
            for copy in own_direct(k):
                copy.start()

        return carry

    lax.fori_loop(0, fold, launch, 0)

    @pl.when(diag)
    def _():
        for copy in own_local():
            copy.start()
        for copy in own_local():
            copy.wait()

    @pl.when(diag)
    def _():
        def relay(t, carry):
            far, copy = relay_second(t)
            pltpu.make_async_copy(relay_b.at[far], relay_b.at[far], arrive_b.at[far]).wait()
            copy.start()
            return carry

        lax.fori_loop(0, fold, relay, 0)

    def await_piece(k):
        s = lax.rem(place - k + fold, fold)

        @pl.when(jnp.logical_not(jnp.logical_and(diag, k == 0)))
        def _():
            for h in range(2):
                pltpu.make_async_copy(recv.at[s, h], recv.at[s, h], recv_sem.at[s, h]).wait()

    proj, weight = gather_sums(0)
    theta = 2.0 * proj / weight
    piece = min(128, rows)

    def finish(k, carry):
        s = lax.rem(place - k + fold, fold)
        await_piece(k)

        def part_of(r, inner):
            squares, spread = inner
            band = pl.ds(pl.multiple_of(r * piece, piece), piece)
            for h in range(2):
                cols = pl.ds(pl.multiple_of(s * rows + h * piece_half, piece_half), piece_half)
                code = recv[s, h, pl.ds(piece_half, 16), band].astype(jnp.int32).astype(jnp.float32)[0:1]
                shrink = jnp.exp2(code * (1.0 / 128.0)) * (1.0 / 32767.0)
                value = recv[s, h, pl.ds(0, piece_half), band].astype(jnp.int32).astype(jnp.float32)
                sigma = acc_ref[band, cols] + (value * shrink).T
                residual = sigma - theta * c_ref[band, cols].astype(jnp.float32)
                update = residual / jnp.maximum(jnp.abs(out_ref[band, cols] - theta), 1.0)
                out_ref[band, cols] = update
                squares = squares + fold_sum(residual * residual)
                spread = spread + fold_sum(update * update)
            return squares, spread

        return lax.fori_loop(0, rows // piece, part_of, carry)

    squares, spread = lax.fori_loop(0, fold, finish, (zero, zero))
    mine_sums[1, 0:8] = squares
    mine_sums[1, 8:16] = spread
    exchange(1, True)
    squares, spread = gather_sums(1)
    stats_ref[0] = theta
    stats_ref[1] = jnp.max(jnp.sqrt(jnp.full((8, 128), squares / total, jnp.float32)))
    scale_ref[0] = jnp.max(lax.rsqrt(jnp.full((8, 128), spread / total + 1e-06, jnp.float32)))

    exchange(0, False)
    exchange(1, False)

    @pl.when(diag)
    def _():
        def done(t, carry):
            @pl.when(t > 0)
            def _():
                for copy in own_direct(t):
                    copy.wait_send()

            relay_first(t)[1].wait_send()
            relay_second(t)[1].wait_send()
            return carry

        lax.fori_loop(0, fold, done, 0)

    @pl.when(jnp.logical_not(diag))
    def _():
        def done(t, carry):
            for copy in own_relayed(t):
                copy.wait_send()
            return carry

        lax.fori_loop(0, fold, done, 0)


def whole_step(ham, tile_mask, coeff, occupation, orbital_energy, coulomb):
    rows, strings = ham.shape
    half = coeff.shape[1]
    fold = half // rows
    count = lax.axis_size("row") * lax.axis_size("col")
    reach = (fold // 2 + 1) * rows
    tall = rows // 2 + 16
    anywhere = pl.BlockSpec(memory_space=pl.ANY)
    vmem = pl.BlockSpec(memory_space=pltpu.VMEM)
    dma = pltpu.SemaphoreType.DMA
    smem = pl.BlockSpec(memory_space=pltpu.SMEM)
    update, _, _, stats, scale = pl.pallas_call(
        functools.partial(step_kernel, float(strings) * float(strings)),
        out_shape=(
            jax.ShapeDtypeStruct((rows, half), jnp.float32),
            jax.ShapeDtypeStruct((fold, rows, half), jnp.bfloat16),
            jax.ShapeDtypeStruct((fold, rows, reach), jnp.bfloat16),
            jax.ShapeDtypeStruct((2,), jnp.float32),
            jax.ShapeDtypeStruct((1,), jnp.float32),
        ),
        in_specs=[anywhere, vmem, anywhere, vmem, vmem, vmem],
        out_specs=(vmem, anywhere, anywhere, smem, smem),
        scratch_shapes=[
            pltpu.VMEM((rows, half), jnp.float32),
            pltpu.VMEM((rows, strings), jnp.bfloat16),
            pltpu.VMEM((2 * rows, half), jnp.bfloat16),
            pltpu.VMEM((rows, reach), jnp.bfloat16),
            pltpu.VMEM((rows, half), jnp.bfloat16),
            pltpu.VMEM((fold, 2, tall, rows), jnp.int16),
            pltpu.VMEM((fold, tall, rows), jnp.int16),
            pltpu.VMEM((fold, tall, rows), jnp.int16),
            pltpu.VMEM((fold, 2, tall, rows), jnp.int16),
            pltpu.VMEM((2, 16, 128), jnp.float32),
            pltpu.VMEM((2, count, 16, 128), jnp.float32),
            dma((4,)),
            dma((100,)),
            dma((fold, 4, 2)),
            dma((fold, 4, 2)),
            dma((fold, 2)),
            dma((fold, 2)),
            dma((fold,)),
            dma((fold,)),
            dma((fold,)),
            dma((fold,)),
            dma((2,)),
            dma((2, count)),
            dma((2, count)),
            dma((fold // 2 + 1,)),
        ],
        compiler_params=pltpu.CompilerParams(
            collective_id=9, has_side_effects=True, vmem_limit_bytes=62 * 1024 * 1024
        ),
        name="whole_step",
    )(ham, tile_mask, coeff, occupation, orbital_energy[None, :], coulomb)
    return update * scale[0], stats


CHUNKS = 2


def body(ham, coeff, tile_mask, occupation, orbital_energy, coulomb):
    tile_rows, strings = ham.shape
    tile_cols = coeff.shape[1]
    fold = tile_cols // tile_rows
    direct = lax.axis_size("col") == 2 and lax.axis_size("row") == 16
    if direct:
        return whole_step(ham, tile_mask, coeff, occupation, orbital_energy, coulomb)
    else:
        occ_float = occupation.astype(jnp.float32)
        occ_alpha = lax.dynamic_slice_in_dim(occ_float, lax.axis_index("row") * tile_rows, tile_rows, 1)
        occ_beta = lax.dynamic_slice_in_dim(occ_float, lax.axis_index("col") * tile_cols, tile_cols, 1)
        energy_alpha = jnp.dot(orbital_energy, occ_alpha, precision=HIGH)
        energy_beta = jnp.dot(orbital_energy, occ_beta, precision=HIGH)
        couple = jnp.dot(occ_alpha.T, coulomb, precision=HIGH)
        diagonal = energy_alpha[:, None] + energy_beta[None, :] + jnp.dot(couple, occ_beta, precision=HIGH)
        mask_cols = tile_mask.shape[1]
        block_size = strings // mask_cols
        mask_rows = tile_rows // block_size
        weights = tile_mask.astype(jnp.bfloat16)[:, None, :, None]
        masked = (ham.reshape(mask_rows, block_size, mask_cols, block_size) * weights).reshape(tile_rows, strings)
        chunks = math.gcd(CHUNKS, fold)
        products = []
        arrived = []
        for q in range(chunks):
            part = jnp.concatenate(
                [coeff[:, s * tile_rows : (s + 1) * tile_rows] for s in range(q, fold, chunks)], axis=1
            )
            gathered = with_layout_constraint(lax.all_gather(part, "row", axis=0, tiled=True), Layout((0, 1)))
            products.append(jnp.dot(masked, gathered, preferred_element_type=jnp.float32))
            result = turn(q, chunks, products, arrived, coeff, diagonal, strings)
            if q < chunks - 1:
                arrived.append(result)
    update, sums = result
    correction = update * lax.rsqrt(sums[2] + 1e-06)
    stats = jnp.stack([sums[0], jnp.sqrt(sums[1])])
    return (correction, stats)


def solution(mesh):
    in_specs = (P("row", None), P("row", "col"), P("row", None), P(), P(), P())
    out_specs = (P("row", "col"), P())
    return jax.shard_map(body, mesh=mesh, in_specs=in_specs, out_specs=out_specs, check_vma=False)
```
